32 devices in a mesh: brick: 8 (over z, y), vec: 4 (over x, core).
Axes of the slice: x: 2, y: 2, z: 4, core: 2. Of those that a mesh axis runs over, the one named last changes fastest.
Arguments:
- right_side: float32 [4, 4, 32, 128, 128], P('vec', None, 'brick'), may hold values from -6 to 6
- diffusivity: float32 [32, 128, 128], P('brick'), may hold values from 0.3 to 3
Outputs:
- precond: float32 [4, 4, 32, 128, 128], P('vec', None, 'brick')
- gram: float32 [4, 4], P('vec')
The draws below stay inside these ranges and needn't reach their ends.
All inputs are finite; a program needn't handle non-finite values.
Results may differ from the reference program's by a relative error of at most 0.0003.
Values may be sent and summed in bfloat16 or wider, within the bound.
A program may use at most 64 MiB of HBM per device.

```python
import math
import jax
import jax.numpy as jnp
from jax import lax

FIELDS = 4
NY = 128
NZ = 128
SWEEPS = 6
NX = 32
VECS = 4


def draw_right_side(key, part):
    key_common = jax.random.fold_in(key, 11)
    key_mixing = jax.random.fold_in(key, 12)
    key_private = jax.random.fold_in(key, 13)
    full_shape = (VECS, FIELDS, NX, NY, NZ)
    mixing = 0.6 * jax.random.normal(key_mixing, (VECS, 3), jnp.float32)
    private_part = 0.7 * jax.random.normal(key_private, full_shape, jnp.float32)
    combined = private_part
    for component in range(3):
        common = jax.random.normal(jax.random.fold_in(key_common, component), (FIELDS, NX, NY, NZ), jnp.float32)
        combined = combined + mixing[:, component][:, None, None, None, None] * common[None]
    return jnp.clip(combined, -6.0, 6.0)


def block_scale(stream_key, extent, split, least, largest):
    def one(axis_at, blocks):
        heights = jax.random.uniform(jax.random.fold_in(jax.random.fold_in(stream_key, 6), axis_at), (blocks,), jnp.float32, least / len(split), largest / len(split))
        return jnp.repeat(jnp.exp(heights), extent[axis_at] // blocks).reshape((-1,) + (1,) * (len(extent) - axis_at - 1))

    loudness = one(*split[0])
    for cut in split[1:]:
        loudness = loudness * one(*cut)
    return loudness


def setup_inputs(seed: int = 0) -> dict:
    splits = jax.random.split(jax.random.key(seed), 3)
    return {
        "right_side": draw_right_side(jax.random.fold_in(splits[2], 71), 0),
        "diffusivity": jnp.clip(jnp.exp(math.log(3.0) - 2.3025851 * jax.random.uniform(splits[1], (NX, NY, NZ), jnp.float32) ** block_scale(splits[1], (NX, NY, NZ), ((0, 8),), -0.2, 0.2)), 0.3, 3.0),
    }


shift_value = 0.1
damping = 0.8


def pad_planes(field):
    widths = [(0, 0)] * (field.ndim - 3) + [(1, 1), (0, 0), (0, 0)]
    return jnp.pad(field, widths)


def neighbours(padded):
    middle = padded[..., 1:-1, :, :]
    total = padded[..., 2:, :, :] + padded[..., :-2, :, :]
    lead = [(0, 0)] * (middle.ndim - 2)
    side_y = jnp.pad(middle, lead + [(1, 1), (0, 0)])
    total = total + side_y[..., 2:, :] + side_y[..., :-2, :]
    side_z = jnp.pad(middle, lead + [(0, 0), (1, 1)])
    total = total + side_z[..., 2:] + side_z[..., :-2]
    return total


def operate(padded, kappa, scale):
    middle = padded[..., 1:-1, :, :]
    return shift_value * middle + scale * kappa * (6.0 * middle - neighbours(padded))


def pair_table(cols):
    fine = jnp.arange(cols, dtype=jnp.int32)
    coarse = jnp.arange(cols // 2, dtype=jnp.int32)
    return jnp.where(fine[:, None] // 2 == coarse[None, :], 1.0, 0.0).astype(jnp.float32)


def restrict(field):
    cols = field.shape[-1]
    summed = field[..., 0::2, :, :] + field[..., 1::2, :, :]
    summed = summed[..., 0::2, :] + summed[..., 1::2, :]
    halved = jnp.dot(summed, pair_table(cols), precision=lax.Precision.HIGHEST, preferred_element_type=jnp.float32)
    return halved * 0.125


def prolong(field):
    lead = field.shape[:-3]
    planes, rows, cols = field.shape[-3:]
    table = pair_table(2 * cols).T
    wide_cols = jnp.dot(field, table, precision=lax.Precision.HIGHEST, preferred_element_type=jnp.float32)
    wide = jnp.broadcast_to(wide_cols[..., :, None, :, None, :], lead + (planes, 2, rows, 2, 2 * cols))
    return wide.reshape(lead + (planes * 2, rows * 2, cols * 2))


def vcycle(right, kappa0):
    kappa1 = restrict(kappa0)
    kappa2 = restrict(kappa1)
    diag0 = shift_value + 6.0 * kappa0
    diag1 = shift_value + 6.0 * 0.25 * kappa1
    diag2 = shift_value + 6.0 * 0.0625 * kappa2
    level0 = damping * right / diag0
    resid0 = right - operate(pad_planes(level0), kappa0, 1.0)
    right1 = restrict(resid0)
    level1 = damping * right1 / diag1
    resid1 = right1 - operate(pad_planes(level1), kappa1, 0.25)
    right2 = restrict(resid1)
    level2 = damping * right2 / diag2
    for sweep in range(SWEEPS - 1):
        level2 = level2 + damping * (right2 - operate(pad_planes(level2), kappa2, 0.0625)) / diag2
    level1 = level1 + prolong(level2)
    level1 = level1 + damping * (right1 - operate(pad_planes(level1), kappa1, 0.25)) / diag1
    level0 = level0 + prolong(level1)
    level0 = level0 + damping * (right - operate(pad_planes(level0), kappa0, 1.0)) / diag0
    return level0


def reference(right_side, diffusivity):
    precond = lax.map(lambda right: vcycle(right, diffusivity), right_side)
    flat = precond.astype(jnp.bfloat16).reshape(right_side.shape[0], -1)
    gram = jnp.dot(flat, flat.T, preferred_element_type=jnp.float32)
    return precond, gram
```

```python
import functools

import jax
import jax.numpy as jnp
from jax import lax
from jax.experimental import pallas as pl
from jax.experimental.pallas import tpu as pltpu
from jax.sharding import PartitionSpec as P

SWEEPS = 6
NEAR = 2
ONE_ROUND = 64
shift_value = 0.1
damping = 0.8
keep = 1.0 - damping
F32 = jnp.float32
BF16 = jnp.bfloat16
MESH = pl.DeviceIdType.MESH


def rolled_sides(x, axis, width):
    size = x.shape[axis]
    place = lax.broadcasted_iota(jnp.int32, x.shape, axis) % width
    low = jnp.where(place == 0, 0.0, pltpu.roll(x, 1, axis))
    high = jnp.where(place == width - 1, 0.0, pltpu.roll(x, size - 1, axis))
    return low + high


def in_plane(x, width):
    return rolled_sides(x, 0, x.shape[0]) + rolled_sides(x, 1, width)


def split_dot(x, table):
    head = x.astype(BF16)
    tail = (x - head.astype(F32)).astype(BF16)
    return jnp.dot(head, table, preferred_element_type=F32) + jnp.dot(
        tail, table, preferred_element_type=F32
    )


def iotas(rows, cols):
    return (lax.broadcasted_iota(jnp.int32, (rows, cols), 0),
            lax.broadcasted_iota(jnp.int32, (rows, cols), 1))


def merge_table(parts, lanes):
    row, col = iotas(parts * lanes, lanes)
    return jnp.where(row // 2 == col, 1.0, 0.0).astype(BF16)


def spread_table(parts, lanes):
    row, col = iotas(lanes, parts * lanes)
    return jnp.where(col // 2 == row, 1.0, 0.0).astype(BF16)


def beside_table(parts, lanes):
    row, col = iotas(lanes, parts * lanes)
    place = col % lanes
    low = ((col - 1) // 2 == row) & (place > 0)
    high = ((col + 1) // 2 == row) & (place < lanes - 1)
    return jnp.where(low | high, 1.0, 0.0).astype(BF16)


def repeat_table(lanes, source, width):
    row, col = iotas(lanes, lanes)
    hit = (row // 2 == col % width) & (row < source)
    return jnp.where(hit, 1.0, 0.0).astype(BF16)


def lane_of(x):
    return lax.broadcasted_iota(jnp.int32, x.shape, x.ndim - 1)


def kernel(bricks, group, reach, rhs_in, kap_in, out, gram, rhs, kap, xp, g0, gk, lo, lb, lr, x0s, x0h, tmp,
           ktmp, k1s, q1s, k1c, k1h, k1e, q1e, b1s, x1p, x1b, x1h, m1, t1, t3, f1s, f1h, q2s, q2c, q2h, x2s, x2b,
           x2h, x2hb, t2, xs, xr, w1, wz, v1, vz, zb, zr, part, g1h, rows_s, g2h, sems_l, sems_r, sems_s):
    fields, planes, ys, zs = rhs.shape
    pairs = fields // 2
    y1, y2 = ys // 2, ys // 4
    width1, width2 = zs // 2, zs // 4
    half = planes // 2
    units = fields * planes
    share = units // group
    whole_fields = share % planes == 0
    b = lax.axis_index("brick")
    v = lax.axis_index("vec")
    has = (b > 0, b < bricks - 1)
    side = (-1, 1)
    edge = (0, planes - 1)
    edge1 = (0, half - 1)
    offs = [sign * size for size in range(1, reach + 1) for sign in (-1, 1)]
    counter = [0]
    sends = []

    def copy(src, dst, sem, brick, vec):
        return pltpu.make_async_remote_copy(
            src_ref=src, dst_ref=dst, send_sem=sems_s.at[sem], recv_sem=sems_r.at[sem],
            device_id=(brick, vec), device_id_type=MESH)

    def begin(cond, src, dst, sem, brick, vec):
        made = copy(src, dst, sem, brick, vec)
        if cond is None:
            made.start()
        else:
            pl.when(cond)(made.start)
        sends.append((cond, made))

    def arrive(cond, dst, sem):
        waiter = copy(dst, dst, sem, b, v)
        if cond is None:
            waiter.wait_recv()
        else:
            pl.when(cond)(waiter.wait_recv)

    def number(count):
        base = counter[0]
        counter[0] += count
        return base

    def inside(off):
        return (b + off >= 0) & (b + off < bricks)

    sem_x0 = number(2 * fields)
    sem_k1 = number(2)
    sem_f1 = number(2)
    sem_x1 = number(4)
    sem_x2 = number(2 * reach + 1)
    sem_q2 = number(2 * reach + 1)
    sem_l = number(3 * group)
    sem_x = number(group)
    sem_g1 = number(group)
    sem_g2 = number(bricks * group if bricks * group <= ONE_ROUND else bricks)

    barrier = pltpu.get_barrier_semaphore()
    for step in range(1, bricks):
        pl.semaphore_signal(barrier, inc=1, device_id=((b + step) % bricks, v),
                            device_id_type=MESH)
    for step in range(1, group):
        pl.semaphore_signal(barrier, inc=1, device_id=(b, (v + step) % group),
                            device_id_type=MESH)
    loads = [pltpu.make_async_copy(kap_in, kap, sems_l.at[0])]
    for f in range(fields):
        loads.append(pltpu.make_async_copy(rhs_in.at[0, f], rhs.at[f], sems_l.at[1 + f]))
    for load in loads:
        load.start()

    for s in range(2):
        @pl.when(jnp.logical_not(has[s]))
        def _(s=s):
            x0h[s] = jnp.zeros_like(x0h.at[s])
            x1h[s] = jnp.zeros_like(x1h.at[s])
            k1h[s] = jnp.zeros_like(k1h.at[s])
            f1h[s] = jnp.zeros_like(f1h.at[s])
    for off in offs:
        @pl.when(jnp.logical_not(inside(off)))
        def _(off=off):
            q2h[off + reach] = jnp.zeros_like(q2h.at[off + reach])
            if abs(off) <= NEAR:
                x2h[off + reach] = jnp.zeros_like(x2h.at[off + reach])
            else:
                x2hb[off + reach] = jnp.zeros_like(x2hb.at[off + reach])

    loads[0].wait()
    for p in range(planes):
        g = damping / (shift_value + 6.0 * kap[p])
        g0[p] = g
        gk[p] = g * kap[p]
    for f in range(fields):
        loads[1 + f].wait()
        for p in range(planes):
            x = g0[p] * rhs[f, p]
            xp[f, p] = x
            for s in range(2):
                if p == edge[s]:
                    x0s[s, f] = x.astype(BF16)

    pl.semaphore_wait(barrier, bricks - 1 + group - 1)
    for f in range(fields):
        for s in range(2):
            begin(has[s], x0s.at[s, f], x0h.at[1 - s, f], sem_x0 + (1 - s) * fields + f,
                  b + side[s], v)

    merge = merge_table(2, zs)
    for h in range(half):
        ktmp[h] = kap[2 * h] + kap[2 * h + 1]
    k1 = []
    for h in range(half):
        summed = ktmp.at[h][pl.ds(0, y1, stride=2), :] + ktmp.at[h][pl.ds(1, y1, stride=2), :]
        k = split_dot(summed, repeat_table(zs, zs, width1)) * 0.125
        k1s[h] = k
        k1.append(k)
    for s in range(2):
        k = k1[edge1[s]]
        low, high = k[:y2], k[y2:]
        k1c[s] = jnp.where(lane_of(low) < width1, low, high)
        begin(has[s], k1c.at[s], k1h.at[1 - s], sem_k1 + 1 - s, b + side[s], v)
    gd1 = [damping / (shift_value + 6.0 * 0.25 * k) for k in k1]
    for h in range(half):
        q1s[h] = gd1[h] * (0.25 * k1[h])
    t1[0] = k1[0] + k1[1]
    summed = t1.at[0][pl.ds(0, y2, stride=2), :] + t1.at[0][pl.ds(1, y2, stride=2), :]
    k2 = split_dot(summed, repeat_table(zs, width1, width2)) * 0.125
    gd2 = damping / (shift_value + 6.0 * 0.0625 * k2)
    q2 = gd2 * (0.0625 * k2)
    q2s[...] = q2
    blocks = zs // width2
    tall2 = y2 // blocks
    packed = q2[:tall2]
    place = lane_of(packed) // width2
    for j in range(1, blocks):
        packed = jnp.where(place == j, q2[j * tall2:(j + 1) * tall2], packed)
    q2c[...] = packed
    for off in offs:
        begin(inside(off), q2c, q2h.at[reach - off], sem_q2 + reach - off, b + off, v)

    for f in range(fields):
        for h in range(half):
            total = None
            for p in (2 * h, 2 * h + 1):
                x = xp[f, p]
                around = in_plane(x, zs)
                if p > 0:
                    around = around + xp[f, p - 1]
                if p < planes - 1:
                    around = around + xp[f, p + 1]
                resid = keep * rhs[f, p] + kap[p] * around
                lo[f, p] = x + g0[p] * resid
                total = resid if total is None else total + resid
            tmp[f, h] = total

    def pack(f, p):
        view = lo.at[f, p]
        for e in range(2):
            lb[f * planes + p, e] = view[pl.ds(e, y1, stride=2), :].astype(BF16)

    steps = sorted(range(1, group), key=lambda step: -min(step, group - step))

    def share_out(first, count, sem):
        for step in steps:
            peer = (v + step) % group
            begin(None, lb.at[pl.ds(peer * share + first, count)], lr.at[v, pl.ds(first, count)],
                  sem + step, b, peer)

    def share_in(first, count, sem):
        for step in steps:
            source = (v + group - step) % group
            arrive(None, lr.at[source, pl.ds(first, count)], sem + step)

    early = share == planes
    for f in range(fields):
        for p in range(1, planes - 1):
            pack(f, p)
    if early:
        share_out(1, planes - 2, sem_l)

    for pair in range(pairs):
        halved = [[None] * 2 for _ in range(half)]
        for inner in range(2):
            f = 2 * pair + inner
            for s in range(2):
                arrive(has[s], x0h.at[s, f], sem_x0 + s * fields + f)
                p = edge[s]
                flux = kap[p] * x0h[s, f].astype(F32)
                tmp[f, edge1[s]] = tmp[f, edge1[s]] + flux
                lo[f, p] = lo[f, p] + g0[p] * flux
            for h in range(half):
                view = tmp.at[f, h]
                halved[h][inner] = view[pl.ds(0, y1, stride=2), :] + view[pl.ds(1, y1, stride=2), :]
        for h in range(half):
            b1 = split_dot(jnp.concatenate(halved[h], axis=1), merge) * 0.125
            b1s[pair, h] = b1
            x1p[pair, h + 2] = gd1[h] * b1

    for s in range(2):
        arrive(has[s], k1h.at[s], sem_k1 + s)
        c = k1h[s]
        turned = pltpu.roll(c, width1, 1)
        lane = lane_of(c)
        k1e[s, :y2] = jnp.where(lane < width1, c, turned)
        k1e[s, y2:] = jnp.where(lane < width1, turned, c)
        halved = []
        for pair in range(pairs):
            t3[s, pair] = k1e[s] * x1p[pair, edge1[s] + 2]
            view = t3.at[s, pair]
            halved.append(view[pl.ds(0, y2, stride=2), :] + view[pl.ds(1, y2, stride=2), :])
        f1s[s] = split_dot(jnp.concatenate(halved, axis=1), merge)
        begin(has[s], f1s.at[s], f1h.at[1 - s], sem_f1 + 1 - s, b + side[s], v)
    for order in range(half):
        for s in range(2):
            plane = order if s == 0 else half - 1 - order
            for pair in range(pairs):
                x1b[s, order, pair] = x1p[pair, plane + 2].astype(BF16)
            begin(has[s], x1b.at[s, order], x1h.at[1 - s, order], sem_x1 + (1 - s) * 2 + order,
                  b + side[s], v)

    halved = []
    for pair in range(pairs):
        total = None
        for h in range(half):
            around = in_plane(x1p[pair, h + 2], width1)
            if h > 0:
                around = around + x1p[pair, h + 1]
            if h < half - 1:
                around = around + x1p[pair, h + 3]
            resid = keep * b1s[pair, h] + 0.25 * k1s[h] * around
            total = resid if total is None else total + resid
        t1[pair] = total
        view = t1.at[pair]
        halved.append(view[pl.ds(0, y2, stride=2), :] + view[pl.ds(1, y2, stride=2), :])
    b2 = split_dot(jnp.concatenate(halved, axis=1), merge) * 0.125

    for s in range(2):
        arrive(has[s], f1h.at[s], sem_f1 + s)
        b2 = b2 + (0.125 * 0.25) * f1h[s]
    x20 = gd2 * b2
    x2s[...] = x20
    x2b[...] = x20.astype(BF16)
    for off in reversed(offs):
        slot = reach - off
        if abs(off) <= NEAR:
            begin(inside(off), x2s, x2h.at[slot], sem_x2 + slot, b + off, v)
        else:
            begin(inside(off), x2b, x2hb.at[slot], sem_x2 + slot, b + off, v)

    for f in range(fields):
        for s in range(2):
            pack(f, edge[s])
    if early:
        share_out(0, 1, sem_l + group)
        share_out(planes - 1, 1, sem_l + 2 * group)
    else:
        share_out(0, share, sem_l)

    q1 = [None] * (half + 4)
    for h in range(half):
        q1[h + 2] = q1s[h]
    for s in range(2):
        k = k1e[s]
        q1e[s] = damping / (shift_value + 6.0 * 0.25 * k) * (0.25 * k)
    for s in range(2):
        for order in range(half):
            arrive(has[s], x1h.at[s, order], sem_x1 + s * 2 + order)
            for pair in range(pairs):
                x1p[pair, 1 - order if s == 0 else half + 2 + order] = x1h[s, order, pair].astype(F32)

    def coeff1(i):
        return q1e[0] if i == 1 else q1e[1] if i == half + 2 else q1s[i - 2]

    for i in range(1, half + 3):
        q = coeff1(i)
        for pair in range(pairs):
            x = x1p[pair, i]
            around = in_plane(x, width1) + x1p[pair, i - 1] + x1p[pair, i + 1]
            m1[pair, i] = (1.0 + keep) * x + q * around

    coeff2 = {0: q2s[...]}
    for off in offs:
        arrive(inside(off), q2h.at[off + reach], sem_q2 + off + reach)
    for off in offs:
        c = q2h[off + reach]
        if abs(off) < SWEEPS:
            parts = []
            for j in range(blocks):
                m = jnp.where(lane_of(c) // width2 == j, c, 0.0)
                shift = width2
                while shift < zs:
                    m = m + pltpu.roll(m, shift, 1)
                    shift *= 2
                parts.append(m)
            coeff2[off] = jnp.concatenate(parts, axis=0)

    start = {0: x20}
    for off in offs:
        arrive(inside(off), (x2h if abs(off) <= NEAR else x2hb).at[off + reach], sem_x2 + off + reach)
    for off in offs:
        start[off] = x2h[off + reach] if abs(off) <= NEAR else x2hb[off + reach].astype(F32)

    level2 = dict(start)
    zero = jnp.zeros_like(x20)
    for sweep in range(1, SWEEPS):
        wide = SWEEPS - sweep
        after = {}
        for off in range(-min(wide, reach), min(wide, reach) + 1):
            x = level2[off]
            around = in_plane(x, width2) + level2.get(off - 1, zero) + level2.get(off + 1, zero)
            after[off] = keep * x + start[off] + coeff2[off] * around
        level2 = after

    spread = spread_table(2, zs)
    lift = [[None] * 3 for _ in range(pairs)]
    flat = [[None] * 3 for _ in range(pairs)]
    for off in (-1, 0, 1):
        wide = split_dot(level2[off], spread)
        for pair in range(pairs):
            view = t2.at[off + 1, pair]
            piece = wide[:, pair * zs:(pair + 1) * zs]
            view[pl.ds(0, y2, stride=2), :] = piece
            view[pl.ds(1, y2, stride=2), :] = piece
            lift[pair][off + 1] = view[...]
            flat[pair][off + 1] = in_plane(view[...], width1)
    final1 = [[None] * (half + 4) for _ in range(pairs)]
    for i in range(1, half + 3):
        q = coeff1(i)
        for pair in range(pairs):
            at = i // half
            around = flat[pair][at] + lift[pair][(i - 1) // half] + lift[pair][(i + 1) // half]
            x = m1[pair, i] + keep * lift[pair][at] + q * around
            final1[pair][i] = x
            low, high = x[:y2], x[y2:]
            lane = lane_of(low)
            xs[2 * pair, i - 1] = jnp.where(lane < width1, low, pltpu.roll(high, width1, 1)).astype(BF16)
            xs[2 * pair + 1, i - 1] = jnp.where(lane < width1, pltpu.roll(low, width1, 1), high).astype(BF16)
    for step in steps:
        peer = (v + step) % group
        begin(None, xs.at[peer * share // planes], xr.at[v], sem_x + step, b, peer)

    beside = beside_table(2, zs)
    for i in range(1, half + 3):
        for pair in range(pairs):
            x = final1[pair][i]
            wide = split_dot(x, spread)
            w1[2 * pair, i - 1] = wide[:, :zs]
            w1[2 * pair + 1, i - 1] = wide[:, zs:]
            if 2 <= i < half + 2:
                wide = split_dot(x, beside)
                wz[2 * pair, i - 2] = wide[:, :zs]
                wz[2 * pair + 1, i - 2] = wide[:, zs:]

    def sides(x):
        row = lax.broadcasted_iota(jnp.int32, x.shape, 0)
        low = jnp.where(row == 0, 0.0, pltpu.roll(x, 1, 0))
        high = jnp.where(row == y1 - 1, 0.0, pltpu.roll(x, y1 - 1, 0))
        return low, high

    for f in range(fields):
        for h in range(half):
            x = w1[f, h + 1]
            base = wz[f, h] + 2.0 * x
            kept = keep * x
            rims = sides(x)
            for e in range(2):
                p = 2 * h + e
                around = base + w1[f, h + 2 * e]
                for r in range(2):
                    rows = pl.ds(r, y1, stride=2)
                    z = lo.at[f, p][rows, :] + kept + gk.at[p][rows, :] * (around + rims[r])
                    out.at[0, f, p][rows, :] = z
                    zb[f * planes + p, r] = z.astype(BF16)
    for i in range(share):
        zr[v, i] = zb[v * share + i]

    if early:
        share_in(1, planes - 2, sem_l)
        share_in(0, 1, sem_l + group)
        share_in(planes - 1, 1, sem_l + 2 * group)
    else:
        share_in(0, share, sem_l)
    row, col = iotas(zs, 4 * zs)
    local = col % zs
    coarse = row % width1
    bottom = row // width1 == col // (2 * zs)
    plain = (local // 2 == coarse) & (col // zs % 2 == 0)
    nexts = ((((local - 1) // 2 == coarse) & (local > 0)) | (((local + 1) // 2 == coarse) & (local < zs - 1))) & (
        col // zs % 2 == 1)
    unfold = jnp.where(bottom & (plain | nexts), 1.0, 0.0).astype(BF16)
    for step in steps:
        arrive(None, xr.at[(v + group - step) % group], sem_x + step)
    for step in steps:
        source = (v + group - step) % group
        for i in range(half + 2):
            wide = jnp.dot(xr[source, i], unfold, preferred_element_type=F32)
            v1[i, :y2] = wide[:, :zs]
            v1[i, y2:] = wide[:, 2 * zs:3 * zs]
            vz[i, :y2] = wide[:, zs:2 * zs]
            vz[i, y2:] = wide[:, 3 * zs:]
        for i in range(share):
            p = i % planes if whole_fields else (v * share + i) % planes
            h, e = p // 2, p % 2
            x = v1[h + 1]
            around = vz[h + 1] + 2.0 * x + v1[h + 2 * e]
            rims = sides(x)
            for r in range(2):
                z = lr[source, i, r].astype(F32) + keep * x + gk.at[p][pl.ds(r, y1, stride=2), :] * (around + rims[r])
                zr[source, i, r] = z.astype(BF16)

    rows = 16
    keys = [(i, j) for i in range(group) for j in range(i, group)]
    per = ys // rows

    def products(step, totals):
        unit = step // per
        first = pl.multiple_of(step % per * rows, rows)
        values = [zr[i, unit, first // y1, pl.ds(pl.multiple_of(first % y1, rows), rows), :].astype(F32)
                  for i in range(group)]
        return tuple(
            total + (values[i] * values[j]).reshape(rows // 8, 8, zs).sum(axis=0)
            for total, (i, j) in zip(totals, keys))

    totals = lax.fori_loop(0, share * per, products,
                           tuple(jnp.zeros((8, zs), F32) for _ in keys), unroll=4)
    lines = [None] * group
    lane = lax.broadcasted_iota(jnp.int32, (1, zs), 1)
    for (i, j), total in zip(keys, totals):
        value = jnp.sum(jnp.sum(total, axis=0, keepdims=True), axis=1, keepdims=True)
        for one, other in {(i, j), (j, i)}:
            placed = jnp.where(lane == other, value, 0.0)
            lines[one] = placed if lines[one] is None else lines[one] + placed
    for i in range(group):
        part[i] = lines[i]
    mine = part[v]
    if bricks * group <= ONE_ROUND:
        for index in range(1, bricks * group):
            brick, vec = (b + index // group) % bricks, (v + index % group) % group
            begin(None, part.at[vec], g2h.at[index], sem_g2 + index, brick, vec)
        for index in range(1, bricks * group):
            arrive(None, g2h.at[index], sem_g2 + index)
            mine = mine + g2h[index]
    else:
        for step in range(1, group):
            peer = (v + step) % group
            begin(None, part.at[peer], g1h.at[step], sem_g1 + step, b, peer)
        for step in range(1, group):
            arrive(None, g1h.at[step], sem_g1 + step)
            mine = mine + g1h[step]
        rows_s[...] = mine
        for step in range(1, bricks):
            begin(None, rows_s, g2h.at[step], sem_g2 + step, (b + step) % bricks, v)
        for step in range(1, bricks):
            arrive(None, g2h.at[step], sem_g2 + step)
            mine = mine + g2h[step]
    gram[...] = mine[:, :group]
    for cond, made in sends:
        if cond is None:
            made.wait_send()
        else:
            pl.when(cond)(made.wait_send)


def local(bricks, group, right_side, diffusivity):
    fields, planes, ys, zs = right_side.shape[1:]
    assert right_side.shape[0] == 1 and planes == 4 and zs == 128 and fields == 4
    pairs, half = fields // 2, planes // 2
    y1, y2 = ys // 2, ys // 4
    reach = min(SWEEPS, bricks - 1)
    units = fields * planes
    share = units // group
    slots = 2 * reach + 1
    ends = bricks * group if bricks * group <= ONE_ROUND else bricks
    count = 2 * fields + 8 + 2 * slots + 5 * group + ends
    vm = pltpu.VMEM
    return pl.pallas_call(
        functools.partial(kernel, bricks, group, reach),
        out_shape=(
            jax.ShapeDtypeStruct(right_side.shape, F32),
            jax.ShapeDtypeStruct((1, group), F32),
        ),
        in_specs=[pl.BlockSpec(memory_space=pl.ANY)] * 2,
        out_specs=(pl.BlockSpec(memory_space=pltpu.VMEM),) * 2,
        scratch_shapes=[
            vm((fields, planes, ys, zs), F32),
            vm((planes, ys, zs), F32),
            vm((fields, planes, ys, zs), F32),
            vm((planes, ys, zs), F32),
            vm((planes, ys, zs), F32),
            vm((fields, planes, ys, zs), F32),
            vm((units, 2, y1, zs), BF16),
            vm((group, share, 2, y1, zs), BF16),
            vm((2, fields, ys, zs), BF16),
            vm((2, fields, ys, zs), BF16),
            vm((fields, half, ys, zs), F32),
            vm((half, ys, zs), F32),
            vm((half, y1, zs), F32),
            vm((half, y1, zs), F32),
            vm((2, y2, zs), F32),
            vm((2, y2, zs), F32),
            vm((2, y1, zs), F32),
            vm((2, y1, zs), F32),
            vm((pairs, half, y1, zs), F32),
            vm((pairs, half + 4, y1, zs), F32),
            vm((2, half, pairs, y1, zs), BF16),
            vm((2, half, pairs, y1, zs), BF16),
            vm((pairs, half + 4, y1, zs), F32),
            vm((pairs, y1, zs), F32),
            vm((2, pairs, y1, zs), F32),
            vm((2, y2, zs), F32),
            vm((2, y2, zs), F32),
            vm((y2, zs), F32),
            vm((8, zs), F32),
            vm((slots, 8, zs), F32),
            vm((y2, zs), F32),
            vm((y2, zs), BF16),
            vm((slots, y2, zs), F32),
            vm((slots, y2, zs), BF16),
            vm((3, pairs, y1, zs), F32),
            vm((fields, half + 2, y2, zs), BF16),
            vm((group, half + 2, y2, zs), BF16),
            vm((fields, half + 2, y1, zs), F32),
            vm((fields, half, y1, zs), F32),
            vm((half + 2, y1, zs), F32),
            vm((half + 2, y1, zs), F32),
            vm((units, 2, y1, zs), BF16),
            vm((group, share, 2, y1, zs), BF16),
            vm((group, 1, zs), F32),
            vm((group, 1, zs), F32),
            vm((1, zs), F32),
            vm((ends, 1, zs), F32),
            pltpu.SemaphoreType.DMA((1 + fields,)),
            pltpu.SemaphoreType.DMA((count,)),
            pltpu.SemaphoreType.DMA((count,)),
        ],
        compiler_params=pltpu.CompilerParams(
            collective_id=0, has_side_effects=True, vmem_limit_bytes=48 << 20
        ),
    )(pltpu.with_memory_space_constraint(right_side, pltpu.HBM), pltpu.with_memory_space_constraint(diffusivity, pltpu.HBM))


def solution(mesh):
    return jax.shard_map(
        functools.partial(local, mesh.shape["brick"], mesh.shape["vec"]),
        mesh=mesh,
        in_specs=(P("vec", None, "brick", None, None), P("brick", None, None)),
        out_specs=(P("vec", None, "brick", None, None), P("vec", None)),
        check_vma=False,
    )
```

```python
import functools

import jax
import jax.numpy as jnp
from jax import lax
from jax.experimental import pallas as pl
from jax.experimental.pallas import tpu as pltpu
from jax.sharding import PartitionSpec as P

SWEEPS = 6
NEAR = 2
ONE_ROUND = 64
shift_value = 0.1
damping = 0.8
keep = 1.0 - damping
F32 = jnp.float32
BF16 = jnp.bfloat16
MESH = pl.DeviceIdType.MESH


def rolled_sides(x, axis, width):
    size = x.shape[axis]
    place = lax.broadcasted_iota(jnp.int32, x.shape, axis) % width
    low = jnp.where(place == 0, 0.0, pltpu.roll(x, 1, axis))
    high = jnp.where(place == width - 1, 0.0, pltpu.roll(x, size - 1, axis))
    return low + high


def in_plane(x, width):
    return rolled_sides(x, 0, x.shape[0]) + rolled_sides(x, 1, width)


def split_dot(x, table):
    head = x.astype(BF16)
    tail = (x - head.astype(F32)).astype(BF16)
    return jnp.dot(head, table, preferred_element_type=F32) + jnp.dot(
        tail, table, preferred_element_type=F32
    )


def iotas(rows, cols):
    return (lax.broadcasted_iota(jnp.int32, (rows, cols), 0),
            lax.broadcasted_iota(jnp.int32, (rows, cols), 1))


def merge_table(parts, lanes):
    row, col = iotas(parts * lanes, lanes)
    return jnp.where(row // 2 == col, 1.0, 0.0).astype(BF16)


def spread_table(parts, lanes):
    row, col = iotas(lanes, parts * lanes)
    return jnp.where(col // 2 == row, 1.0, 0.0).astype(BF16)


def beside_table(parts, lanes):
    row, col = iotas(lanes, parts * lanes)
    place = col % lanes
    low = ((col - 1) // 2 == row) & (place > 0)
    high = ((col + 1) // 2 == row) & (place < lanes - 1)
    return jnp.where(low | high, 1.0, 0.0).astype(BF16)


def repeat_table(lanes, source, width):
    row, col = iotas(lanes, lanes)
    hit = (row // 2 == col % width) & (row < source)
    return jnp.where(hit, 1.0, 0.0).astype(BF16)


def lane_of(x):
    return lax.broadcasted_iota(jnp.int32, x.shape, x.ndim - 1)


def write(result, rows, out, gram, sems):
    copies = [pltpu.make_async_copy(result, out, sems.at[0]), pltpu.make_async_copy(rows, gram, sems.at[1])]
    for made in copies:
        made.start()
    for made in copies:
        made.wait()


def kernel(bricks, group, reach, rhs_in, kap_in, out, gram, rhs, kap, xp, g0, gk, lo, lb, lr, x0s, x0h, tmp,
           ktmp, k1s, q1s, k1c, k1h, k1e, q1e, b1s, x1p, x1b, x1h, m1, t1, t3, f1s, f1h, q2s, q2c, q2h, x2s, x2b,
           x2h, x2hb, x2c, sl, t2, t4, ms, mr, w1, wz, v1, vz, zr, part, g1h, rows_s, g2h, waves, sems_l, sems_r, sems_s):
    fields, planes, ys, zs = rhs.shape
    pairs = fields // 2
    y1, y2 = ys // 2, ys // 4
    width1, width2 = zs // 2, zs // 4
    half = planes // 2
    units = fields * planes
    share = units // group
    whole_fields = share % planes == 0
    b = lax.axis_index("brick")
    v = lax.axis_index("vec")
    has = (b > 0, b < bricks - 1)
    turns = (b % 2, 1 - b % 2)
    side = (-1, 1)
    edge = (0, planes - 1)
    edge1 = (0, half - 1)
    offs = [sign * size for size in range(1, reach + 1) for sign in (-1, 1)]
    counter = [0]
    sends = []

    def copy(src, dst, sem, brick, vec, hear=None):
        return pltpu.make_async_remote_copy(
            src_ref=src, dst_ref=dst, send_sem=sems_s.at[sem], recv_sem=sems_r.at[sem if hear is None else hear],
            device_id=(brick, vec), device_id_type=MESH)

    def begin(cond, src, dst, sem, brick, vec, hear=None):
        made = copy(src, dst, sem, brick, vec, hear)
        if cond is None:
            made.start()
        else:
            pl.when(cond)(made.start)
        sends.append((cond, made))

    def arrive(cond, dst, sem):
        waiter = copy(dst, dst, sem, b, v)
        if cond is None:
            waiter.wait_recv()
        else:
            pl.when(cond)(waiter.wait_recv)

    def number(count):
        base = counter[0]
        counter[0] += count
        return base

    def inside(off):
        return (b + off >= 0) & (b + off < bricks)

    sem_x0 = number(2 * fields)
    sem_k1 = number(2)
    sem_f1 = number(2)
    sem_x1 = number(4)
    sem_x2 = number(2 * reach + 1)
    sem_q2 = number(2 * reach + 1)
    sem_l = number(3 * group)
    sem_m = number(group)
    sem_s = number((2 * reach + 1) * group)
    sem_g1 = number(group)
    sem_g2 = number(bricks * group if bricks * group <= ONE_ROUND else bricks)

    barrier = pltpu.get_barrier_semaphore()
    for s in range(2):
        @pl.when(has[s])
        def _(s=s):
            pl.semaphore_signal(barrier, inc=1, device_id=(b + side[s], v), device_id_type=MESH)
    for step in range(1, group):
        pl.semaphore_signal(barrier, inc=1, device_id=(b, (v + step) % group),
                            device_id_type=MESH)
    load_kap = pltpu.make_async_copy(kap_in, kap, sems_l.at[0])
    load_rim = [[pltpu.make_async_copy(rhs_in.at[0, f, edge[s]], rhs.at[f, edge[s]], sems_l.at[1 + 2 * f + s])
                 for s in range(2)] for f in range(fields)]
    load_mid = pltpu.make_async_copy(rhs_in.at[0, :, pl.ds(1, planes - 2)], rhs.at[:, pl.ds(1, planes - 2)],
                                     sems_l.at[1 + 2 * fields])
    load_kap.start()
    for f in range(fields):
        for s in range(2):
            load_rim[f][s].start()
    load_mid.start()

    for s in range(2):
        @pl.when(jnp.logical_not(has[s]))
        def _(s=s):
            x0h[s] = jnp.zeros_like(x0h.at[s])
            x1h[s] = jnp.zeros_like(x1h.at[s])
            k1h[s] = jnp.zeros_like(k1h.at[s])
            f1h[s] = jnp.zeros_like(f1h.at[s])
    for off in offs:
        @pl.when(jnp.logical_not(inside(off)))
        def _(off=off):
            q2h[off + reach] = jnp.zeros_like(q2h.at[off + reach])
            sl[off + reach] = jnp.zeros_like(sl.at[off + reach])
            if abs(off) <= NEAR:
                x2h[off + reach] = jnp.zeros_like(x2h.at[off + reach])
            else:
                x2hb[off + reach] = jnp.zeros_like(x2hb.at[off + reach])

    load_kap.wait()
    for p in range(planes):
        g = damping / (shift_value + 6.0 * kap[p])
        g0[p] = g
        gk[p] = g * kap[p]
    pl.semaphore_wait(barrier, (b > 0).astype(jnp.int32) + (b < bricks - 1).astype(jnp.int32) + group - 1)
    for f in range(fields):
        for s in range(2):
            load_rim[f][s].wait()
            x = g0[edge[s]] * rhs[f, edge[s]]
            xp[f, edge[s]] = x
            x0s[s, f] = x.astype(BF16)
    for s in turns:
        for f in range(fields):
            begin(inside(2 * s - 1), x0s.at[s, f], x0h.at[1 - s, f], sem_x0 + (1 - s) * fields + f,
                  b + 2 * s - 1, v)

    def tell(stage, far):
        for s in range(2):
            @pl.when(inside(side[s] * far))
            def _(s=s):
                pl.semaphore_signal(waves.at[1 - s, stage], inc=1, device_id=(b + side[s] * far, v), device_id_type=MESH)

    def hear(stage, far):
        for s in range(2):
            @pl.when(inside(side[s] * far))
            def _(s=s):
                pl.semaphore_wait(waves.at[s, stage], 1)

    tell(0, 1)

    merge = merge_table(2, zs)
    for h in range(half):
        ktmp[h] = kap[2 * h] + kap[2 * h + 1]
    k1 = []
    for h in range(half):
        summed = ktmp.at[h][pl.ds(0, y1, stride=2), :] + ktmp.at[h][pl.ds(1, y1, stride=2), :]
        k = split_dot(summed, repeat_table(zs, zs, width1)) * 0.125
        k1s[h] = k
        k1.append(k)
    for s in range(2):
        k = k1[edge1[s]]
        low, high = k[:y2], k[y2:]
        k1c[s] = jnp.where(lane_of(low) < width1, low, high)
    for s in turns:
        begin(inside(2 * s - 1), k1c.at[s], k1h.at[1 - s], sem_k1 + 1 - s, b + 2 * s - 1, v)
    gd1 = [damping / (shift_value + 6.0 * 0.25 * k) for k in k1]
    for h in range(half):
        q1s[h] = gd1[h] * (0.25 * k1[h])
    t1[0] = k1[0] + k1[1]
    summed = t1.at[0][pl.ds(0, y2, stride=2), :] + t1.at[0][pl.ds(1, y2, stride=2), :]
    k2 = split_dot(summed, repeat_table(zs, width1, width2)) * 0.125
    gd2 = damping / (shift_value + 6.0 * 0.0625 * k2)
    q2 = gd2 * (0.0625 * k2)
    q2s[...] = q2
    blocks = zs // width2
    tall2 = y2 // blocks
    packed = q2[:tall2]
    place = lane_of(packed) // width2
    for j in range(1, blocks):
        packed = jnp.where(place == j, q2[j * tall2:(j + 1) * tall2], packed)
    q2c[...] = packed

    load_mid.wait()
    for f in range(fields):
        for p in range(1, planes - 1):
            xp[f, p] = g0[p] * rhs[f, p]
    for f in range(fields):
        for h in range(half):
            total = None
            for p in (2 * h, 2 * h + 1):
                x = xp[f, p]
                around = in_plane(x, zs)
                if p > 0:
                    around = around + xp[f, p - 1]
                if p < planes - 1:
                    around = around + xp[f, p + 1]
                resid = keep * rhs[f, p] + kap[p] * around
                lo[f, p] = x + g0[p] * resid
                total = resid if total is None else total + resid
            tmp[f, h] = total

    def pack(f, p):
        view = lo.at[f, p]
        for e in range(2):
            lb[f * planes + p, e] = view[pl.ds(e, y1, stride=2), :].astype(BF16)

    steps = sorted(range(1, group), key=lambda step: -min(step, group - step))

    def share_out(first, count, sem):
        for step in steps:
            peer = (v + step) % group
            begin(None, lb.at[pl.ds(peer * share + first, count)], lr.at[v, pl.ds(first, count)],
                  sem + step, b, peer)

    def share_in(first, count, sem):
        for step in steps:
            source = (v + group - step) % group
            arrive(None, lr.at[source, pl.ds(first, count)], sem + step)

    early = share == planes
    for f in range(fields):
        for p in range(1, planes - 1):
            pack(f, p)
    if early:
        share_out(1, planes - 2, sem_l)

    def send_x1(pair):
        for s in range(2):
            for order in range(half):
                plane = order if s == 0 else half - 1 - order
                x1b[s, pair, order] = x1p[pair, plane + 2].astype(BF16)
        for s in turns:
            begin(inside(2 * s - 1), x1b.at[s, pair], x1h.at[1 - s, pair], sem_x1 + (1 - s) * pairs + pair,
                  b + 2 * s - 1, v)

    hear(0, 1)
    tell(1, 2)
    for pair in range(pairs):
        halved = [[None] * 2 for _ in range(half)]
        for inner in range(2):
            f = 2 * pair + inner
            for s in range(2):
                arrive(has[s], x0h.at[s, f], sem_x0 + s * fields + f)
                p = edge[s]
                flux = kap[p] * x0h[s, f].astype(F32)
                tmp[f, edge1[s]] = tmp[f, edge1[s]] + flux
                lo[f, p] = lo[f, p] + g0[p] * flux
            for h in range(half):
                view = tmp.at[f, h]
                halved[h][inner] = view[pl.ds(0, y1, stride=2), :] + view[pl.ds(1, y1, stride=2), :]
        for h in range(half):
            b1 = split_dot(jnp.concatenate(halved[h], axis=1), merge) * 0.125
            b1s[pair, h] = b1
            x1p[pair, h + 2] = gd1[h] * b1
        if pair < pairs - 1:
            send_x1(pair)
        if pair == 0:
            hear(1, 2)
            tell(2, 2)
    hear(2, 2)

    for s in range(2):
        arrive(has[s], k1h.at[s], sem_k1 + s)
        c = k1h[s]
        turned = pltpu.roll(c, width1, 1)
        lane = lane_of(c)
        k1e[s, :y2] = jnp.where(lane < width1, c, turned)
        k1e[s, y2:] = jnp.where(lane < width1, turned, c)
        halved = []
        for pair in range(pairs):
            t3[s, pair] = k1e[s] * x1p[pair, edge1[s] + 2]
            view = t3.at[s, pair]
            halved.append(view[pl.ds(0, y2, stride=2), :] + view[pl.ds(1, y2, stride=2), :])
        f1s[s] = split_dot(jnp.concatenate(halved, axis=1), merge)
    for s in turns:
        begin(inside(2 * s - 1), f1s.at[s], f1h.at[1 - s], sem_f1 + 1 - s, b + 2 * s - 1, v)
    send_x1(pairs - 1)
    for off in offs:
        begin(inside(off), q2c, q2h.at[reach - off], sem_q2 + reach - off, b + off, v)

    for f in range(fields):
        for s in range(2):
            pack(f, edge[s])
    if early:
        share_out(0, 1, sem_l + group)
        share_out(planes - 1, 1, sem_l + 2 * group)
    else:
        share_out(0, share, sem_l)

    for i in range(share):
        lr[v, i] = lb[v * share + i]
    halved = []
    for pair in range(pairs):
        total = None
        for h in range(half):
            around = in_plane(x1p[pair, h + 2], width1)
            if h > 0:
                around = around + x1p[pair, h + 1]
            if h < half - 1:
                around = around + x1p[pair, h + 3]
            resid = keep * b1s[pair, h] + 0.25 * k1s[h] * around
            total = resid if total is None else total + resid
        t1[pair] = total
        view = t1.at[pair]
        halved.append(view[pl.ds(0, y2, stride=2), :] + view[pl.ds(1, y2, stride=2), :])
    b2 = split_dot(jnp.concatenate(halved, axis=1), merge) * 0.125

    for s in range(2):
        k = k1e[s]
        q1e[s] = damping / (shift_value + 6.0 * 0.25 * k) * (0.25 * k)

    def coeff1(i):
        return q1e[0] if i == 1 else q1e[1] if i == half + 2 else q1s[i - 2]

    def field_of(vec):
        return vec * share // planes

    def raise_m(pair):
        for s in range(2):
            arrive(has[s], x1h.at[s, pair], sem_x1 + s * pairs + pair)
            for order in range(half):
                x1p[pair, 1 - order if s == 0 else half + 2 + order] = x1h[s, pair, order].astype(F32)
        for i in range(1, half + 3):
            x = x1p[pair, i]
            around = in_plane(x, width1) + x1p[pair, i - 1] + x1p[pair, i + 1]
            x = (1.0 + keep) * x + coeff1(i) * around
            m1[pair, i] = x
            low, high = x[:y2], x[y2:]
            left = lane_of(low) < width1
            ms[2 * pair, i - 1] = jnp.where(left, low, pltpu.roll(high, width1, 1)).astype(BF16)
            ms[2 * pair + 1, i - 1] = jnp.where(left, pltpu.roll(low, width1, 1), high).astype(BF16)
        for step in steps:
            peer = (v + step) % group
            begin(field_of(peer) // 2 == pair, ms.at[field_of(peer)], mr.at[v], sem_m + step, b, peer)

    for pair in range(pairs - 1):
        raise_m(pair)
    for s in range(2):
        arrive(has[s], f1h.at[s], sem_f1 + s)
        b2 = b2 + (0.125 * 0.25) * f1h[s]
    x20 = gd2 * b2
    x2s[...] = x20
    x2b[...] = x20.astype(BF16)
    quad = lane_of(x20[:tall2]) // width2
    for f in range(fields):
        slab = None
        for j in range(blocks):
            piece = x20[j * tall2:(j + 1) * tall2]
            if j != f:
                piece = pltpu.roll(piece, width2 * ((j - f) % blocks), 1)
            slab = piece if slab is None else jnp.where(quad == j, piece, slab)
        x2c[f] = slab.astype(BF16)

    for off in reversed(offs):
        for step in range(group):
            peer = (v + step) % group
            slot = reach - off
            begin(inside(off), x2c.at[field_of(peer)], sl.at[slot, v], sem_s + slot * group + step,
                  b + off, peer, sem_s + slot * group)
    for step in steps:
        peer = (v + step) % group
        begin(None, x2c.at[field_of(peer)], sl.at[reach, v], sem_s + reach * group + step,
              b, peer, sem_s + reach * group)
    sl[reach, v] = x2c[field_of(v)]
    for off in reversed(offs):
        slot = reach - off
        if abs(off) <= NEAR:
            begin(inside(off), x2s, x2h.at[slot], sem_x2 + slot, b + off, v)
        else:
            begin(inside(off), x2b, x2hb.at[slot], sem_x2 + slot, b + off, v)

    raise_m(pairs - 1)
    mr[v] = ms[field_of(v)]

    coeff2 = {0: q2s[...]}
    for off in offs:
        arrive(inside(off), q2h.at[off + reach], sem_q2 + off + reach)
    for off in offs:
        c = q2h[off + reach]
        if abs(off) < SWEEPS:
            parts = []
            for j in range(blocks):
                m = jnp.where(lane_of(c) // width2 == j, c, 0.0)
                shift = width2
                while shift < zs:
                    m = m + pltpu.roll(m, shift, 1)
                    shift *= 2
                parts.append(m)
            coeff2[off] = jnp.concatenate(parts, axis=0)

    spread = spread_table(2, zs)
    beside = beside_table(2, zs)

    def sweeps(start):
        level2 = start
        zero = jnp.zeros_like(start[0])
        for sweep in range(1, SWEEPS):
            wide = SWEEPS - sweep
            after = {}
            for off in range(-min(wide, reach), min(wide, reach) + 1):
                x = level2[off]
                around = in_plane(x, width2) + level2.get(off - 1, zero) + level2.get(off + 1, zero)
                after[off] = keep * x + start[off] + coeff2[off] * around
            level2 = after
        return level2

    def lift_up(level2, at, room, dot):
        wide = dot(level2[at], spread)
        plane, flat = [], []
        for pair in range(2):
            view = room.at[pair]
            piece = wide[:, pair * zs:(pair + 1) * zs]
            view[pl.ds(0, y2, stride=2), :] = piece
            view[pl.ds(1, y2, stride=2), :] = piece
            plane.append(view[...])
            flat.append(in_plane(view[...], width1))
        return plane, flat

    def sides(x):
        row = lax.broadcasted_iota(jnp.int32, x.shape, 0)
        low = jnp.where(row == 0, 0.0, pltpu.roll(x, 1, 0))
        high = jnp.where(row == y1 - 1, 0.0, pltpu.roll(x, y1 - 1, 0))
        return low, high

    def half_dot(x, table):
        return jnp.dot(x.astype(BF16), table, preferred_element_type=F32)

    for off in offs:
        slot = off + reach
        arrive(inside(off), sl.at[slot], sem_s + slot * group)
    if group > 1:
        arrive(None, sl.at[reach, pl.ds(0, group - 1)], sem_s + reach * group)
    quads = group // blocks
    starts = [{} for _ in range(quads)]
    for off in range(-reach, reach + 1):
        for q in range(quads):
            parts = [None] * blocks
            for u in range(blocks):
                c = sl[off + reach, q * blocks + u].astype(F32)
                for j in range(blocks):
                    piece = c if j == u else pltpu.roll(c, width2 * ((u - j) % blocks), 1)
                    parts[j] = piece if u == 0 else jnp.where(quad == u, piece, parts[j])
            starts[q][off] = jnp.concatenate(parts, axis=0)
    ends = [sweeps(start) for start in starts]
    for step in steps:
        arrive(None, mr.at[(v + group - step) % group], sem_m + step)
    for q in range(quads):
        raised = [lift_up(ends[q], off, t4.at[off + 1], half_dot) for off in (-1, 0, 1)]
        for pair in range(2):
            first = q * blocks + 2 * pair
            for i in range(1, half + 3):
                even, odd = mr[first, i - 1].astype(F32), mr[first + 1, i - 1].astype(F32)
                left = lane_of(even) < width1
                mixed = jnp.concatenate([jnp.where(left, even, pltpu.roll(odd, width1, 1)),
                                         jnp.where(left, pltpu.roll(even, width1, 1), odd)], axis=0)
                at = i // half
                around = raised[at][1][pair] + raised[(i - 1) // half][0][pair] + raised[(i + 1) // half][0][pair]
                x = mixed + keep * raised[at][0][pair] + coeff1(i) * around
                x = x.astype(BF16)
                wide = jnp.dot(x, spread, preferred_element_type=F32)
                v1[first, i - 1] = wide[:, :zs]
                v1[first + 1, i - 1] = wide[:, zs:]
                if 2 <= i < half + 2:
                    wide = jnp.dot(x, beside, preferred_element_type=F32)
                    vz[first, i - 2] = wide[:, :zs]
                    vz[first + 1, i - 2] = wide[:, zs:]
    if early:
        share_in(1, planes - 2, sem_l)
        share_in(0, 1, sem_l + group)
        share_in(planes - 1, 1, sem_l + 2 * group)
    else:
        share_in(0, share, sem_l)
    for i in range(share):
        p = i % planes if whole_fields else (v * share + i) % planes
        h, e = p // 2, p % 2
        gks = [gk.at[p][pl.ds(r, y1, stride=2), :] for r in range(2)]
        for u in range(group):
            x = v1[u, h + 1]
            around = vz[u, h] + 2.0 * x + v1[u, h + 2 * e]
            rims = sides(x)
            for r in range(2):
                z = lr[u, i, r].astype(F32) + keep * x + gks[r] * (around + rims[r])
                zr[u, i, r] = z.astype(BF16)

    rows = 16
    keys = [(i, j) for i in range(group) for j in range(i, group)]
    per = ys // rows

    def products(step, totals):
        unit = step // per
        first = pl.multiple_of(step % per * rows, rows)
        values = [zr[i, unit, first // y1, pl.ds(pl.multiple_of(first % y1, rows), rows), :].astype(F32)
                  for i in range(group)]
        return tuple(
            total + (values[i] * values[j]).reshape(rows // 8, 8, zs).sum(axis=0)
            for total, (i, j) in zip(totals, keys))

    totals = lax.fori_loop(0, share * per, products,
                           tuple(jnp.zeros((8, zs), F32) for _ in keys), unroll=4)
    lines = [None] * group
    lane = lax.broadcasted_iota(jnp.int32, (1, zs), 1)
    for (i, j), total in zip(keys, totals):
        value = jnp.sum(jnp.sum(total, axis=0, keepdims=True), axis=1, keepdims=True)
        for one, other in {(i, j), (j, i)}:
            placed = jnp.where(lane == other, value, 0.0)
            lines[one] = placed if lines[one] is None else lines[one] + placed
    for i in range(group):
        part[i] = lines[i]
    mine = part[v]
    def own():
        start = {0: x20}
        for off in offs:
            arrive(inside(off), (x2h if abs(off) <= NEAR else x2hb).at[off + reach], sem_x2 + off + reach)
        for off in offs:
            start[off] = x2h[off + reach] if abs(off) <= NEAR else x2hb[off + reach].astype(F32)
        level2 = sweeps(start)
        raised = [lift_up(level2, off, t2.at[off + 1], split_dot) for off in (-1, 0, 1)]
        for i in range(1, half + 3):
            for pair in range(pairs):
                at = i // half
                around = raised[at][1][pair] + raised[(i - 1) // half][0][pair] + raised[(i + 1) // half][0][pair]
                x = m1[pair, i] + keep * raised[at][0][pair] + coeff1(i) * around
                wide = split_dot(x, spread)
                w1[2 * pair, i - 1] = wide[:, :zs]
                w1[2 * pair + 1, i - 1] = wide[:, zs:]
                if 2 <= i < half + 2:
                    wide = split_dot(x, beside)
                    wz[2 * pair, i - 2] = wide[:, :zs]
                    wz[2 * pair + 1, i - 2] = wide[:, zs:]
        for f in range(fields):
            for h in range(half):
                x = w1[f, h + 1]
                base = wz[f, h] + 2.0 * x
                kept = keep * x
                rims = sides(x)
                for e in range(2):
                    p = 2 * h + e
                    around = base + w1[f, h + 2 * e]
                    for r in range(2):
                        rows = pl.ds(r, y1, stride=2)
                        out.at[0, f, p][rows, :] = (
                            lo.at[f, p][rows, :] + kept + gk.at[p][rows, :] * (around + rims[r]))


    if bricks * group <= ONE_ROUND:
        for index in range(1, bricks * group):
            brick, vec = (b + index // group) % bricks, (v + index % group) % group
            begin(None, part.at[vec], g2h.at[index], sem_g2 + index, brick, vec)
        own()
        for index in range(1, bricks * group):
            arrive(None, g2h.at[index], sem_g2 + index)
            mine = mine + g2h[index]
    else:
        for step in range(1, group):
            peer = (v + step) % group
            begin(None, part.at[peer], g1h.at[step], sem_g1 + step, b, peer)
        own()
        for step in range(1, group):
            arrive(None, g1h.at[step], sem_g1 + step)
            mine = mine + g1h[step]
        rows_s[...] = mine
        for step in range(1, bricks):
            begin(None, rows_s, g2h.at[step], sem_g2 + step, (b + step) % bricks, v)
        for step in range(1, bricks):
            arrive(None, g2h.at[step], sem_g2 + step)
            mine = mine + g2h[step]
    gram[...] = mine[:, :group]
    for cond, made in sends:
        if cond is None:
            made.wait_send()
        else:
            pl.when(cond)(made.wait_send)


def local(bricks, group, right_side, diffusivity):
    fields, planes, ys, zs = right_side.shape[1:]
    assert right_side.shape[0] == 1 and planes == 4 and ys == zs == 128 and fields == 4 and group % 4 == 0 and SWEEPS == 6
    pairs, half = fields // 2, planes // 2
    y1, y2 = ys // 2, ys // 4
    reach = min(SWEEPS, bricks - 1)
    units = fields * planes
    share = units // group
    slots = 2 * reach + 1
    ends = bricks * group if bricks * group <= ONE_ROUND else bricks
    count = 2 * fields + 8 + (2 + group) * slots + 5 * group + ends
    vm = pltpu.VMEM
    result, rows = pl.pallas_call(
        functools.partial(kernel, bricks, group, reach),
        out_shape=(
            jax.ShapeDtypeStruct(right_side.shape, F32),
            jax.ShapeDtypeStruct((1, group), F32),
        ),
        in_specs=[pl.BlockSpec(memory_space=pl.ANY)] * 2,
        out_specs=(pl.BlockSpec(memory_space=pltpu.VMEM),) * 2,
        scratch_shapes=[
            vm((fields, planes, ys, zs), F32),
            vm((planes, ys, zs), F32),
            vm((fields, planes, ys, zs), F32),
            vm((planes, ys, zs), F32),
            vm((planes, ys, zs), F32),
            vm((fields, planes, ys, zs), F32),
            vm((units, 2, y1, zs), BF16),
            vm((group, share, 2, y1, zs), BF16),
            vm((2, fields, ys, zs), BF16),
            vm((2, fields, ys, zs), BF16),
            vm((fields, half, ys, zs), F32),
            vm((half, ys, zs), F32),
            vm((half, y1, zs), F32),
            vm((half, y1, zs), F32),
            vm((2, y2, zs), F32),
            vm((2, y2, zs), F32),
            vm((2, y1, zs), F32),
            vm((2, y1, zs), F32),
            vm((pairs, half, y1, zs), F32),
            vm((pairs, half + 4, y1, zs), F32),
            vm((2, pairs, half, y1, zs), BF16),
            vm((2, pairs, half, y1, zs), BF16),
            vm((pairs, half + 4, y1, zs), F32),
            vm((pairs, y1, zs), F32),
            vm((2, pairs, y1, zs), F32),
            vm((2, y2, zs), F32),
            vm((2, y2, zs), F32),
            vm((y2, zs), F32),
            vm((8, zs), F32),
            vm((slots, 8, zs), F32),
            vm((y2, zs), F32),
            vm((y2, zs), BF16),
            vm((slots, y2, zs), F32),
            vm((slots, y2, zs), BF16),
            vm((fields, 8, zs), BF16),
            vm((slots, group, 8, zs), BF16),
            vm((3, pairs, y1, zs), F32),
            vm((3, 2, y1, zs), F32),
            vm((fields, half + 2, y2, zs), BF16),
            vm((group, half + 2, y2, zs), BF16),
            vm((fields, half + 2, y1, zs), F32),
            vm((fields, half, y1, zs), F32),
            vm((group, half + 2, y1, zs), F32),
            vm((group, half, y1, zs), F32),
            vm((group, share, 2, y1, zs), BF16),
            vm((group, 1, zs), F32),
            vm((group, 1, zs), F32),
            vm((1, zs), F32),
            vm((ends, 1, zs), F32),
            pltpu.SemaphoreType.REGULAR((2, 3)),
            pltpu.SemaphoreType.DMA((2 + 2 * fields,)),
            pltpu.SemaphoreType.DMA((count,)),
            pltpu.SemaphoreType.DMA((count,)),
        ],
        compiler_params=pltpu.CompilerParams(
            collective_id=0, has_side_effects=True, vmem_limit_bytes=48 << 20
        ),
    )(pltpu.with_memory_space_constraint(right_side, pltpu.HBM), pltpu.with_memory_space_constraint(diffusivity, pltpu.HBM))
    return pl.pallas_call(
        write,
        out_shape=(
            jax.ShapeDtypeStruct(right_side.shape, F32),
            jax.ShapeDtypeStruct((1, group), F32),
        ),
        in_specs=[pl.BlockSpec(memory_space=pltpu.VMEM)] * 2,
        out_specs=(pl.BlockSpec(memory_space=pl.ANY),) * 2,
        scratch_shapes=[pltpu.SemaphoreType.DMA((2,))],
    )(pltpu.with_memory_space_constraint(result, pltpu.VMEM), pltpu.with_memory_space_constraint(rows, pltpu.VMEM))


def solution(mesh):
    return jax.shard_map(
        functools.partial(local, mesh.shape["brick"], mesh.shape["vec"]),
        mesh=mesh,
        in_specs=(P("vec", None, "brick", None, None), P("brick", None, None)),
        out_specs=(P("vec", None, "brick", None, None), P("vec", None)),
        check_vma=False,
    )
```

```python
import functools

import jax
import jax.numpy as jnp
from jax import lax
from jax.experimental import pallas as pl
from jax.experimental.pallas import tpu as pltpu
from jax.sharding import PartitionSpec as P

SWEEPS = 6
NEAR = 2
ONE_ROUND = 64
shift_value = 0.1
damping = 0.8
keep = 1.0 - damping
F32 = jnp.float32
BF16 = jnp.bfloat16
MESH = pl.DeviceIdType.MESH


def rolled_sides(x, axis, width):
    size = x.shape[axis]
    place = lax.broadcasted_iota(jnp.int32, x.shape, axis) % width
    low = jnp.where(place == 0, 0.0, pltpu.roll(x, 1, axis))
    high = jnp.where(place == width - 1, 0.0, pltpu.roll(x, size - 1, axis))
    return low + high


def in_plane(x, width):
    return rolled_sides(x, 0, x.shape[0]) + rolled_sides(x, 1, width)


def split_dot(x, table):
    head = x.astype(BF16)
    tail = (x - head.astype(F32)).astype(BF16)
    return jnp.dot(head, table, preferred_element_type=F32) + jnp.dot(
        tail, table, preferred_element_type=F32
    )


def iotas(rows, cols):
    return (lax.broadcasted_iota(jnp.int32, (rows, cols), 0),
            lax.broadcasted_iota(jnp.int32, (rows, cols), 1))


def merge_table(parts, lanes):
    row, col = iotas(parts * lanes, lanes)
    return jnp.where(row // 2 == col, 1.0, 0.0).astype(BF16)


def spread_table(parts, lanes):
    row, col = iotas(lanes, parts * lanes)
    return jnp.where(col // 2 == row, 1.0, 0.0).astype(BF16)


def beside_table(parts, lanes):
    row, col = iotas(lanes, parts * lanes)
    place = col % lanes
    low = ((col - 1) // 2 == row) & (place > 0)
    high = ((col + 1) // 2 == row) & (place < lanes - 1)
    return jnp.where(low | high, 1.0, 0.0).astype(BF16)


def repeat_table(lanes, source, width):
    row, col = iotas(lanes, lanes)
    hit = (row // 2 == col % width) & (row < source)
    return jnp.where(hit, 1.0, 0.0).astype(BF16)


def lane_of(x):
    return lax.broadcasted_iota(jnp.int32, x.shape, x.ndim - 1)


def write(result, rows, out, gram, sems):
    copies = [pltpu.make_async_copy(result, out, sems.at[0]), pltpu.make_async_copy(rows, gram, sems.at[1])]
    for made in copies:
        made.start()
    for made in copies:
        made.wait()


def kernel(bricks, group, reach, rhs_in, kap_in, out, gram, rhs, kap, xp, g0, gk, lo, lb, lr, x0s, x0h, tmp,
           ktmp, k1s, q1s, k1c, k1h, k1e, q1e, b1s, x1p, x1b, x1h, m1, t1, t3, f1s, f1h, q2s, q2c, q2h, x2s, x2b,
           x2h, x2hb, x2c, sl, t2, t4, ms, mr, w1, wz, v1, vz, zr, part, g1h, rows_s, g2h, waves, sems_l, sems_r, sems_s):
    fields, planes, ys, zs = rhs.shape
    pairs = fields // 2
    y1, y2 = ys // 2, ys // 4
    width1, width2 = zs // 2, zs // 4
    half = planes // 2
    units = fields * planes
    share = units // group
    whole_fields = share % planes == 0
    b = lax.axis_index("brick")
    v = lax.axis_index("vec")
    has = (b > 0, b < bricks - 1)
    turns = (b % 2, 1 - b % 2)
    side = (-1, 1)
    edge = (0, planes - 1)
    edge1 = (0, half - 1)
    offs = [sign * size for size in range(1, reach + 1) for sign in (-1, 1)]
    counter = [0]
    sends = []

    def copy(src, dst, sem, brick, vec):
        return pltpu.make_async_remote_copy(
            src_ref=src, dst_ref=dst, send_sem=sems_s.at[0], recv_sem=sems_r.at[sem],
            device_id=(brick, vec), device_id_type=MESH)

    def begin(cond, src, dst, sem, brick, vec):
        made = copy(src, dst, sem, brick, vec)
        if cond is None:
            made.start()
        else:
            pl.when(cond)(made.start)
        sends.append((cond, made))

    def arrive(cond, dst, sem):
        waiter = copy(dst, dst, sem, b, v)
        if cond is None:
            waiter.wait_recv()
        else:
            pl.when(cond)(waiter.wait_recv)

    def number(count):
        base = counter[0]
        counter[0] += count
        return base

    def inside(off):
        return (b + off >= 0) & (b + off < bricks)

    sem_x0 = number(2 * pairs)
    sem_k1 = number(2)
    sem_f1 = number(2)
    sem_x1 = number(2 * pairs)
    sem_x2 = number(2 * reach + 1)
    sem_q2 = number(2 * reach + 1)
    sem_s = number(2 * reach + 1)
    sem_l, sem_m, sem_g1, sem_g2 = (number(1) for _ in range(4))

    barrier = pltpu.get_barrier_semaphore()
    for s in range(2):
        @pl.when(has[s])
        def _(s=s):
            pl.semaphore_signal(barrier, inc=1, device_id=(b + side[s], v), device_id_type=MESH)
    for step in range(1, group):
        pl.semaphore_signal(barrier, inc=1, device_id=(b, (v + step) % group),
                            device_id_type=MESH)
    load_kap = pltpu.make_async_copy(kap_in, kap, sems_l.at[0])
    load_kap.start()
    for p in edge:
        pltpu.make_async_copy(rhs_in.at[0, :, p], rhs.at[:, p], sems_l.at[1]).start()
    load_mid = pltpu.make_async_copy(rhs_in.at[0, :, pl.ds(1, planes - 2)], rhs.at[:, pl.ds(1, planes - 2)],
                                     sems_l.at[2])
    load_mid.start()

    for s in range(2):
        @pl.when(jnp.logical_not(has[s]))
        def _(s=s):
            x0h[s] = jnp.zeros_like(x0h.at[s])
            x1h[s] = jnp.zeros_like(x1h.at[s])
            k1h[s] = jnp.zeros_like(k1h.at[s])
            f1h[s] = jnp.zeros_like(f1h.at[s])
    for off in offs:
        @pl.when(jnp.logical_not(inside(off)))
        def _(off=off):
            q2h[off + reach] = jnp.zeros_like(q2h.at[off + reach])
            sl[off + reach] = jnp.zeros_like(sl.at[off + reach])
            if abs(off) <= NEAR:
                x2h[off + reach] = jnp.zeros_like(x2h.at[off + reach])
            else:
                x2hb[off + reach] = jnp.zeros_like(x2hb.at[off + reach])

    load_kap.wait()
    for p in range(planes):
        g = damping / (shift_value + 6.0 * kap[p])
        g0[p] = g
        gk[p] = g * kap[p]
    pl.semaphore_wait(barrier, (b > 0).astype(jnp.int32) + (b < bricks - 1).astype(jnp.int32) + group - 1)
    pltpu.make_async_copy(rhs.at[:, pl.ds(0, 2)], rhs.at[:, pl.ds(0, 2)], sems_l.at[1]).wait()
    for f in range(fields):
        for s in range(2):
            x = g0[edge[s]] * rhs[f, edge[s]]
            xp[f, edge[s]] = x
            x0s[s, f] = x.astype(BF16)
    for s in turns:
        for f in range(fields):
            begin(inside(2 * s - 1), x0s.at[s, f], x0h.at[1 - s, f], sem_x0 + (1 - s) * pairs + f // 2,
                  b + 2 * s - 1, v)

    def tell(stage, far):
        for s in range(2):
            @pl.when(inside(side[s] * far))
            def _(s=s):
                pl.semaphore_signal(waves.at[1 - s, stage], inc=1, device_id=(b + side[s] * far, v), device_id_type=MESH)

    def hear(stage, far):
        for s in range(2):
            @pl.when(inside(side[s] * far))
            def _(s=s):
                pl.semaphore_wait(waves.at[s, stage], 1)

    tell(0, 1)

    merge = merge_table(2, zs)
    for h in range(half):
        ktmp[h] = kap[2 * h] + kap[2 * h + 1]
    k1 = []
    for h in range(half):
        summed = ktmp.at[h][pl.ds(0, y1, stride=2), :] + ktmp.at[h][pl.ds(1, y1, stride=2), :]
        k = split_dot(summed, repeat_table(zs, zs, width1)) * 0.125
        k1s[h] = k
        k1.append(k)
    for s in range(2):
        k = k1[edge1[s]]
        low, high = k[:y2], k[y2:]
        k1c[s] = jnp.where(lane_of(low) < width1, low, high)
    for s in turns:
        begin(inside(2 * s - 1), k1c.at[s], k1h.at[1 - s], sem_k1 + 1 - s, b + 2 * s - 1, v)
    gd1 = [damping / (shift_value + 6.0 * 0.25 * k) for k in k1]
    for h in range(half):
        q1s[h] = gd1[h] * (0.25 * k1[h])
    t1[0] = k1[0] + k1[1]
    summed = t1.at[0][pl.ds(0, y2, stride=2), :] + t1.at[0][pl.ds(1, y2, stride=2), :]
    k2 = split_dot(summed, repeat_table(zs, width1, width2)) * 0.125
    gd2 = damping / (shift_value + 6.0 * 0.0625 * k2)
    q2 = gd2 * (0.0625 * k2)
    q2s[...] = q2
    blocks = zs // width2
    tall2 = y2 // blocks
    packed = q2[:tall2]
    place = lane_of(packed) // width2
    for j in range(1, blocks):
        packed = jnp.where(place == j, q2[j * tall2:(j + 1) * tall2], packed)
    q2c[...] = packed

    load_mid.wait()
    for f in range(fields):
        for p in range(1, planes - 1):
            xp[f, p] = g0[p] * rhs[f, p]
    for f in range(fields):
        for h in range(half):
            total = None
            for p in (2 * h, 2 * h + 1):
                x = xp[f, p]
                around = in_plane(x, zs)
                if p > 0:
                    around = around + xp[f, p - 1]
                if p < planes - 1:
                    around = around + xp[f, p + 1]
                resid = keep * rhs[f, p] + kap[p] * around
                lo[f, p] = x + g0[p] * resid
                total = resid if total is None else total + resid
            tmp[f, h] = total

    def pack(f, p):
        view = lo.at[f, p]
        for e in range(2):
            lb[f * planes + p, e] = view[pl.ds(e, y1, stride=2), :].astype(BF16)

    steps = sorted(range(1, group), key=lambda step: -min(step, group - step))

    def share_out(first, count):
        for step in steps:
            peer = (v + step) % group
            begin(None, lb.at[pl.ds(peer * share + first, count)], lr.at[v, pl.ds(first, count)], sem_l, b, peer)

    early = share == planes
    for f in range(fields):
        for p in range(1, planes - 1):
            pack(f, p)
    if early:
        share_out(1, planes - 2)

    def send_x1(pair):
        for s in range(2):
            for order in range(half):
                plane = order if s == 0 else half - 1 - order
                x1b[s, pair, order] = x1p[pair, plane + 2].astype(BF16)
        for s in turns:
            begin(inside(2 * s - 1), x1b.at[s, pair], x1h.at[1 - s, pair], sem_x1 + (1 - s) * pairs + pair,
                  b + 2 * s - 1, v)

    hear(0, 1)
    tell(1, 2)
    for pair in range(pairs):
        halved = [[None] * 2 for _ in range(half)]
        for s in range(2):
            arrive(has[s], x0h.at[s, pl.ds(2 * pair, 2)], sem_x0 + s * pairs + pair)
        for inner in range(2):
            f = 2 * pair + inner
            for s in range(2):
                p = edge[s]
                flux = kap[p] * x0h[s, f].astype(F32)
                tmp[f, edge1[s]] = tmp[f, edge1[s]] + flux
                lo[f, p] = lo[f, p] + g0[p] * flux
            for h in range(half):
                view = tmp.at[f, h]
                halved[h][inner] = view[pl.ds(0, y1, stride=2), :] + view[pl.ds(1, y1, stride=2), :]
        for h in range(half):
            b1 = split_dot(jnp.concatenate(halved[h], axis=1), merge) * 0.125
            b1s[pair, h] = b1
            x1p[pair, h + 2] = gd1[h] * b1
        if pair < pairs - 1:
            send_x1(pair)
        if pair == 0:
            hear(1, 2)
            tell(2, 2)
    hear(2, 2)

    for s in range(2):
        arrive(has[s], k1h.at[s], sem_k1 + s)
        c = k1h[s]
        turned = pltpu.roll(c, width1, 1)
        lane = lane_of(c)
        k1e[s, :y2] = jnp.where(lane < width1, c, turned)
        k1e[s, y2:] = jnp.where(lane < width1, turned, c)
        halved = []
        for pair in range(pairs):
            t3[s, pair] = k1e[s] * x1p[pair, edge1[s] + 2]
            view = t3.at[s, pair]
            halved.append(view[pl.ds(0, y2, stride=2), :] + view[pl.ds(1, y2, stride=2), :])
        f1s[s] = split_dot(jnp.concatenate(halved, axis=1), merge)
    for s in turns:
        begin(inside(2 * s - 1), f1s.at[s], f1h.at[1 - s], sem_f1 + 1 - s, b + 2 * s - 1, v)
    send_x1(pairs - 1)
    for off in offs:
        begin(inside(off), q2c, q2h.at[reach - off], sem_q2 + reach - off, b + off, v)

    for f in range(fields):
        for s in range(2):
            pack(f, edge[s])
    if early:
        share_out(0, 1)
        share_out(planes - 1, 1)
    else:
        share_out(0, share)

    for i in range(share):
        lr[v, i] = lb[v * share + i]
    halved = []
    for pair in range(pairs):
        total = None
        for h in range(half):
            around = in_plane(x1p[pair, h + 2], width1)
            if h > 0:
                around = around + x1p[pair, h + 1]
            if h < half - 1:
                around = around + x1p[pair, h + 3]
            resid = keep * b1s[pair, h] + 0.25 * k1s[h] * around
            total = resid if total is None else total + resid
        t1[pair] = total
        view = t1.at[pair]
        halved.append(view[pl.ds(0, y2, stride=2), :] + view[pl.ds(1, y2, stride=2), :])
    b2 = split_dot(jnp.concatenate(halved, axis=1), merge) * 0.125

    for s in range(2):
        k = k1e[s]
        q1e[s] = damping / (shift_value + 6.0 * 0.25 * k) * (0.25 * k)

    def coeff1(i):
        return q1e[0] if i == 1 else q1e[1] if i == half + 2 else q1s[i - 2]

    def field_of(vec):
        return vec * share // planes

    def raise_m(pair):
        for s in range(2):
            arrive(has[s], x1h.at[s, pair], sem_x1 + s * pairs + pair)
            for order in range(half):
                x1p[pair, 1 - order if s == 0 else half + 2 + order] = x1h[s, pair, order].astype(F32)
        for i in range(1, half + 3):
            x = x1p[pair, i]
            around = in_plane(x, width1) + x1p[pair, i - 1] + x1p[pair, i + 1]
            x = (1.0 + keep) * x + coeff1(i) * around
            m1[pair, i] = x
            low, high = x[:y2], x[y2:]
            left = lane_of(low) < width1
            ms[2 * pair, i - 1] = jnp.where(left, low, pltpu.roll(high, width1, 1)).astype(BF16)
            ms[2 * pair + 1, i - 1] = jnp.where(left, pltpu.roll(low, width1, 1), high).astype(BF16)
        for step in steps:
            peer = (v + step) % group
            begin(field_of(peer) // 2 == pair, ms.at[field_of(peer)], mr.at[v], sem_m, b, peer)

    for pair in range(pairs - 1):
        raise_m(pair)
    for s in range(2):
        arrive(has[s], f1h.at[s], sem_f1 + s)
        b2 = b2 + (0.125 * 0.25) * f1h[s]
    x20 = gd2 * b2
    x2s[...] = x20
    x2b[...] = x20.astype(BF16)
    quad = lane_of(x20[:tall2]) // width2
    for f in range(fields):
        slab = None
        for j in range(blocks):
            piece = x20[j * tall2:(j + 1) * tall2]
            if j != f:
                piece = pltpu.roll(piece, width2 * ((j - f) % blocks), 1)
            slab = piece if slab is None else jnp.where(quad == j, piece, slab)
        x2c[f] = slab.astype(BF16)

    for off in reversed(offs):
        for step in range(group):
            peer = (v + step) % group
            slot = reach - off
            begin(inside(off), x2c.at[field_of(peer)], sl.at[slot, v], sem_s + slot, b + off, peer)
    for step in steps:
        peer = (v + step) % group
        begin(None, x2c.at[field_of(peer)], sl.at[reach, v], sem_s + reach, b, peer)
    sl[reach, v] = x2c[field_of(v)]
    for off in reversed(offs):
        slot = reach - off
        if abs(off) <= NEAR:
            begin(inside(off), x2s, x2h.at[slot], sem_x2 + slot, b + off, v)
        else:
            begin(inside(off), x2b, x2hb.at[slot], sem_x2 + slot, b + off, v)

    raise_m(pairs - 1)
    mr[v] = ms[field_of(v)]

    coeff2 = {0: q2s[...]}
    for off in offs:
        arrive(inside(off), q2h.at[off + reach], sem_q2 + off + reach)
    for off in offs:
        c = q2h[off + reach]
        if abs(off) < SWEEPS:
            parts = []
            for j in range(blocks):
                m = jnp.where(lane_of(c) // width2 == j, c, 0.0)
                shift = width2
                while shift < zs:
                    m = m + pltpu.roll(m, shift, 1)
                    shift *= 2
                parts.append(m)
            coeff2[off] = jnp.concatenate(parts, axis=0)

    spread = spread_table(2, zs)
    beside = beside_table(2, zs)

    def sweeps(start):
        level2 = start
        zero = jnp.zeros_like(start[0])
        for sweep in range(1, SWEEPS):
            wide = SWEEPS - sweep
            after = {}
            for off in range(-min(wide, reach), min(wide, reach) + 1):
                x = level2[off]
                around = in_plane(x, width2) + level2.get(off - 1, zero) + level2.get(off + 1, zero)
                after[off] = keep * x + start[off] + coeff2[off] * around
            level2 = after
        return level2

    def lift_up(level2, at, room, dot):
        wide = dot(level2[at], spread)
        plane, flat = [], []
        for pair in range(2):
            view = room.at[pair]
            piece = wide[:, pair * zs:(pair + 1) * zs]
            view[pl.ds(0, y2, stride=2), :] = piece
            view[pl.ds(1, y2, stride=2), :] = piece
            plane.append(view[...])
            flat.append(in_plane(view[...], width1))
        return plane, flat

    def sides(x):
        row = lax.broadcasted_iota(jnp.int32, x.shape, 0)
        low = jnp.where(row == 0, 0.0, pltpu.roll(x, 1, 0))
        high = jnp.where(row == y1 - 1, 0.0, pltpu.roll(x, y1 - 1, 0))
        return low, high

    def half_dot(x, table):
        return jnp.dot(x.astype(BF16), table, preferred_element_type=F32)

    for off in offs:
        slot = off + reach
        arrive(inside(off), sl.at[slot], sem_s + slot)
    if group > 1:
        arrive(None, sl.at[reach, pl.ds(0, group - 1)], sem_s + reach)
    quads = group // blocks
    starts = [{} for _ in range(quads)]
    for off in range(-reach, reach + 1):
        for q in range(quads):
            parts = [None] * blocks
            for u in range(blocks):
                c = sl[off + reach, q * blocks + u].astype(F32)
                for j in range(blocks):
                    piece = c if j == u else pltpu.roll(c, width2 * ((u - j) % blocks), 1)
                    parts[j] = piece if u == 0 else jnp.where(quad == u, piece, parts[j])
            starts[q][off] = jnp.concatenate(parts, axis=0)
    ends = [sweeps(start) for start in starts]
    arrive(None, mr.at[pl.ds(0, group - 1)], sem_m)
    for q in range(quads):
        raised = [lift_up(ends[q], off, t4.at[off + 1], half_dot) for off in (-1, 0, 1)]
        for pair in range(2):
            first = q * blocks + 2 * pair
            for i in range(1, half + 3):
                even, odd = mr[first, i - 1].astype(F32), mr[first + 1, i - 1].astype(F32)
                left = lane_of(even) < width1
                mixed = jnp.concatenate([jnp.where(left, even, pltpu.roll(odd, width1, 1)),
                                         jnp.where(left, pltpu.roll(even, width1, 1), odd)], axis=0)
                at = i // half
                around = raised[at][1][pair] + raised[(i - 1) // half][0][pair] + raised[(i + 1) // half][0][pair]
                x = mixed + keep * raised[at][0][pair] + coeff1(i) * around
                x = x.astype(BF16)
                wide = jnp.dot(x, spread, preferred_element_type=F32)
                v1[first, i - 1] = wide[:, :zs]
                v1[first + 1, i - 1] = wide[:, zs:]
                if 2 <= i < half + 2:
                    wide = jnp.dot(x, beside, preferred_element_type=F32)
                    vz[first, i - 2] = wide[:, :zs]
                    vz[first + 1, i - 2] = wide[:, zs:]
    arrive(None, lr.at[pl.ds(0, group - 1)], sem_l)
    for i in range(share):
        p = i % planes if whole_fields else (v * share + i) % planes
        h, e = p // 2, p % 2
        gks = [gk.at[p][pl.ds(r, y1, stride=2), :] for r in range(2)]
        for u in range(group):
            x = v1[u, h + 1]
            around = vz[u, h] + 2.0 * x + v1[u, h + 2 * e]
            rims = sides(x)
            for r in range(2):
                z = lr[u, i, r].astype(F32) + keep * x + gks[r] * (around + rims[r])
                zr[u, i, r] = z.astype(BF16)

    rows = 16
    keys = [(i, j) for i in range(group) for j in range(i, group)]
    per = ys // rows

    def products(step, totals):
        unit = step // per
        first = pl.multiple_of(step % per * rows, rows)
        values = [zr[i, unit, first // y1, pl.ds(pl.multiple_of(first % y1, rows), rows), :].astype(F32)
                  for i in range(group)]
        return tuple(
            total + (values[i] * values[j]).reshape(rows // 8, 8, zs).sum(axis=0)
            for total, (i, j) in zip(totals, keys))

    totals = lax.fori_loop(0, share * per, products,
                           tuple(jnp.zeros((8, zs), F32) for _ in keys), unroll=4)
    lines = [None] * group
    lane = lax.broadcasted_iota(jnp.int32, (1, zs), 1)
    for (i, j), total in zip(keys, totals):
        value = jnp.sum(jnp.sum(total, axis=0, keepdims=True), axis=1, keepdims=True)
        for one, other in {(i, j), (j, i)}:
            placed = jnp.where(lane == other, value, 0.0)
            lines[one] = placed if lines[one] is None else lines[one] + placed
    for i in range(group):
        part[i] = lines[i]
    mine = part[v]
    def own():
        start = {0: x20}
        for off in offs:
            arrive(inside(off), (x2h if abs(off) <= NEAR else x2hb).at[off + reach], sem_x2 + off + reach)
        for off in offs:
            start[off] = x2h[off + reach] if abs(off) <= NEAR else x2hb[off + reach].astype(F32)
        level2 = sweeps(start)
        raised = [lift_up(level2, off, t2.at[off + 1], split_dot) for off in (-1, 0, 1)]
        for i in range(1, half + 3):
            for pair in range(pairs):
                at = i // half
                around = raised[at][1][pair] + raised[(i - 1) // half][0][pair] + raised[(i + 1) // half][0][pair]
                x = m1[pair, i] + keep * raised[at][0][pair] + coeff1(i) * around
                wide = split_dot(x, spread)
                w1[2 * pair, i - 1] = wide[:, :zs]
                w1[2 * pair + 1, i - 1] = wide[:, zs:]
                if 2 <= i < half + 2:
                    wide = split_dot(x, beside)
                    wz[2 * pair, i - 2] = wide[:, :zs]
                    wz[2 * pair + 1, i - 2] = wide[:, zs:]
        for f in range(fields):
            for h in range(half):
                x = w1[f, h + 1]
                base = wz[f, h] + 2.0 * x
                kept = keep * x
                rims = sides(x)
                for e in range(2):
                    p = 2 * h + e
                    around = base + w1[f, h + 2 * e]
                    for r in range(2):
                        rows = pl.ds(r, y1, stride=2)
                        out.at[0, f, p][rows, :] = (
                            lo.at[f, p][rows, :] + kept + gk.at[p][rows, :] * (around + rims[r]))


    if bricks * group <= ONE_ROUND:
        for index in range(1, bricks * group):
            brick, vec = (b + index // group) % bricks, (v + index % group) % group
            begin(None, part.at[vec], g2h.at[index], sem_g2, brick, vec)
        own()
        arrive(None, g2h.at[pl.ds(1, bricks * group - 1)], sem_g2)
        for index in range(1, bricks * group):
            mine = mine + g2h[index]
    else:
        for step in range(1, group):
            peer = (v + step) % group
            begin(None, part.at[peer], g1h.at[step], sem_g1, b, peer)
        own()
        arrive(None, g1h.at[pl.ds(1, group - 1)], sem_g1)
        for step in range(1, group):
            mine = mine + g1h[step]
        rows_s[...] = mine
        for step in range(1, bricks):
            begin(None, rows_s, g2h.at[step], sem_g2, (b + step) % bricks, v)
        arrive(None, g2h.at[pl.ds(1, bricks - 1)], sem_g2)
        for step in range(1, bricks):
            mine = mine + g2h[step]
    gram[...] = mine[:, :group]
    for cond, made in sends:
        if cond is None:
            made.wait_send()
        else:
            pl.when(cond)(made.wait_send)


def local(bricks, group, right_side, diffusivity):
    fields, planes, ys, zs = right_side.shape[1:]
    assert right_side.shape[0] == 1 and planes == 4 and ys == zs == 128 and fields == 4 and group % 4 == 0 and SWEEPS == 6
    pairs, half = fields // 2, planes // 2
    y1, y2 = ys // 2, ys // 4
    reach = min(SWEEPS, bricks - 1)
    units = fields * planes
    share = units // group
    slots = 2 * reach + 1
    ends = bricks * group if bricks * group <= ONE_ROUND else bricks
    count = 4 * pairs + 4 + 3 * slots + 4
    vm = pltpu.VMEM
    result, rows = pl.pallas_call(
        functools.partial(kernel, bricks, group, reach),
        out_shape=(
            jax.ShapeDtypeStruct(right_side.shape, F32),
            jax.ShapeDtypeStruct((1, group), F32),
        ),
        in_specs=[pl.BlockSpec(memory_space=pl.ANY)] * 2,
        out_specs=(pl.BlockSpec(memory_space=pltpu.VMEM),) * 2,
        scratch_shapes=[
            vm((fields, planes, ys, zs), F32),
            vm((planes, ys, zs), F32),
            vm((fields, planes, ys, zs), F32),
            vm((planes, ys, zs), F32),
            vm((planes, ys, zs), F32),
            vm((fields, planes, ys, zs), F32),
            vm((units, 2, y1, zs), BF16),
            vm((group, share, 2, y1, zs), BF16),
            vm((2, fields, ys, zs), BF16),
            vm((2, fields, ys, zs), BF16),
            vm((fields, half, ys, zs), F32),
            vm((half, ys, zs), F32),
            vm((half, y1, zs), F32),
            vm((half, y1, zs), F32),
            vm((2, y2, zs), F32),
            vm((2, y2, zs), F32),
            vm((2, y1, zs), F32),
            vm((2, y1, zs), F32),
            vm((pairs, half, y1, zs), F32),
            vm((pairs, half + 4, y1, zs), F32),
            vm((2, pairs, half, y1, zs), BF16),
            vm((2, pairs, half, y1, zs), BF16),
            vm((pairs, half + 4, y1, zs), F32),
            vm((pairs, y1, zs), F32),
            vm((2, pairs, y1, zs), F32),
            vm((2, y2, zs), F32),
            vm((2, y2, zs), F32),
            vm((y2, zs), F32),
            vm((8, zs), F32),
            vm((slots, 8, zs), F32),
            vm((y2, zs), F32),
            vm((y2, zs), BF16),
            vm((slots, y2, zs), F32),
            vm((slots, y2, zs), BF16),
            vm((fields, 8, zs), BF16),
            vm((slots, group, 8, zs), BF16),
            vm((3, pairs, y1, zs), F32),
            vm((3, 2, y1, zs), F32),
            vm((fields, half + 2, y2, zs), BF16),
            vm((group, half + 2, y2, zs), BF16),
            vm((fields, half + 2, y1, zs), F32),
            vm((fields, half, y1, zs), F32),
            vm((group, half + 2, y1, zs), F32),
            vm((group, half, y1, zs), F32),
            vm((group, share, 2, y1, zs), BF16),
            vm((group, 1, zs), F32),
            vm((group, 1, zs), F32),
            vm((1, zs), F32),
            vm((ends, 1, zs), F32),
            pltpu.SemaphoreType.REGULAR((2, 3)),
            pltpu.SemaphoreType.DMA((3,)),
            pltpu.SemaphoreType.DMA((count,)),
            pltpu.SemaphoreType.DMA((1,)),
        ],
        compiler_params=pltpu.CompilerParams(
            collective_id=0, has_side_effects=True, vmem_limit_bytes=48 << 20
        ),
    )(pltpu.with_memory_space_constraint(right_side, pltpu.HBM), pltpu.with_memory_space_constraint(diffusivity, pltpu.HBM))
    return pl.pallas_call(
        write,
        out_shape=(
            jax.ShapeDtypeStruct(right_side.shape, F32),
            jax.ShapeDtypeStruct((1, group), F32),
        ),
        in_specs=[pl.BlockSpec(memory_space=pltpu.VMEM)] * 2,
        out_specs=(pl.BlockSpec(memory_space=pl.ANY),) * 2,
        scratch_shapes=[pltpu.SemaphoreType.DMA((2,))],
    )(pltpu.with_memory_space_constraint(result, pltpu.VMEM), pltpu.with_memory_space_constraint(rows, pltpu.VMEM))


def solution(mesh):
    return jax.shard_map(
        functools.partial(local, mesh.shape["brick"], mesh.shape["vec"]),
        mesh=mesh,
        in_specs=(P("vec", None, "brick", None, None), P("brick", None, None)),
        out_specs=(P("vec", None, "brick", None, None), P("vec", None)),
        check_vma=False,
    )
```

```python
import functools

import jax
import jax.numpy as jnp
from jax import lax
from jax.experimental import pallas as pl
from jax.experimental.pallas import tpu as pltpu
from jax.sharding import PartitionSpec as P

SWEEPS = 6
NEAR = 2
ONE_ROUND = 64
shift_value = 0.1
damping = 0.8
keep = 1.0 - damping
F32 = jnp.float32
BF16 = jnp.bfloat16
MESH = pl.DeviceIdType.MESH


def rolled_sides(x, axis, width):
    size = x.shape[axis]
    place = lax.broadcasted_iota(jnp.int32, x.shape, axis) % width
    low = jnp.where(place == 0, 0.0, pltpu.roll(x, 1, axis))
    high = jnp.where(place == width - 1, 0.0, pltpu.roll(x, size - 1, axis))
    return low + high


def in_plane(x, width):
    return rolled_sides(x, 0, x.shape[0]) + rolled_sides(x, 1, width)


def split_dot(x, table):
    head = x.astype(BF16)
    tail = (x - head.astype(F32)).astype(BF16)
    return jnp.dot(head, table, preferred_element_type=F32) + jnp.dot(
        tail, table, preferred_element_type=F32
    )


def iotas(rows, cols):
    return (lax.broadcasted_iota(jnp.int32, (rows, cols), 0),
            lax.broadcasted_iota(jnp.int32, (rows, cols), 1))


def merge_table(parts, lanes):
    row, col = iotas(parts * lanes, lanes)
    return jnp.where(row // 2 == col, 1.0, 0.0).astype(BF16)


def spread_table(parts, lanes):
    row, col = iotas(lanes, parts * lanes)
    return jnp.where(col // 2 == row, 1.0, 0.0).astype(BF16)


def beside_table(parts, lanes):
    row, col = iotas(lanes, parts * lanes)
    place = col % lanes
    low = ((col - 1) // 2 == row) & (place > 0)
    high = ((col + 1) // 2 == row) & (place < lanes - 1)
    return jnp.where(low | high, 1.0, 0.0).astype(BF16)


def repeat_table(lanes, source, width):
    row, col = iotas(lanes, lanes)
    hit = (row // 2 == col % width) & (row < source)
    return jnp.where(hit, 1.0, 0.0).astype(BF16)


def lane_of(x):
    return lax.broadcasted_iota(jnp.int32, x.shape, x.ndim - 1)


def write(result, rows, out, gram, sems):
    copies = [pltpu.make_async_copy(result, out, sems.at[0]), pltpu.make_async_copy(rows, gram, sems.at[1])]
    for made in copies:
        made.start()
    for made in copies:
        made.wait()


def kernel(bricks, group, reach, rhs_in, kap_in, out, gram, rhs, kap, xp, g0, gk, lo, lb, lr, x0s, x0h, tmp,
           ktmp, k1s, q1s, k1c, k1h, k1e, q1e, b1s, x1p, x1b, x1h, m1, t1, t3, f1s, f1h, q2s, q2c, q2h, x2s, x2b,
           x2h, x2hb, x2c, sl, t2, t4, ms, mr, w1, wz, v1, vz, zr, part, g1h, rows_s, g2h, waves, sems_l, sems_r, sems_s):
    fields, planes, ys, zs = rhs.shape
    pairs = fields // 2
    y1, y2 = ys // 2, ys // 4
    width1, width2 = zs // 2, zs // 4
    half = planes // 2
    units = fields * planes
    share = units // group
    whole_fields = share % planes == 0
    b = lax.axis_index("brick")
    v = lax.axis_index("vec")
    has = (b > 0, b < bricks - 1)
    turns = (b % 2, 1 - b % 2)
    side = (-1, 1)
    edge = (0, planes - 1)
    edge1 = (0, half - 1)
    offs = [sign * size for size in range(1, reach + 1) for sign in (-1, 1)]
    counter = [0]
    sends = []

    def copy(src, dst, sem, brick, vec):
        return pltpu.make_async_remote_copy(
            src_ref=src, dst_ref=dst, send_sem=sems_s.at[0], recv_sem=sems_r.at[sem],
            device_id=(brick, vec), device_id_type=MESH)

    def begin(cond, src, dst, sem, brick, vec):
        made = copy(src, dst, sem, brick, vec)
        if cond is None:
            made.start()
        else:
            pl.when(cond)(made.start)
        sends.append((cond, made))

    def arrive(dst, sem):
        copy(dst, dst, sem, b, v).wait_recv()

    def number(count):
        base = counter[0]
        counter[0] += count
        return base

    def inside(off):
        return (b + off >= 0) & (b + off < bricks)

    def arrive_from(hops, view, sem):
        count = sum(inside(hop).astype(jnp.int32) for hop in hops)
        for n in sorted({sum(0 <= brick + hop < bricks for hop in hops) for brick in range(bricks)} - {0}):
            pl.when(count == n)(copy(view(n), view(n), sem, b, v).wait_recv)

    sem_x0, sem_x1 = number(pairs), number(pairs)
    sem_k1, sem_f1, sem_near, sem_far, sem_q2, sem_s, sem_c, sem_l, sem_m, sem_g1, sem_g2 = (
        number(1) for _ in range(11))
    near = [off for off in offs if abs(off) <= NEAR]
    far = [off for off in offs if abs(off) > NEAR]

    barrier = pltpu.get_barrier_semaphore()
    for s in range(2):
        @pl.when(has[s])
        def _(s=s):
            pl.semaphore_signal(barrier, inc=1, device_id=(b + side[s], v), device_id_type=MESH)
    for step in range(1, group):
        pl.semaphore_signal(barrier, inc=1, device_id=(b, (v + step) % group),
                            device_id_type=MESH)
    load_kap = pltpu.make_async_copy(kap_in, kap, sems_l.at[0])
    load_kap.start()
    for p in edge:
        pltpu.make_async_copy(rhs_in.at[0, :, p], rhs.at[:, p], sems_l.at[1]).start()
    load_mid = pltpu.make_async_copy(rhs_in.at[0, :, pl.ds(1, planes - 2)], rhs.at[:, pl.ds(1, planes - 2)],
                                     sems_l.at[2])
    load_mid.start()

    for s in range(2):
        @pl.when(jnp.logical_not(has[s]))
        def _(s=s):
            x0h[s] = jnp.zeros_like(x0h.at[s])
            x1h[s] = jnp.zeros_like(x1h.at[s])
            k1h[s] = jnp.zeros_like(k1h.at[s])
            f1h[s] = jnp.zeros_like(f1h.at[s])
    for off in offs:
        @pl.when(jnp.logical_not(inside(off)))
        def _(off=off):
            q2h[off + reach] = jnp.zeros_like(q2h.at[off + reach])
            sl[off + reach] = jnp.zeros_like(sl.at[off + reach])
            if abs(off) <= NEAR:
                x2h[off + reach] = jnp.zeros_like(x2h.at[off + reach])
            else:
                x2hb[off + reach] = jnp.zeros_like(x2hb.at[off + reach])

    load_kap.wait()
    for p in range(planes):
        g = damping / (shift_value + 6.0 * kap[p])
        g0[p] = g
        gk[p] = g * kap[p]
    pl.semaphore_wait(barrier, (b > 0).astype(jnp.int32) + (b < bricks - 1).astype(jnp.int32) + group - 1)
    pltpu.make_async_copy(rhs.at[:, pl.ds(0, 2)], rhs.at[:, pl.ds(0, 2)], sems_l.at[1]).wait()
    for f in range(fields):
        for s in range(2):
            x = g0[edge[s]] * rhs[f, edge[s]]
            xp[f, edge[s]] = x
            x0s[s, f] = x.astype(BF16)
    for s in turns:
        for f in range(fields):
            begin(inside(2 * s - 1), x0s.at[s, f], x0h.at[1 - s, f], sem_x0 + f // 2,
                  b + 2 * s - 1, v)

    def tell(stage, far):
        for s in range(2):
            @pl.when(inside(side[s] * far))
            def _(s=s):
                pl.semaphore_signal(waves.at[1 - s, stage], inc=1, device_id=(b + side[s] * far, v), device_id_type=MESH)

    def hear(stage, far):
        for s in range(2):
            @pl.when(inside(side[s] * far))
            def _(s=s):
                pl.semaphore_wait(waves.at[s, stage], 1)

    tell(0, 1)

    merge = merge_table(2, zs)
    for h in range(half):
        ktmp[h] = kap[2 * h] + kap[2 * h + 1]
    k1 = []
    for h in range(half):
        summed = ktmp.at[h][pl.ds(0, y1, stride=2), :] + ktmp.at[h][pl.ds(1, y1, stride=2), :]
        k = split_dot(summed, repeat_table(zs, zs, width1)) * 0.125
        k1s[h] = k
        k1.append(k)
    for s in range(2):
        k = k1[edge1[s]]
        low, high = k[:y2], k[y2:]
        k1c[s] = jnp.where(lane_of(low) < width1, low, high)
    for s in turns:
        begin(inside(2 * s - 1), k1c.at[s], k1h.at[1 - s], sem_k1, b + 2 * s - 1, v)
    gd1 = [damping / (shift_value + 6.0 * 0.25 * k) for k in k1]
    for h in range(half):
        q1s[h] = gd1[h] * (0.25 * k1[h])
    t1[0] = k1[0] + k1[1]
    summed = t1.at[0][pl.ds(0, y2, stride=2), :] + t1.at[0][pl.ds(1, y2, stride=2), :]
    k2 = split_dot(summed, repeat_table(zs, width1, width2)) * 0.125
    gd2 = damping / (shift_value + 6.0 * 0.0625 * k2)
    q2 = gd2 * (0.0625 * k2)
    q2s[...] = q2
    blocks = zs // width2
    tall2 = y2 // blocks
    packed = q2[:tall2]
    place = lane_of(packed) // width2
    for j in range(1, blocks):
        packed = jnp.where(place == j, q2[j * tall2:(j + 1) * tall2], packed)
    q2c[...] = packed

    load_mid.wait()
    for f in range(fields):
        for p in range(1, planes - 1):
            xp[f, p] = g0[p] * rhs[f, p]
    for f in range(fields):
        for h in range(half):
            total = None
            for p in (2 * h, 2 * h + 1):
                x = xp[f, p]
                around = in_plane(x, zs)
                if p > 0:
                    around = around + xp[f, p - 1]
                if p < planes - 1:
                    around = around + xp[f, p + 1]
                resid = keep * rhs[f, p] + kap[p] * around
                lo[f, p] = x + g0[p] * resid
                total = resid if total is None else total + resid
            tmp[f, h] = total

    def pack(f, p):
        view = lo.at[f, p]
        for e in range(2):
            lb[f * planes + p, e] = view[pl.ds(e, y1, stride=2), :].astype(BF16)

    steps = sorted(range(1, group), key=lambda step: -min(step, group - step))

    def share_out(first, count):
        for step in steps:
            peer = (v + step) % group
            begin(None, lb.at[pl.ds(peer * share + first, count)], lr.at[v, pl.ds(first, count)], sem_l, b, peer)

    early = share == planes
    for f in range(fields):
        for p in range(1, planes - 1):
            pack(f, p)
    if early:
        share_out(1, planes - 2)

    def send_x1(pair):
        for s in range(2):
            for order in range(half):
                plane = order if s == 0 else half - 1 - order
                x1b[s, pair, order] = x1p[pair, plane + 2].astype(BF16)
        for s in turns:
            begin(inside(2 * s - 1), x1b.at[s, pair], x1h.at[1 - s, pair], sem_x1 + pair,
                  b + 2 * s - 1, v)

    hear(0, 1)
    tell(1, 2)
    for pair in range(pairs):
        halved = [[None] * 2 for _ in range(half)]
        arrive_from(side, lambda n: x0h.at[pl.ds(0, n), pl.ds(2 * pair, 2)], sem_x0 + pair)
        for inner in range(2):
            f = 2 * pair + inner
            for s in range(2):
                p = edge[s]
                flux = kap[p] * x0h[s, f].astype(F32)
                tmp[f, edge1[s]] = tmp[f, edge1[s]] + flux
                lo[f, p] = lo[f, p] + g0[p] * flux
            for h in range(half):
                view = tmp.at[f, h]
                halved[h][inner] = view[pl.ds(0, y1, stride=2), :] + view[pl.ds(1, y1, stride=2), :]
        for h in range(half):
            b1 = split_dot(jnp.concatenate(halved[h], axis=1), merge) * 0.125
            b1s[pair, h] = b1
            x1p[pair, h + 2] = gd1[h] * b1
        if pair < pairs - 1:
            send_x1(pair)
        if pair == 0:
            hear(1, 2)
            tell(2, 2)
    hear(2, 2)

    arrive_from(side, lambda n: k1h.at[pl.ds(0, n)], sem_k1)
    for s in range(2):
        c = k1h[s]
        turned = pltpu.roll(c, width1, 1)
        lane = lane_of(c)
        k1e[s, :y2] = jnp.where(lane < width1, c, turned)
        k1e[s, y2:] = jnp.where(lane < width1, turned, c)
        halved = []
        for pair in range(pairs):
            t3[s, pair] = k1e[s] * x1p[pair, edge1[s] + 2]
            view = t3.at[s, pair]
            halved.append(view[pl.ds(0, y2, stride=2), :] + view[pl.ds(1, y2, stride=2), :])
        f1s[s] = split_dot(jnp.concatenate(halved, axis=1), merge)
    for s in turns:
        begin(inside(2 * s - 1), f1s.at[s], f1h.at[1 - s], sem_f1, b + 2 * s - 1, v)
    send_x1(pairs - 1)
    for off in offs:
        begin(inside(off), q2c, q2h.at[reach - off], sem_q2, b + off, v)

    for f in range(fields):
        for s in range(2):
            pack(f, edge[s])
    if early:
        share_out(0, 1)
        share_out(planes - 1, 1)
    else:
        share_out(0, share)

    for i in range(share):
        lr[v, i] = lb[v * share + i]
    halved = []
    for pair in range(pairs):
        total = None
        for h in range(half):
            around = in_plane(x1p[pair, h + 2], width1)
            if h > 0:
                around = around + x1p[pair, h + 1]
            if h < half - 1:
                around = around + x1p[pair, h + 3]
            resid = keep * b1s[pair, h] + 0.25 * k1s[h] * around
            total = resid if total is None else total + resid
        t1[pair] = total
        view = t1.at[pair]
        halved.append(view[pl.ds(0, y2, stride=2), :] + view[pl.ds(1, y2, stride=2), :])
    b2 = split_dot(jnp.concatenate(halved, axis=1), merge) * 0.125

    for s in range(2):
        k = k1e[s]
        q1e[s] = damping / (shift_value + 6.0 * 0.25 * k) * (0.25 * k)

    def coeff1(i):
        return q1e[0] if i == 1 else q1e[1] if i == half + 2 else q1s[i - 2]

    def field_of(vec):
        return vec * share // planes

    def raise_m(pair):
        arrive_from(side, lambda n: x1h.at[pl.ds(0, n), pair], sem_x1 + pair)
        for s in range(2):
            for order in range(half):
                x1p[pair, 1 - order if s == 0 else half + 2 + order] = x1h[s, pair, order].astype(F32)
        for i in range(1, half + 3):
            x = x1p[pair, i]
            around = in_plane(x, width1) + x1p[pair, i - 1] + x1p[pair, i + 1]
            x = (1.0 + keep) * x + coeff1(i) * around
            m1[pair, i] = x
            low, high = x[:y2], x[y2:]
            left = lane_of(low) < width1
            ms[2 * pair, i - 1] = jnp.where(left, low, pltpu.roll(high, width1, 1)).astype(BF16)
            ms[2 * pair + 1, i - 1] = jnp.where(left, pltpu.roll(low, width1, 1), high).astype(BF16)
        for step in steps:
            peer = (v + step) % group
            begin(field_of(peer) // 2 == pair, ms.at[field_of(peer)], mr.at[v], sem_m, b, peer)

    for pair in range(pairs - 1):
        raise_m(pair)
    arrive_from(side, lambda n: f1h.at[pl.ds(0, n)], sem_f1)
    for s in range(2):
        b2 = b2 + (0.125 * 0.25) * f1h[s]
    x20 = gd2 * b2
    x2s[...] = x20
    x2b[...] = x20.astype(BF16)
    quad = lane_of(x20[:tall2]) // width2
    for f in range(fields):
        slab = None
        for j in range(blocks):
            piece = x20[j * tall2:(j + 1) * tall2]
            if j != f:
                piece = pltpu.roll(piece, width2 * ((j - f) % blocks), 1)
            slab = piece if slab is None else jnp.where(quad == j, piece, slab)
        x2c[f] = slab.astype(BF16)

    for off in reversed(offs):
        for step in range(group):
            peer = (v + step) % group
            slot = reach - off
            begin(inside(off), x2c.at[field_of(peer)], sl.at[slot, v], sem_s, b + off, peer)
    for step in steps:
        peer = (v + step) % group
        begin(None, x2c.at[field_of(peer)], sl.at[reach, v], sem_c, b, peer)
    sl[reach, v] = x2c[field_of(v)]
    for off in reversed(offs):
        slot = reach - off
        if abs(off) <= NEAR:
            begin(inside(off), x2s, x2h.at[slot], sem_near, b + off, v)
        else:
            begin(inside(off), x2b, x2hb.at[slot], sem_far, b + off, v)

    raise_m(pairs - 1)
    mr[v] = ms[field_of(v)]

    coeff2 = {0: q2s[...]}
    arrive_from(offs, lambda n: q2h.at[pl.ds(0, n)], sem_q2)
    for off in offs:
        c = q2h[off + reach]
        if abs(off) < SWEEPS:
            parts = []
            for j in range(blocks):
                m = jnp.where(lane_of(c) // width2 == j, c, 0.0)
                shift = width2
                while shift < zs:
                    m = m + pltpu.roll(m, shift, 1)
                    shift *= 2
                parts.append(m)
            coeff2[off] = jnp.concatenate(parts, axis=0)

    spread = spread_table(2, zs)
    beside = beside_table(2, zs)

    def sweeps(start):
        level2 = start
        zero = jnp.zeros_like(start[0])
        for sweep in range(1, SWEEPS):
            wide = SWEEPS - sweep
            after = {}
            for off in range(-min(wide, reach), min(wide, reach) + 1):
                x = level2[off]
                around = in_plane(x, width2) + level2.get(off - 1, zero) + level2.get(off + 1, zero)
                after[off] = keep * x + start[off] + coeff2[off] * around
            level2 = after
        return level2

    def lift_up(level2, at, room, dot):
        wide = dot(level2[at], spread)
        plane, flat = [], []
        for pair in range(2):
            view = room.at[pair]
            piece = wide[:, pair * zs:(pair + 1) * zs]
            view[pl.ds(0, y2, stride=2), :] = piece
            view[pl.ds(1, y2, stride=2), :] = piece
            plane.append(view[...])
            flat.append(in_plane(view[...], width1))
        return plane, flat

    def sides(x):
        row = lax.broadcasted_iota(jnp.int32, x.shape, 0)
        low = jnp.where(row == 0, 0.0, pltpu.roll(x, 1, 0))
        high = jnp.where(row == y1 - 1, 0.0, pltpu.roll(x, y1 - 1, 0))
        return low, high

    def half_dot(x, table):
        return jnp.dot(x.astype(BF16), table, preferred_element_type=F32)

    arrive_from(offs, lambda n: sl.at[pl.ds(0, n)], sem_s)
    arrive(sl.at[reach, pl.ds(0, group - 1)], sem_c)
    quads = group // blocks
    starts = [{} for _ in range(quads)]
    for off in range(-reach, reach + 1):
        for q in range(quads):
            parts = [None] * blocks
            for u in range(blocks):
                c = sl[off + reach, q * blocks + u].astype(F32)
                for j in range(blocks):
                    piece = c if j == u else pltpu.roll(c, width2 * ((u - j) % blocks), 1)
                    parts[j] = piece if u == 0 else jnp.where(quad == u, piece, parts[j])
            starts[q][off] = jnp.concatenate(parts, axis=0)
    ends = [sweeps(start) for start in starts]
    arrive(mr.at[pl.ds(0, group - 1)], sem_m)
    for q in range(quads):
        raised = [lift_up(ends[q], off, t4.at[off + 1], half_dot) for off in (-1, 0, 1)]
        for pair in range(2):
            first = q * blocks + 2 * pair
            for i in range(1, half + 3):
                even, odd = mr[first, i - 1].astype(F32), mr[first + 1, i - 1].astype(F32)
                left = lane_of(even) < width1
                mixed = jnp.concatenate([jnp.where(left, even, pltpu.roll(odd, width1, 1)),
                                         jnp.where(left, pltpu.roll(even, width1, 1), odd)], axis=0)
                at = i // half
                around = raised[at][1][pair] + raised[(i - 1) // half][0][pair] + raised[(i + 1) // half][0][pair]
                x = mixed + keep * raised[at][0][pair] + coeff1(i) * around
                x = x.astype(BF16)
                wide = jnp.dot(x, spread, preferred_element_type=F32)
                v1[first, i - 1] = wide[:, :zs]
                v1[first + 1, i - 1] = wide[:, zs:]
                if 2 <= i < half + 2:
                    wide = jnp.dot(x, beside, preferred_element_type=F32)
                    vz[first, i - 2] = wide[:, :zs]
                    vz[first + 1, i - 2] = wide[:, zs:]
    arrive(lr.at[pl.ds(0, group - 1)], sem_l)
    for i in range(share):
        p = i % planes if whole_fields else (v * share + i) % planes
        h, e = p // 2, p % 2
        gks = [gk.at[p][pl.ds(r, y1, stride=2), :] for r in range(2)]
        for u in range(group):
            x = v1[u, h + 1]
            around = vz[u, h] + 2.0 * x + v1[u, h + 2 * e]
            rims = sides(x)
            for r in range(2):
                z = lr[u, i, r].astype(F32) + keep * x + gks[r] * (around + rims[r])
                zr[u, i, r] = z.astype(BF16)

    rows = 16
    keys = [(i, j) for i in range(group) for j in range(i, group)]
    per = ys // rows

    def products(step, totals):
        unit = step // per
        first = pl.multiple_of(step % per * rows, rows)
        values = [zr[i, unit, first // y1, pl.ds(pl.multiple_of(first % y1, rows), rows), :].astype(F32)
                  for i in range(group)]
        return tuple(
            total + (values[i] * values[j]).reshape(rows // 8, 8, zs).sum(axis=0)
            for total, (i, j) in zip(totals, keys))

    totals = lax.fori_loop(0, share * per, products,
                           tuple(jnp.zeros((8, zs), F32) for _ in keys), unroll=4)
    lines = [None] * group
    lane = lax.broadcasted_iota(jnp.int32, (1, zs), 1)
    for (i, j), total in zip(keys, totals):
        value = jnp.sum(jnp.sum(total, axis=0, keepdims=True), axis=1, keepdims=True)
        for one, other in {(i, j), (j, i)}:
            placed = jnp.where(lane == other, value, 0.0)
            lines[one] = placed if lines[one] is None else lines[one] + placed
    for i in range(group):
        part[i] = lines[i]
    mine = part[v]
    def own():
        start = {0: x20}
        arrive_from(near, lambda n: x2h.at[pl.ds(0, n)], sem_near)
        if far:
            arrive_from(far, lambda n: x2hb.at[pl.ds(0, n)], sem_far)
        for off in offs:
            start[off] = x2h[off + reach] if abs(off) <= NEAR else x2hb[off + reach].astype(F32)
        level2 = sweeps(start)
        raised = [lift_up(level2, off, t2.at[off + 1], split_dot) for off in (-1, 0, 1)]
        for i in range(1, half + 3):
            for pair in range(pairs):
                at = i // half
                around = raised[at][1][pair] + raised[(i - 1) // half][0][pair] + raised[(i + 1) // half][0][pair]
                x = m1[pair, i] + keep * raised[at][0][pair] + coeff1(i) * around
                wide = split_dot(x, spread)
                w1[2 * pair, i - 1] = wide[:, :zs]
                w1[2 * pair + 1, i - 1] = wide[:, zs:]
                if 2 <= i < half + 2:
                    wide = split_dot(x, beside)
                    wz[2 * pair, i - 2] = wide[:, :zs]
                    wz[2 * pair + 1, i - 2] = wide[:, zs:]
        for f in range(fields):
            for h in range(half):
                x = w1[f, h + 1]
                base = wz[f, h] + 2.0 * x
                kept = keep * x
                rims = sides(x)
                for e in range(2):
                    p = 2 * h + e
                    around = base + w1[f, h + 2 * e]
                    for r in range(2):
                        rows = pl.ds(r, y1, stride=2)
                        out.at[0, f, p][rows, :] = (
                            lo.at[f, p][rows, :] + kept + gk.at[p][rows, :] * (around + rims[r]))


    if bricks * group <= ONE_ROUND:
        for index in range(1, bricks * group):
            brick, vec = (b + index // group) % bricks, (v + index % group) % group
            begin(None, part.at[vec], g2h.at[index], sem_g2, brick, vec)
        own()
        arrive(g2h.at[pl.ds(1, bricks * group - 1)], sem_g2)
        for index in range(1, bricks * group):
            mine = mine + g2h[index]
    else:
        for step in range(1, group):
            peer = (v + step) % group
            begin(None, part.at[peer], g1h.at[step], sem_g1, b, peer)
        own()
        arrive(g1h.at[pl.ds(1, group - 1)], sem_g1)
        for step in range(1, group):
            mine = mine + g1h[step]
        rows_s[...] = mine
        for step in range(1, bricks):
            begin(None, rows_s, g2h.at[step], sem_g2, (b + step) % bricks, v)
        arrive(g2h.at[pl.ds(1, bricks - 1)], sem_g2)
        for step in range(1, bricks):
            mine = mine + g2h[step]
    gram[...] = mine[:, :group]
    for cond, made in sends:
        if cond is None:
            made.wait_send()
        else:
            pl.when(cond)(made.wait_send)


def local(bricks, group, right_side, diffusivity):
    fields, planes, ys, zs = right_side.shape[1:]
    assert right_side.shape[0] == 1 and planes == 4 and ys == zs == 128 and fields == 4 and group % 4 == 0 and SWEEPS == 6
    pairs, half = fields // 2, planes // 2
    y1, y2 = ys // 2, ys // 4
    reach = min(SWEEPS, bricks - 1)
    units = fields * planes
    share = units // group
    slots = 2 * reach + 1
    ends = bricks * group if bricks * group <= ONE_ROUND else bricks
    count = 2 * pairs + 11
    vm = pltpu.VMEM
    result, rows = pl.pallas_call(
        functools.partial(kernel, bricks, group, reach),
        out_shape=(
            jax.ShapeDtypeStruct(right_side.shape, F32),
            jax.ShapeDtypeStruct((1, group), F32),
        ),
        in_specs=[pl.BlockSpec(memory_space=pl.ANY)] * 2,
        out_specs=(pl.BlockSpec(memory_space=pltpu.VMEM),) * 2,
        scratch_shapes=[
            vm((fields, planes, ys, zs), F32),
            vm((planes, ys, zs), F32),
            vm((fields, planes, ys, zs), F32),
            vm((planes, ys, zs), F32),
            vm((planes, ys, zs), F32),
            vm((fields, planes, ys, zs), F32),
            vm((units, 2, y1, zs), BF16),
            vm((group, share, 2, y1, zs), BF16),
            vm((2, fields, ys, zs), BF16),
            vm((2, fields, ys, zs), BF16),
            vm((fields, half, ys, zs), F32),
            vm((half, ys, zs), F32),
            vm((half, y1, zs), F32),
            vm((half, y1, zs), F32),
            vm((2, y2, zs), F32),
            vm((2, y2, zs), F32),
            vm((2, y1, zs), F32),
            vm((2, y1, zs), F32),
            vm((pairs, half, y1, zs), F32),
            vm((pairs, half + 4, y1, zs), F32),
            vm((2, pairs, half, y1, zs), BF16),
            vm((2, pairs, half, y1, zs), BF16),
            vm((pairs, half + 4, y1, zs), F32),
            vm((pairs, y1, zs), F32),
            vm((2, pairs, y1, zs), F32),
            vm((2, y2, zs), F32),
            vm((2, y2, zs), F32),
            vm((y2, zs), F32),
            vm((8, zs), F32),
            vm((slots, 8, zs), F32),
            vm((y2, zs), F32),
            vm((y2, zs), BF16),
            vm((slots, y2, zs), F32),
            vm((slots, y2, zs), BF16),
            vm((fields, 8, zs), BF16),
            vm((slots, group, 8, zs), BF16),
            vm((3, pairs, y1, zs), F32),
            vm((3, 2, y1, zs), F32),
            vm((fields, half + 2, y2, zs), BF16),
            vm((group, half + 2, y2, zs), BF16),
            vm((fields, half + 2, y1, zs), F32),
            vm((fields, half, y1, zs), F32),
            vm((group, half + 2, y1, zs), F32),
            vm((group, half, y1, zs), F32),
            vm((group, share, 2, y1, zs), BF16),
            vm((group, 1, zs), F32),
            vm((group, 1, zs), F32),
            vm((1, zs), F32),
            vm((ends, 1, zs), F32),
            pltpu.SemaphoreType.REGULAR((2, 3)),
            pltpu.SemaphoreType.DMA((3,)),
            pltpu.SemaphoreType.DMA((count,)),
            pltpu.SemaphoreType.DMA((1,)),
        ],
        compiler_params=pltpu.CompilerParams(
            collective_id=0, has_side_effects=True, vmem_limit_bytes=48 << 20
        ),
    )(pltpu.with_memory_space_constraint(right_side, pltpu.HBM), pltpu.with_memory_space_constraint(diffusivity, pltpu.HBM))
    return pl.pallas_call(
        write,
        out_shape=(
            jax.ShapeDtypeStruct(right_side.shape, F32),
            jax.ShapeDtypeStruct((1, group), F32),
        ),
        in_specs=[pl.BlockSpec(memory_space=pltpu.VMEM)] * 2,
        out_specs=(pl.BlockSpec(memory_space=pl.ANY),) * 2,
        scratch_shapes=[pltpu.SemaphoreType.DMA((2,))],
    )(pltpu.with_memory_space_constraint(result, pltpu.VMEM), pltpu.with_memory_space_constraint(rows, pltpu.VMEM))


def solution(mesh):
    return jax.shard_map(
        functools.partial(local, mesh.shape["brick"], mesh.shape["vec"]),
        mesh=mesh,
        in_specs=(P("vec", None, "brick", None, None), P("brick", None, None)),
        out_specs=(P("vec", None, "brick", None, None), P("vec", None)),
        check_vma=False,
    )
```

```python
import functools

import jax
import jax.numpy as jnp
from jax import lax
from jax.experimental import pallas as pl
from jax.experimental.pallas import tpu as pltpu
from jax.sharding import PartitionSpec as P

SWEEPS = 6
NEAR = 2
ONE_ROUND = 64
shift_value = 0.1
damping = 0.8
keep = 1.0 - damping
F32 = jnp.float32
BF16 = jnp.bfloat16
MESH = pl.DeviceIdType.MESH


def rolled_sides(x, axis, width):
    size = x.shape[axis]
    place = lax.broadcasted_iota(jnp.int32, x.shape, axis) % width
    low = jnp.where(place == 0, 0.0, pltpu.roll(x, 1, axis))
    high = jnp.where(place == width - 1, 0.0, pltpu.roll(x, size - 1, axis))
    return low + high


def in_plane(x, width):
    return rolled_sides(x, 0, x.shape[0]) + rolled_sides(x, 1, width)


def split_dot(x, table):
    head = x.astype(BF16)
    tail = (x - head.astype(F32)).astype(BF16)
    return jnp.dot(head, table, preferred_element_type=F32) + jnp.dot(
        tail, table, preferred_element_type=F32
    )


def iotas(rows, cols):
    return (lax.broadcasted_iota(jnp.int32, (rows, cols), 0),
            lax.broadcasted_iota(jnp.int32, (rows, cols), 1))


def merge_table(parts, lanes):
    row, col = iotas(parts * lanes, lanes)
    return jnp.where(row // 2 == col, 1.0, 0.0).astype(BF16)


def spread_table(parts, lanes):
    row, col = iotas(lanes, parts * lanes)
    return jnp.where(col // 2 == row, 1.0, 0.0).astype(BF16)


def beside_table(parts, lanes):
    row, col = iotas(lanes, parts * lanes)
    place = col % lanes
    low = ((col - 1) // 2 == row) & (place > 0)
    high = ((col + 1) // 2 == row) & (place < lanes - 1)
    return jnp.where(low | high, 1.0, 0.0).astype(BF16)


def repeat_table(lanes, source, width):
    row, col = iotas(lanes, lanes)
    hit = (row // 2 == col % width) & (row < source)
    return jnp.where(hit, 1.0, 0.0).astype(BF16)


def lane_of(x):
    return lax.broadcasted_iota(jnp.int32, x.shape, x.ndim - 1)


def write(result, rows, out, gram, sems):
    copies = [pltpu.make_async_copy(result, out, sems.at[0]), pltpu.make_async_copy(rows, gram, sems.at[1])]
    for made in copies:
        made.start()
    for made in copies:
        made.wait()


def kernel(bricks, group, reach, rhs_in, kap_in, out, gram, rhs, kap, xp, g0, gk, lo, lb, lr, x0s, x0h, tmp,
           ktmp, k1s, q1s, kaps, kaph, fix, f1e, k1c, k1h, k1e, q1e, b1s, x1p, x1b, x1h, m1, t1, t3, f1s, f1h, q2s, q2c, q2h, x2s, x2b,
           x2h, x2hb, x2c, sl, t2, t4, ms, mr, w1, wz, v1, vz, zr, part, g1h, rows_s, g2h, waves, sems_l, sems_r, sems_s):
    fields, planes, ys, zs = rhs.shape
    pairs = fields // 2
    y1, y2 = ys // 2, ys // 4
    width1, width2 = zs // 2, zs // 4
    half = planes // 2
    units = fields * planes
    share = units // group
    whole_fields = share % planes == 0
    b = lax.axis_index("brick")
    v = lax.axis_index("vec")
    has = (b > 0, b < bricks - 1)
    turns = (b % 2, 1 - b % 2)
    side = (-1, 1)
    edge = (0, planes - 1)
    edge1 = (0, half - 1)
    offs = [sign * size for size in range(1, reach + 1) for sign in (-1, 1)]
    counter = [0]
    sends = []

    def copy(src, dst, sem, brick, vec):
        return pltpu.make_async_remote_copy(
            src_ref=src, dst_ref=dst, send_sem=sems_s.at[0], recv_sem=sems_r.at[sem],
            device_id=(brick, vec), device_id_type=MESH)

    def begin(cond, src, dst, sem, brick, vec):
        made = copy(src, dst, sem, brick, vec)
        if cond is None:
            made.start()
        else:
            pl.when(cond)(made.start)
        sends.append((cond, made))

    def arrive(dst, sem):
        copy(dst, dst, sem, b, v).wait_recv()

    def number(count):
        base = counter[0]
        counter[0] += count
        return base

    def inside(off):
        return (b + off >= 0) & (b + off < bricks)

    def arrive_from(hops, view, sem):
        count = sum(inside(hop).astype(jnp.int32) for hop in hops)
        for n in sorted({sum(0 <= brick + hop < bricks for hop in hops) for brick in range(bricks)} - {0}):
            pl.when(count == n)(copy(view(n), view(n), sem, b, v).wait_recv)

    sem_x0, sem_x1 = number(pairs), number(pairs)
    sem_kap, sem_k1 = number(2), number(2)
    sem_f1, sem_near, sem_far, sem_q2, sem_s, sem_c, sem_l, sem_m, sem_g1, sem_g2 = (
        number(1) for _ in range(10))
    near = [off for off in offs if abs(off) <= NEAR]
    far = [off for off in offs if abs(off) > NEAR]

    barrier = pltpu.get_barrier_semaphore()
    for s in range(2):
        @pl.when(has[s])
        def _(s=s):
            pl.semaphore_signal(barrier, inc=1, device_id=(b + side[s], v), device_id_type=MESH)
    for step in range(1, group):
        pl.semaphore_signal(barrier, inc=1, device_id=(b, (v + step) % group),
                            device_id_type=MESH)
    load_kap = pltpu.make_async_copy(kap_in, kap, sems_l.at[0])
    load_kap.start()
    for p in edge:
        pltpu.make_async_copy(rhs_in.at[0, :, p], rhs.at[:, p], sems_l.at[1]).start()
    load_mid = pltpu.make_async_copy(rhs_in.at[0, :, pl.ds(1, planes - 2)], rhs.at[:, pl.ds(1, planes - 2)],
                                     sems_l.at[2])
    load_mid.start()

    for s in range(2):
        @pl.when(jnp.logical_not(has[s]))
        def _(s=s):
            x0h[s] = jnp.zeros_like(x0h.at[s])
            x1h[s] = jnp.zeros_like(x1h.at[s])
            k1h[s] = jnp.zeros_like(k1h.at[s])
            kaph[s] = jnp.zeros_like(kaph.at[s])
            f1h[s] = jnp.zeros_like(f1h.at[s])
    for off in offs:
        @pl.when(jnp.logical_not(inside(off)))
        def _(off=off):
            q2h[off + reach] = jnp.zeros_like(q2h.at[off + reach])
            sl[off + reach] = jnp.zeros_like(sl.at[off + reach])
            if abs(off) <= NEAR:
                x2h[off + reach] = jnp.zeros_like(x2h.at[off + reach])
            else:
                x2hb[off + reach] = jnp.zeros_like(x2hb.at[off + reach])

    load_kap.wait()
    for p in range(planes):
        g = damping / (shift_value + 6.0 * kap[p])
        g0[p] = g
        gk[p] = g * kap[p]
    for s in range(2):
        for r in range(2):
            kaps[s, r] = kap[edge[s], r * y1:(r + 1) * y1].astype(BF16)
    pl.semaphore_wait(barrier, (b > 0).astype(jnp.int32) + (b < bricks - 1).astype(jnp.int32) + group - 1)
    core = v % 2
    mate = v + 1 - 2 * core
    for s in turns:
        begin(inside(2 * s - 1), kaps.at[s, core], kaph.at[1 - s, core], sem_kap, b + 2 * s - 1, v)
    pltpu.make_async_copy(rhs.at[:, pl.ds(0, 2)], rhs.at[:, pl.ds(0, 2)], sems_l.at[1]).wait()
    for f in range(fields):
        for s in range(2):
            x = g0[edge[s]] * rhs[f, edge[s]]
            xp[f, edge[s]] = x
            x0s[s, f] = x.astype(BF16)

    def tell(stage, far):
        for s in range(2):
            @pl.when(inside(side[s] * far))
            def _(s=s):
                pl.semaphore_signal(waves.at[1 - s, stage], inc=1, device_id=(b + side[s] * far, v), device_id_type=MESH)

    def hear(stage, far):
        for s in range(2):
            @pl.when(inside(side[s] * far))
            def _(s=s):
                pl.semaphore_wait(waves.at[s, stage], 1)

    tell(0, 1)

    merge = merge_table(2, zs)
    for h in range(half):
        ktmp[h] = kap[2 * h] + kap[2 * h + 1]
    k1 = []
    for h in range(half):
        summed = ktmp.at[h][pl.ds(0, y1, stride=2), :] + ktmp.at[h][pl.ds(1, y1, stride=2), :]
        k = split_dot(summed, repeat_table(zs, zs, width1)) * 0.125
        k1s[h] = k
        k1.append(k)
    for s in range(2):
        k = k1[edge1[s]]
        low, high = k[:y2], k[y2:]
        packed = jnp.where(lane_of(low) < width1, low, high)
        for r in range(2):
            k1c[s, r] = packed[r * y2 // 2:(r + 1) * y2 // 2]
    for s in turns:
        begin(inside(2 * s - 1), k1c.at[s, core], k1h.at[1 - s, core], sem_k1, b + 2 * s - 1, v)
    for pair in range(pairs):
        for s in turns:
            both = pl.ds(2 * pair, 2)
            begin(inside(2 * s - 1), x0s.at[s, both], x0h.at[1 - s, both], sem_x0 + pair, b + 2 * s - 1, v)

    gd1 = [damping / (shift_value + 6.0 * 0.25 * k) for k in k1]
    for h in range(half):
        q1s[h] = gd1[h] * (0.25 * k1[h])
    t1[0] = k1[0] + k1[1]
    summed = t1.at[0][pl.ds(0, y2, stride=2), :] + t1.at[0][pl.ds(1, y2, stride=2), :]
    k2 = split_dot(summed, repeat_table(zs, width1, width2)) * 0.125
    gd2 = damping / (shift_value + 6.0 * 0.0625 * k2)
    q2 = gd2 * (0.0625 * k2)
    q2s[...] = q2
    blocks = zs // width2
    tall2 = y2 // blocks
    packed = q2[:tall2]
    place = lane_of(packed) // width2
    for j in range(1, blocks):
        packed = jnp.where(place == j, q2[j * tall2:(j + 1) * tall2], packed)
    q2c[...] = packed

    load_mid.wait()
    for f in range(fields):
        for p in range(1, planes - 1):
            xp[f, p] = g0[p] * rhs[f, p]
    for f in range(fields):
        for h in range(half):
            total = None
            for p in (2 * h, 2 * h + 1):
                x = xp[f, p]
                around = in_plane(x, zs)
                if p > 0:
                    around = around + xp[f, p - 1]
                if p < planes - 1:
                    around = around + xp[f, p + 1]
                resid = keep * rhs[f, p] + kap[p] * around
                lo[f, p] = x + g0[p] * resid
                total = resid if total is None else total + resid
            tmp[f, h] = total

    def pack(f, p):
        view = lo.at[f, p]
        for e in range(2):
            lb[f * planes + p, e] = view[pl.ds(e, y1, stride=2), :].astype(BF16)

    def place_of(vec):
        return vec % 2 * (group // 2) + vec // 2

    steps = sorted(range(1, group), key=lambda step: -min(step, group - step))

    def field_of(vec):
        return place_of(vec) * share // planes

    def share_out(first, count, chosen):
        for step in steps:
            peer = (v + step) % group
            begin(chosen(peer), lb.at[pl.ds(place_of(peer) * share + first, count)], lr.at[v, pl.ds(first, count)],
                  sem_l, b, peer)

    early = share == planes
    for f in range(fields):
        for p in range(1, planes - 1):
            pack(f, p)
    if early:
        share_out(1, planes - 2, lambda peer: None)

    def send_x1(pair, orders):
        for s in range(2):
            for order in orders:
                plane = order if s == 0 else half - 1 - order
                x1b[s, pair, order] = x1p[pair, plane + 2].astype(BF16)
        for s in turns:
            part = pl.ds(orders[0], len(orders))
            begin(inside(2 * s - 1), x1b.at[s, pair, part], x1h.at[1 - s, pair, part], sem_x1 + pair,
                  b + 2 * s - 1, v)

    hear(0, 1)
    tell(1, 2)

    def to_level1(source):
        for pair in range(pairs):
            parts = [view[pl.ds(0, y1, stride=2), :] + view[pl.ds(1, y1, stride=2), :]
                     for view in (source(2 * pair), source(2 * pair + 1))]
            yield pair, split_dot(jnp.concatenate(parts, axis=1), merge) * 0.125

    def to_level2(source):
        parts = [view[pl.ds(0, y2, stride=2), :] + view[pl.ds(1, y2, stride=2), :] for view in map(source, range(pairs))]
        return split_dot(jnp.concatenate(parts, axis=1), merge)

    for h in range(half):
        for pair, b1 in to_level1(lambda f: tmp.at[f, h]):
            b1s[pair, h] = b1
            x1p[pair, h + 2] = gd1[h] * b1
    for halo, sem in ((k1h, sem_k1), (kaph, sem_kap)):
        arrive_from(side, lambda n: halo.at[pl.ds(0, n), 0], sem)
        for s in range(2):
            begin(has[s], halo.at[s, core], halo.at[s, core], sem + 1, b, mate)
    arrive_from(side, lambda n: k1h.at[pl.ds(0, n), 0], sem_k1 + 1)
    for s in range(2):
        c = jnp.concatenate([k1h[s, 0], k1h[s, 1]], axis=0)
        turned = pltpu.roll(c, width1, 1)
        lane = lane_of(c)
        k1e[s, :y2] = jnp.where(lane < width1, c, turned)
        k1e[s, y2:] = jnp.where(lane < width1, turned, c)
        for pair in range(pairs):
            t3[s, pair] = k1e[s] * x1p[pair, edge1[s] + 2]
        f1s[s] = to_level2(lambda pair: t3.at[s, pair])
    for s in turns:
        begin(inside(2 * s - 1), f1s.at[s], f1h.at[1 - s], sem_f1, b + 2 * s - 1, v)
    hear(1, 2)
    tell(2, 3)

    def fix_f1():
        arrive_from(side, lambda n: kaph.at[pl.ds(0, n), 0], sem_kap + 1)
        for s in range(2):
            k = k1e[s]
            gd = damping / (shift_value + 6.0 * 0.25 * k)
            q1e[s] = gd * (0.25 * k)
            for f in range(fields):
                for r in range(2):
                    rows = slice(r * y1, (r + 1) * y1)
                    fix[f, rows] = kaph[s, r].astype(F32) * xp[f, edge[s], rows]
            for pair, flux in to_level1(lambda f: fix.at[f]):
                t3[s, pair] = k1s[edge1[s]] * gd * flux
            f1e[s] = to_level2(lambda pair: t3.at[s, pair])

    def rim_out(pair):
        for f in (2 * pair, 2 * pair + 1):
            for s in range(2):
                pack(f, edge[s])
        if early:
            for p in edge:
                share_out(p, 1, lambda peer: field_of(peer) // 2 == pair)
        elif pair == pairs - 1:
            share_out(0, share, lambda peer: None)

    for pair in range(pairs):
        arrive_from(side, lambda n: x0h.at[pl.ds(0, n), pl.ds(2 * pair, 2)], sem_x0 + pair)
        for s in range(2):
            p, h = edge[s], edge1[s]
            halved = []
            for f in (2 * pair, 2 * pair + 1):
                flux = kap[p] * x0h[s, f].astype(F32)
                tmp[f, h] = flux
                lo[f, p] = lo[f, p] + g0[p] * flux
                view = tmp.at[f, h]
                halved.append(view[pl.ds(0, y1, stride=2), :] + view[pl.ds(1, y1, stride=2), :])
            b1 = split_dot(jnp.concatenate(halved, axis=1), merge) * 0.125
            b1s[pair, h] = b1s[pair, h] + b1
            x1p[pair, h + 2] = x1p[pair, h + 2] + gd1[h] * b1
        if pair < pairs - 1:
            send_x1(pair, tuple(range(half)))
        if pair == 0:
            fix_f1()
            rim_out(pair)
            hear(2, 3)
            for off in offs:
                begin(inside(off), q2c, q2h.at[reach - off], sem_q2, b + off, v)

    send_x1(pairs - 1, tuple(range(half)))
    halved = []
    for pair in range(pairs):
        total = None
        for h in range(half):
            around = in_plane(x1p[pair, h + 2], width1)
            if h > 0:
                around = around + x1p[pair, h + 1]
            if h < half - 1:
                around = around + x1p[pair, h + 3]
            resid = keep * b1s[pair, h] + 0.25 * k1s[h] * around
            total = resid if total is None else total + resid
        t1[pair] = total
        view = t1.at[pair]
        halved.append(view[pl.ds(0, y2, stride=2), :] + view[pl.ds(1, y2, stride=2), :])
    b2 = split_dot(jnp.concatenate(halved, axis=1), merge) * 0.125

    arrive_from(side, lambda n: f1h.at[pl.ds(0, n)], sem_f1)
    for s in range(2):
        b2 = b2 + (0.125 * 0.25) * (f1h[s] + f1e[s])
    x20 = gd2 * b2
    x2s[...] = x20
    x2b[...] = x20.astype(BF16)
    quad = lane_of(x20[:tall2]) // width2
    for f in range(fields):
        slab = None
        for j in range(blocks):
            piece = x20[j * tall2:(j + 1) * tall2]
            if j != f:
                piece = pltpu.roll(piece, width2 * ((j - f) % blocks), 1)
            slab = piece if slab is None else jnp.where(quad == j, piece, slab)
        x2c[f] = slab.astype(BF16)

    for off in reversed(offs):
        for step in range(group):
            peer = (v + step) % group
            slot = reach - off
            begin(inside(off), x2c.at[field_of(peer)], sl.at[slot, v], sem_s, b + off, peer)
    for step in steps:
        peer = (v + step) % group
        begin(None, x2c.at[field_of(peer)], sl.at[reach, v], sem_c, b, peer)
    sl[reach, v] = x2c[field_of(v)]
    for off in reversed(offs):
        slot = reach - off
        if abs(off) <= NEAR:
            begin(inside(off), x2s, x2h.at[slot], sem_near, b + off, v)
        else:
            begin(inside(off), x2b, x2hb.at[slot], sem_far, b + off, v)

    rim_out(pairs - 1)
    for i in range(share):
        lr[v, i] = lb[place_of(v) * share + i]
    def coeff1(i):
        return q1e[0] if i == 1 else q1e[1] if i == half + 2 else q1s[i - 2]

    def raise_m(pair):
        arrive_from(side, lambda n: x1h.at[pl.ds(0, n), pair], sem_x1 + pair)
        for s in range(2):
            for order in range(half):
                x1p[pair, 1 - order if s == 0 else half + 2 + order] = x1h[s, pair, order].astype(F32)
        for i in range(1, half + 3):
            x = x1p[pair, i]
            around = in_plane(x, width1) + x1p[pair, i - 1] + x1p[pair, i + 1]
            x = (1.0 + keep) * x + coeff1(i) * around
            m1[pair, i] = x
            low, high = x[:y2], x[y2:]
            left = lane_of(low) < width1
            ms[2 * pair, i - 1] = jnp.where(left, low, pltpu.roll(high, width1, 1)).astype(BF16)
            ms[2 * pair + 1, i - 1] = jnp.where(left, pltpu.roll(low, width1, 1), high).astype(BF16)
        for step in steps:
            peer = (v + step) % group
            begin(field_of(peer) // 2 == pair, ms.at[field_of(peer)], mr.at[v], sem_m, b, peer)

    for pair in range(pairs - 1):
        raise_m(pair)
    raise_m(pairs - 1)
    mr[v] = ms[field_of(v)]

    coeff2 = {0: q2s[...]}
    arrive_from(offs, lambda n: q2h.at[pl.ds(0, n)], sem_q2)
    for off in offs:
        c = q2h[off + reach]
        if abs(off) < SWEEPS:
            parts = []
            for j in range(blocks):
                m = jnp.where(lane_of(c) // width2 == j, c, 0.0)
                shift = width2
                while shift < zs:
                    m = m + pltpu.roll(m, shift, 1)
                    shift *= 2
                parts.append(m)
            coeff2[off] = jnp.concatenate(parts, axis=0)

    spread = spread_table(2, zs)
    beside = beside_table(2, zs)

    def sweeps(start):
        level2 = start
        zero = jnp.zeros_like(start[0])
        for sweep in range(1, SWEEPS):
            wide = SWEEPS - sweep
            after = {}
            for off in range(-min(wide, reach), min(wide, reach) + 1):
                x = level2[off]
                around = in_plane(x, width2) + level2.get(off - 1, zero) + level2.get(off + 1, zero)
                after[off] = keep * x + start[off] + coeff2[off] * around
            level2 = after
        return level2

    def lift_up(level2, at, room, dot):
        wide = dot(level2[at], spread)
        plane, flat = [], []
        for pair in range(2):
            view = room.at[pair]
            piece = wide[:, pair * zs:(pair + 1) * zs]
            view[pl.ds(0, y2, stride=2), :] = piece
            view[pl.ds(1, y2, stride=2), :] = piece
            plane.append(view[...])
            flat.append(in_plane(view[...], width1))
        return plane, flat

    def sides(x):
        row = lax.broadcasted_iota(jnp.int32, x.shape, 0)
        low = jnp.where(row == 0, 0.0, pltpu.roll(x, 1, 0))
        high = jnp.where(row == y1 - 1, 0.0, pltpu.roll(x, y1 - 1, 0))
        return low, high

    def half_dot(x, table):
        return jnp.dot(x.astype(BF16), table, preferred_element_type=F32)

    arrive_from(offs, lambda n: sl.at[pl.ds(0, n)], sem_s)
    arrive(sl.at[reach, pl.ds(0, group - 1)], sem_c)
    quads = group // blocks
    starts = [{} for _ in range(quads)]
    for off in range(-reach, reach + 1):
        for q in range(quads):
            parts = [None] * blocks
            for u in range(blocks):
                c = sl[off + reach, q * blocks + u].astype(F32)
                for j in range(blocks):
                    piece = c if j == u else pltpu.roll(c, width2 * ((u - j) % blocks), 1)
                    parts[j] = piece if u == 0 else jnp.where(quad == u, piece, parts[j])
            starts[q][off] = jnp.concatenate(parts, axis=0)
    ends = [sweeps(start) for start in starts]
    arrive(mr.at[pl.ds(0, group - 1)], sem_m)
    for q in range(quads):
        raised = [lift_up(ends[q], off, t4.at[off + 1], half_dot) for off in (-1, 0, 1)]
        for pair in range(2):
            first = q * blocks + 2 * pair
            for i in range(1, half + 3):
                even, odd = mr[first, i - 1].astype(F32), mr[first + 1, i - 1].astype(F32)
                left = lane_of(even) < width1
                mixed = jnp.concatenate([jnp.where(left, even, pltpu.roll(odd, width1, 1)),
                                         jnp.where(left, pltpu.roll(even, width1, 1), odd)], axis=0)
                at = i // half
                around = raised[at][1][pair] + raised[(i - 1) // half][0][pair] + raised[(i + 1) // half][0][pair]
                x = mixed + keep * raised[at][0][pair] + coeff1(i) * around
                x = x.astype(BF16)
                wide = jnp.dot(x, spread, preferred_element_type=F32)
                v1[first, i - 1] = wide[:, :zs]
                v1[first + 1, i - 1] = wide[:, zs:]
                if 2 <= i < half + 2:
                    wide = jnp.dot(x, beside, preferred_element_type=F32)
                    vz[first, i - 2] = wide[:, :zs]
                    vz[first + 1, i - 2] = wide[:, zs:]
    arrive(lr.at[pl.ds(0, group - 1)], sem_l)
    for i in range(share):
        p = i % planes if whole_fields else (place_of(v) * share + i) % planes
        h, e = p // 2, p % 2
        gks = [gk.at[p][pl.ds(r, y1, stride=2), :] for r in range(2)]
        for u in range(group):
            x = v1[u, h + 1]
            around = vz[u, h] + 2.0 * x + v1[u, h + 2 * e]
            rims = sides(x)
            for r in range(2):
                z = lr[u, i, r].astype(F32) + keep * x + gks[r] * (around + rims[r])
                zr[u, i, r] = z.astype(BF16)

    rows = 16
    keys = [(i, j) for i in range(group) for j in range(i, group)]
    per = ys // rows

    def products(step, totals):
        unit = step // per
        first = pl.multiple_of(step % per * rows, rows)
        values = [zr[i, unit, first // y1, pl.ds(pl.multiple_of(first % y1, rows), rows), :].astype(F32)
                  for i in range(group)]
        return tuple(
            total + (values[i] * values[j]).reshape(rows // 8, 8, zs).sum(axis=0)
            for total, (i, j) in zip(totals, keys))

    totals = lax.fori_loop(0, share * per, products,
                           tuple(jnp.zeros((8, zs), F32) for _ in keys), unroll=4)
    lines = [None] * group
    lane = lax.broadcasted_iota(jnp.int32, (1, zs), 1)
    for (i, j), total in zip(keys, totals):
        value = jnp.sum(jnp.sum(total, axis=0, keepdims=True), axis=1, keepdims=True)
        for one, other in {(i, j), (j, i)}:
            placed = jnp.where(lane == other, value, 0.0)
            lines[one] = placed if lines[one] is None else lines[one] + placed
    for i in range(group):
        part[i] = lines[i]
    mine = part[v]
    def own():
        start = {0: x20}
        arrive_from(near, lambda n: x2h.at[pl.ds(0, n)], sem_near)
        if far:
            arrive_from(far, lambda n: x2hb.at[pl.ds(0, n)], sem_far)
        for off in offs:
            start[off] = x2h[off + reach] if abs(off) <= NEAR else x2hb[off + reach].astype(F32)
        level2 = sweeps(start)
        raised = [lift_up(level2, off, t2.at[off + 1], split_dot) for off in (-1, 0, 1)]
        for i in range(1, half + 3):
            for pair in range(pairs):
                at = i // half
                around = raised[at][1][pair] + raised[(i - 1) // half][0][pair] + raised[(i + 1) // half][0][pair]
                x = m1[pair, i] + keep * raised[at][0][pair] + coeff1(i) * around
                wide = split_dot(x, spread)
                w1[2 * pair, i - 1] = wide[:, :zs]
                w1[2 * pair + 1, i - 1] = wide[:, zs:]
                if 2 <= i < half + 2:
                    wide = split_dot(x, beside)
                    wz[2 * pair, i - 2] = wide[:, :zs]
                    wz[2 * pair + 1, i - 2] = wide[:, zs:]
        for f in range(fields):
            for h in range(half):
                x = w1[f, h + 1]
                base = wz[f, h] + 2.0 * x
                kept = keep * x
                rims = sides(x)
                for e in range(2):
                    p = 2 * h + e
                    around = base + w1[f, h + 2 * e]
                    for r in range(2):
                        rows = pl.ds(r, y1, stride=2)
                        out.at[0, f, p][rows, :] = (
                            lo.at[f, p][rows, :] + kept + gk.at[p][rows, :] * (around + rims[r]))


    if bricks * group <= ONE_ROUND:
        for index in range(1, bricks * group):
            brick, vec = (b + index // group) % bricks, (v + index % group) % group
            begin(None, part.at[vec], g2h.at[index], sem_g2, brick, vec)
        own()
        arrive(g2h.at[pl.ds(1, bricks * group - 1)], sem_g2)
        for index in range(1, bricks * group):
            mine = mine + g2h[index]
    else:
        for step in range(1, group):
            peer = (v + step) % group
            begin(None, part.at[peer], g1h.at[step], sem_g1, b, peer)
        own()
        arrive(g1h.at[pl.ds(1, group - 1)], sem_g1)
        for step in range(1, group):
            mine = mine + g1h[step]
        rows_s[...] = mine
        for step in range(1, bricks):
            begin(None, rows_s, g2h.at[step], sem_g2, (b + step) % bricks, v)
        arrive(g2h.at[pl.ds(1, bricks - 1)], sem_g2)
        for step in range(1, bricks):
            mine = mine + g2h[step]
    gram[...] = mine[:, :group]
    for cond, made in sends:
        if cond is None:
            made.wait_send()
        else:
            pl.when(cond)(made.wait_send)


def local(bricks, group, right_side, diffusivity):
    fields, planes, ys, zs = right_side.shape[1:]
    assert right_side.shape[0] == 1 and planes == 4 and ys == zs == 128 and fields == 4 and group % 4 == 0 and SWEEPS == 6
    pairs, half = fields // 2, planes // 2
    y1, y2 = ys // 2, ys // 4
    reach = min(SWEEPS, bricks - 1)
    units = fields * planes
    share = units // group
    slots = 2 * reach + 1
    ends = bricks * group if bricks * group <= ONE_ROUND else bricks
    count = 2 * pairs + 14
    vm = pltpu.VMEM
    result, rows = pl.pallas_call(
        functools.partial(kernel, bricks, group, reach),
        out_shape=(
            jax.ShapeDtypeStruct(right_side.shape, F32),
            jax.ShapeDtypeStruct((1, group), F32),
        ),
        in_specs=[pl.BlockSpec(memory_space=pl.ANY)] * 2,
        out_specs=(pl.BlockSpec(memory_space=pltpu.VMEM),) * 2,
        scratch_shapes=[
            vm((fields, planes, ys, zs), F32),
            vm((planes, ys, zs), F32),
            vm((fields, planes, ys, zs), F32),
            vm((planes, ys, zs), F32),
            vm((planes, ys, zs), F32),
            vm((fields, planes, ys, zs), F32),
            vm((units, 2, y1, zs), BF16),
            vm((group, share, 2, y1, zs), BF16),
            vm((2, fields, ys, zs), BF16),
            vm((2, fields, ys, zs), BF16),
            vm((fields, half, ys, zs), F32),
            vm((half, ys, zs), F32),
            vm((half, y1, zs), F32),
            vm((half, y1, zs), F32),
            vm((2, 2, y1, zs), BF16),
            vm((2, 2, y1, zs), BF16),
            vm((fields, ys, zs), F32),
            vm((2, y2, zs), F32),
            vm((2, 2, y2 // 2, zs), F32),
            vm((2, 2, y2 // 2, zs), F32),
            vm((2, y1, zs), F32),
            vm((2, y1, zs), F32),
            vm((pairs, half, y1, zs), F32),
            vm((pairs, half + 4, y1, zs), F32),
            vm((2, pairs, half, y1, zs), BF16),
            vm((2, pairs, half, y1, zs), BF16),
            vm((pairs, half + 4, y1, zs), F32),
            vm((pairs, y1, zs), F32),
            vm((2, pairs, y1, zs), F32),
            vm((2, y2, zs), F32),
            vm((2, y2, zs), F32),
            vm((y2, zs), F32),
            vm((8, zs), F32),
            vm((slots, 8, zs), F32),
            vm((y2, zs), F32),
            vm((y2, zs), BF16),
            vm((slots, y2, zs), F32),
            vm((slots, y2, zs), BF16),
            vm((fields, 8, zs), BF16),
            vm((slots, group, 8, zs), BF16),
            vm((3, pairs, y1, zs), F32),
            vm((3, 2, y1, zs), F32),
            vm((fields, half + 2, y2, zs), BF16),
            vm((group, half + 2, y2, zs), BF16),
            vm((fields, half + 2, y1, zs), F32),
            vm((fields, half, y1, zs), F32),
            vm((group, half + 2, y1, zs), F32),
            vm((group, half, y1, zs), F32),
            vm((group, share, 2, y1, zs), BF16),
            vm((group, 1, zs), F32),
            vm((group, 1, zs), F32),
            vm((1, zs), F32),
            vm((ends, 1, zs), F32),
            pltpu.SemaphoreType.REGULAR((2, 3)),
            pltpu.SemaphoreType.DMA((3,)),
            pltpu.SemaphoreType.DMA((count,)),
            pltpu.SemaphoreType.DMA((1,)),
        ],
        compiler_params=pltpu.CompilerParams(
            collective_id=0, has_side_effects=True, vmem_limit_bytes=48 << 20
        ),
    )(pltpu.with_memory_space_constraint(right_side, pltpu.HBM), pltpu.with_memory_space_constraint(diffusivity, pltpu.HBM))
    return pl.pallas_call(
        write,
        out_shape=(
            jax.ShapeDtypeStruct(right_side.shape, F32),
            jax.ShapeDtypeStruct((1, group), F32),
        ),
        in_specs=[pl.BlockSpec(memory_space=pltpu.VMEM)] * 2,
        out_specs=(pl.BlockSpec(memory_space=pl.ANY),) * 2,
        scratch_shapes=[pltpu.SemaphoreType.DMA((2,))],
    )(pltpu.with_memory_space_constraint(result, pltpu.VMEM), pltpu.with_memory_space_constraint(rows, pltpu.VMEM))


def solution(mesh):
    return jax.shard_map(
        functools.partial(local, mesh.shape["brick"], mesh.shape["vec"]),
        mesh=mesh,
        in_specs=(P("vec", None, "brick", None, None), P("brick", None, None)),
        out_specs=(P("vec", None, "brick", None, None), P("vec", None)),
        check_vma=False,
    )
```

```python
import functools

import jax
import jax.numpy as jnp
from jax import lax
from jax.experimental import pallas as pl
from jax.experimental.pallas import tpu as pltpu
from jax.sharding import PartitionSpec as P

SWEEPS = 6
NEAR = 2
ONE_ROUND = 64
shift_value = 0.1
damping = 0.8
keep = 1.0 - damping
F32 = jnp.float32
BF16 = jnp.bfloat16
MESH = pl.DeviceIdType.MESH


def rolled_sides(x, axis, width):
    size = x.shape[axis]
    place = lax.broadcasted_iota(jnp.int32, x.shape, axis) % width
    low = jnp.where(place == 0, 0.0, pltpu.roll(x, 1, axis))
    high = jnp.where(place == width - 1, 0.0, pltpu.roll(x, size - 1, axis))
    return low + high


def in_plane(x, width):
    return rolled_sides(x, 0, x.shape[0]) + rolled_sides(x, 1, width)


def split_dot(x, table):
    head = x.astype(BF16)
    tail = (x - head.astype(F32)).astype(BF16)
    return jnp.dot(head, table, preferred_element_type=F32) + jnp.dot(
        tail, table, preferred_element_type=F32
    )


def iotas(rows, cols):
    return (lax.broadcasted_iota(jnp.int32, (rows, cols), 0),
            lax.broadcasted_iota(jnp.int32, (rows, cols), 1))


def merge_table(parts, lanes):
    row, col = iotas(parts * lanes, lanes)
    return jnp.where(row // 2 == col, 1.0, 0.0).astype(BF16)


def spread_table(parts, lanes):
    row, col = iotas(lanes, parts * lanes)
    return jnp.where(col // 2 == row, 1.0, 0.0).astype(BF16)


def beside_table(parts, lanes, width):
    row, col = iotas(lanes, parts * lanes)
    place = col % width
    low = ((col - 1) // 2 == row) & (place > 0)
    high = ((col + 1) // 2 == row) & (place < width - 1)
    return jnp.where(low | high, 1.0, 0.0).astype(BF16)


def repeat_table(lanes, source, width):
    row, col = iotas(lanes, lanes)
    hit = (row // 2 == col % width) & (row < source)
    return jnp.where(hit, 1.0, 0.0).astype(BF16)


def lane_of(x):
    return lax.broadcasted_iota(jnp.int32, x.shape, x.ndim - 1)


def write(result, rows, out, gram, sems):
    copies = [pltpu.make_async_copy(result, out, sems.at[0]), pltpu.make_async_copy(rows, gram, sems.at[1])]
    for made in copies:
        made.start()
    for made in copies:
        made.wait()


def kernel(bricks, group, reach, rhs_in, kap_in, out, gram, rhs, kap, xp, g0, gk, lo, lb, lr, x0s, x0h, tmp,
           ktmp, k1s, q1s, kaps, kaph, fix, f1e, k1c, k1h, k1e, q1e, b1s, x1p, x1b, x1h, m1, t1, t3, f1s, f1h, q2s, q2c, q2h, x2s, x2b,
           x2h, x2hb, x2c, sl, t2, t4, t5, pad2, ms, mr, w1, wz, v1, vz, part, g1h, rows_s, g2h, waves, sems_l, sems_r, sems_s):
    fields, planes, ys, zs = rhs.shape
    pairs = fields // 2
    y1, y2 = ys // 2, ys // 4
    width1, width2 = zs // 2, zs // 4
    half = planes // 2
    units = fields * planes
    share = units // group
    whole_fields = share % planes == 0
    b = lax.axis_index("brick")
    v = lax.axis_index("vec")
    has = (b > 0, b < bricks - 1)
    turns = (b % 2, 1 - b % 2)
    side = (-1, 1)
    edge = (0, planes - 1)
    edge1 = (0, half - 1)
    offs = [sign * size for size in range(1, reach + 1) for sign in (-1, 1)]
    counter = [0]
    sends = []

    def copy(src, dst, sem, brick, vec):
        return pltpu.make_async_remote_copy(
            src_ref=src, dst_ref=dst, send_sem=sems_s.at[0], recv_sem=sems_r.at[sem],
            device_id=(brick, vec), device_id_type=MESH)

    def begin(cond, *asked):
        asked = [asked] if len(asked) == 5 else asked[0]

        def start():
            for one in asked:
                copy(*one).start()

        def finish():
            for one in asked:
                copy(*one).wait_send()

        if cond is None:
            start()
            sends.append(finish)
        else:
            pl.when(cond)(start)
            sends.append(lambda: pl.when(cond)(finish))

    def arrive(dst, sem):
        copy(dst, dst, sem, b, v).wait_recv()

    def number(count):
        base = counter[0]
        counter[0] += count
        return base

    def inside(off):
        return (b + off >= 0) & (b + off < bricks)

    def arrive_from(hops, view, sem):
        count = sum(inside(hop).astype(jnp.int32) for hop in hops)
        for n in sorted({sum(0 <= brick + hop < bricks for hop in hops) for brick in range(bricks)} - {0}):
            pl.when(count == n)(copy(view(n), view(n), sem, b, v).wait_recv)

    sem_x0, sem_x1 = number(pairs), number(pairs)
    sem_kap, sem_k1 = number(2), number(2)
    sem_f1, sem_near, sem_far, sem_q2, sem_s, sem_c, sem_l, sem_m, sem_g1, sem_g2 = (
        number(1) for _ in range(10))
    near = [off for off in offs if abs(off) <= NEAR]
    far = [off for off in offs if abs(off) > NEAR]

    load_kap = pltpu.make_async_copy(kap_in, kap, sems_l.at[0])
    load_kap.start()
    for p in edge:
        pltpu.make_async_copy(rhs_in.at[0, :, p], rhs.at[:, p], sems_l.at[1]).start()
    load_mid = pltpu.make_async_copy(rhs_in.at[0, :, pl.ds(1, planes - 2)], rhs.at[:, pl.ds(1, planes - 2)],
                                     sems_l.at[2])
    load_mid.start()

    barrier = pltpu.get_barrier_semaphore()
    for s in range(2):
        @pl.when(has[s])
        def _(s=s):
            pl.semaphore_signal(barrier, inc=1, device_id=(b + side[s], v), device_id_type=MESH)
    for step in range(1, group):
        pl.semaphore_signal(barrier, inc=1, device_id=(b, (v + step) % group),
                            device_id_type=MESH)
    for pad in (t4, v1):
        for rows in (pl.ds(0, 8), pl.ds(y1 + 8, 8)):
            pad[:, :, rows, :] = jnp.zeros_like(pad.at[:, :, rows, :])
    for rows in (pl.ds(0, 8), pl.ds(y2 + 8, 8)):
        pad2[:, rows, :] = jnp.zeros_like(pad2.at[:, rows, :])
    for s in range(2):
        @pl.when(jnp.logical_not(has[s]))
        def _(s=s):
            x0h[s] = jnp.zeros_like(x0h.at[s])
            x1h[s] = jnp.zeros_like(x1h.at[s])
            k1h[s] = jnp.zeros_like(k1h.at[s])
            kaph[s] = jnp.zeros_like(kaph.at[s])
            f1h[s] = jnp.zeros_like(f1h.at[s])
    for off in offs:
        @pl.when(jnp.logical_not(inside(off)))
        def _(off=off):
            q2h[off + reach] = jnp.zeros_like(q2h.at[off + reach])
            sl[off + reach] = jnp.zeros_like(sl.at[off + reach])
            if abs(off) <= NEAR:
                x2h[off + reach] = jnp.zeros_like(x2h.at[off + reach])
            else:
                x2hb[off + reach] = jnp.zeros_like(x2hb.at[off + reach])

    load_kap.wait()
    for p in range(planes):
        g = damping / (shift_value + 6.0 * kap[p])
        g0[p] = g
        gk[p] = g * kap[p]
    for s in range(2):
        for r in range(2):
            kaps[s, r] = kap[edge[s], r * y1:(r + 1) * y1].astype(BF16)
    pl.semaphore_wait(barrier, (b > 0).astype(jnp.int32) + (b < bricks - 1).astype(jnp.int32) + group - 1)
    core = v % 2
    mate = v + 1 - 2 * core
    for s in turns:
        begin(inside(2 * s - 1), kaps.at[s, core], kaph.at[1 - s, core], sem_kap, b + 2 * s - 1, v)
    pltpu.make_async_copy(rhs.at[:, pl.ds(0, 2)], rhs.at[:, pl.ds(0, 2)], sems_l.at[1]).wait()
    for f in range(fields):
        for s in range(2):
            x = g0[edge[s]] * rhs[f, edge[s]]
            xp[f, edge[s]] = x
            x0s[s, f] = x.astype(BF16)

    def tell(stage, far):
        for s in range(2):
            @pl.when(inside(side[s] * far))
            def _(s=s):
                pl.semaphore_signal(waves.at[1 - s, stage], inc=1, device_id=(b + side[s] * far, v), device_id_type=MESH)

    def hear(stage, far):
        for s in range(2):
            @pl.when(inside(side[s] * far))
            def _(s=s):
                pl.semaphore_wait(waves.at[s, stage], 1)

    tell(0, 1)

    merge = merge_table(2, zs)
    for h in range(half):
        ktmp[h] = kap[2 * h] + kap[2 * h + 1]
    k1 = []
    for h in range(half):
        summed = ktmp.at[h][pl.ds(0, y1, stride=2), :] + ktmp.at[h][pl.ds(1, y1, stride=2), :]
        k = split_dot(summed, repeat_table(zs, zs, width1)) * 0.125
        k1s[h] = k
        k1.append(k)
    for s in range(2):
        k = k1[edge1[s]]
        low, high = k[:y2], k[y2:]
        packed = jnp.where(lane_of(low) < width1, low, high)
        for r in range(2):
            k1c[s, r] = packed[r * y2 // 2:(r + 1) * y2 // 2]
    for s in turns:
        begin(inside(2 * s - 1), k1c.at[s, core], k1h.at[1 - s, core], sem_k1, b + 2 * s - 1, v)
    for pair in range(pairs):
        for s in turns:
            both = pl.ds(2 * pair, 2)
            begin(inside(2 * s - 1), x0s.at[s, both], x0h.at[1 - s, both], sem_x0 + pair, b + 2 * s - 1, v)

    gd1 = [damping / (shift_value + 6.0 * 0.25 * k) for k in k1]
    for h in range(half):
        q1s[h] = gd1[h] * (0.25 * k1[h])
    t1[0] = k1[0] + k1[1]
    summed = t1.at[0][pl.ds(0, y2, stride=2), :] + t1.at[0][pl.ds(1, y2, stride=2), :]
    k2 = split_dot(summed, repeat_table(zs, width1, width2)) * 0.125
    gd2 = damping / (shift_value + 6.0 * 0.0625 * k2)
    q2 = gd2 * (0.0625 * k2)
    q2s[...] = q2
    blocks = zs // width2
    tall2 = y2 // blocks
    packed = q2[:tall2]
    place = lane_of(packed) // width2
    for j in range(1, blocks):
        packed = jnp.where(place == j, q2[j * tall2:(j + 1) * tall2], packed)
    q2c[...] = packed

    load_mid.wait()
    for f in range(fields):
        for p in range(1, planes - 1):
            xp[f, p] = g0[p] * rhs[f, p]
    for f in range(fields):
        for h in range(half):
            total = None
            for p in (2 * h, 2 * h + 1):
                x = xp[f, p]
                around = in_plane(x, zs)
                if p > 0:
                    around = around + xp[f, p - 1]
                if p < planes - 1:
                    around = around + xp[f, p + 1]
                resid = keep * rhs[f, p] + kap[p] * around
                lo[f, p] = x + g0[p] * resid
                total = resid if total is None else total + resid
            tmp[f, h] = total

    def pack(f, p):
        view = lo.at[f, p]
        for e in range(2):
            lb[f * planes + p, e] = view[pl.ds(e, y1, stride=2), :].astype(BF16)

    def place_of(vec):
        return vec % 2 * (group // 2) + vec // 2

    steps = sorted(range(1, group), key=lambda step: -min(step, group - step))

    def field_of(vec):
        return place_of(vec) * share // planes

    def share_out(first, count, chosen):
        for step in steps:
            peer = (v + step) % group
            begin(chosen(peer), lb.at[pl.ds(place_of(peer) * share + first, count)], lr.at[v, pl.ds(first, count)],
                  sem_l, b, peer)

    early = share == planes
    for f in range(fields):
        for p in range(1, planes - 1):
            pack(f, p)
    if early:
        share_out(1, planes - 2, lambda peer: None)

    def send_x1(pair, orders):
        for s in range(2):
            for order in orders:
                plane = order if s == 0 else half - 1 - order
                x1b[s, pair, order] = x1p[pair, plane + 2].astype(BF16)
        for s in turns:
            part = pl.ds(orders[0], len(orders))
            begin(inside(2 * s - 1), x1b.at[s, pair, part], x1h.at[1 - s, pair, part], sem_x1 + pair,
                  b + 2 * s - 1, v)

    hear(0, 1)
    tell(1, 2)

    def to_level1(source):
        for pair in range(pairs):
            parts = [view[pl.ds(0, y1, stride=2), :] + view[pl.ds(1, y1, stride=2), :]
                     for view in (source(2 * pair), source(2 * pair + 1))]
            yield pair, split_dot(jnp.concatenate(parts, axis=1), merge) * 0.125

    def to_level2(source):
        parts = [view[pl.ds(0, y2, stride=2), :] + view[pl.ds(1, y2, stride=2), :] for view in map(source, range(pairs))]
        return split_dot(jnp.concatenate(parts, axis=1), merge)

    for h in range(half):
        for pair, b1 in to_level1(lambda f: tmp.at[f, h]):
            b1s[pair, h] = b1
            x1p[pair, h + 2] = gd1[h] * b1
    for halo, sem in ((k1h, sem_k1), (kaph, sem_kap)):
        arrive_from(side, lambda n: halo.at[pl.ds(0, n), 0], sem)
        for s in range(2):
            begin(has[s], halo.at[s, core], halo.at[s, core], sem + 1, b, mate)
    arrive_from(side, lambda n: k1h.at[pl.ds(0, n), 0], sem_k1 + 1)
    for s in range(2):
        c = jnp.concatenate([k1h[s, 0], k1h[s, 1]], axis=0)
        turned = pltpu.roll(c, width1, 1)
        lane = lane_of(c)
        k1e[s, :y2] = jnp.where(lane < width1, c, turned)
        k1e[s, y2:] = jnp.where(lane < width1, turned, c)
        for pair in range(pairs):
            t3[s, pair] = k1e[s] * x1p[pair, edge1[s] + 2]
        f1s[s] = to_level2(lambda pair: t3.at[s, pair])
    for s in turns:
        begin(inside(2 * s - 1), f1s.at[s], f1h.at[1 - s], sem_f1, b + 2 * s - 1, v)
    hear(1, 2)
    tell(2, 3)

    def fix_f1():
        arrive_from(side, lambda n: kaph.at[pl.ds(0, n), 0], sem_kap + 1)
        for s in range(2):
            k = k1e[s]
            gd = damping / (shift_value + 6.0 * 0.25 * k)
            q1e[s] = gd * (0.25 * k)
            for f in range(fields):
                for r in range(2):
                    rows = slice(r * y1, (r + 1) * y1)
                    fix[f, rows] = kaph[s, r].astype(F32) * xp[f, edge[s], rows]
            for pair, flux in to_level1(lambda f: fix.at[f]):
                t3[s, pair] = k1s[edge1[s]] * gd * flux
            f1e[s] = to_level2(lambda pair: t3.at[s, pair])

    def rim_out(pair):
        for f in (2 * pair, 2 * pair + 1):
            for s in range(2):
                pack(f, edge[s])
        if early:
            for p in edge:
                share_out(p, 1, lambda peer: field_of(peer) // 2 == pair)
        elif pair == pairs - 1:
            share_out(0, share, lambda peer: None)

    for pair in range(pairs):
        arrive_from(side, lambda n: x0h.at[pl.ds(0, n), pl.ds(2 * pair, 2)], sem_x0 + pair)
        for s in range(2):
            p, h = edge[s], edge1[s]
            halved = []
            for f in (2 * pair, 2 * pair + 1):
                flux = kap[p] * x0h[s, f].astype(F32)
                tmp[f, h] = flux
                lo[f, p] = lo[f, p] + g0[p] * flux
                view = tmp.at[f, h]
                halved.append(view[pl.ds(0, y1, stride=2), :] + view[pl.ds(1, y1, stride=2), :])
            b1 = split_dot(jnp.concatenate(halved, axis=1), merge) * 0.125
            b1s[pair, h] = b1s[pair, h] + b1
            x1p[pair, h + 2] = x1p[pair, h + 2] + gd1[h] * b1
        if pair < pairs - 1:
            send_x1(pair, tuple(range(half)))
        if pair == 0:
            fix_f1()
            rim_out(pair)
            hear(2, 3)
            for off in offs:
                begin(inside(off), q2c, q2h.at[reach - off], sem_q2, b + off, v)

    send_x1(pairs - 1, tuple(range(half)))
    halved = []
    for pair in range(pairs):
        total = None
        for h in range(half):
            around = in_plane(x1p[pair, h + 2], width1)
            if h > 0:
                around = around + x1p[pair, h + 1]
            if h < half - 1:
                around = around + x1p[pair, h + 3]
            resid = keep * b1s[pair, h] + 0.25 * k1s[h] * around
            total = resid if total is None else total + resid
        t1[pair] = total
        view = t1.at[pair]
        halved.append(view[pl.ds(0, y2, stride=2), :] + view[pl.ds(1, y2, stride=2), :])
    b2 = split_dot(jnp.concatenate(halved, axis=1), merge) * 0.125

    arrive_from(side, lambda n: f1h.at[pl.ds(0, n)], sem_f1)
    for s in range(2):
        b2 = b2 + (0.125 * 0.25) * (f1h[s] + f1e[s])
    x20 = gd2 * b2
    x2s[...] = x20
    x2b[...] = x20.astype(BF16)
    quad = lane_of(x20[:tall2]) // width2
    for f in range(fields):
        slab = None
        for j in range(blocks):
            piece = x20[j * tall2:(j + 1) * tall2]
            if j != f:
                piece = pltpu.roll(piece, width2 * ((j - f) % blocks), 1)
            slab = piece if slab is None else jnp.where(quad == j, piece, slab)
        x2c[f] = slab.astype(BF16)

    peers = [(v + step) % group for step in range(group)]
    for off in reversed(offs):
        begin(inside(off), [(x2c.at[field_of(peer)], sl.at[reach - off, v], sem_s, b + off, peer) for peer in peers])
    for step in steps:
        peer = (v + step) % group
        begin(None, x2c.at[field_of(peer)], sl.at[reach, v], sem_c, b, peer)
    sl[reach, v] = x2c[field_of(v)]
    for off in reversed(offs):
        slot = reach - off
        if abs(off) <= NEAR:
            begin(inside(off), x2s, x2h.at[slot], sem_near, b + off, v)
        else:
            begin(inside(off), x2b, x2hb.at[slot], sem_far, b + off, v)

    rim_out(pairs - 1)
    for i in range(share):
        lr[v, i] = lb[place_of(v) * share + i]
    def coeff1(i):
        return q1e[0] if i == 1 else q1e[1] if i == half + 2 else q1s[i - 2]

    def raise_m(pair):
        arrive_from(side, lambda n: x1h.at[pl.ds(0, n), pair], sem_x1 + pair)
        for s in range(2):
            for order in range(half):
                x1p[pair, 1 - order if s == 0 else half + 2 + order] = x1h[s, pair, order].astype(F32)
        for i in range(1, half + 3):
            x = x1p[pair, i]
            around = in_plane(x, width1) + x1p[pair, i - 1] + x1p[pair, i + 1]
            x = (1.0 + keep) * x + coeff1(i) * around
            m1[pair, i] = x
            low, high = x[:y2], x[y2:]
            left = lane_of(low) < width1
            ms[2 * pair, i - 1] = jnp.where(left, low, pltpu.roll(high, width1, 1)).astype(BF16)
            ms[2 * pair + 1, i - 1] = jnp.where(left, pltpu.roll(low, width1, 1), high).astype(BF16)
        for step in steps:
            peer = (v + step) % group
            begin(field_of(peer) // 2 == pair, ms.at[field_of(peer)], mr.at[v], sem_m, b, peer)

    for pair in range(pairs - 1):
        raise_m(pair)
    raise_m(pairs - 1)
    mr[v] = ms[field_of(v)]

    coeff2 = {0: q2s[...]}
    arrive_from(offs, lambda n: q2h.at[pl.ds(0, n)], sem_q2)
    for off in offs:
        c = q2h[off + reach]
        if abs(off) < SWEEPS:
            parts = []
            for j in range(blocks):
                m = jnp.where(lane_of(c) // width2 == j, c, 0.0)
                shift = width2
                while shift < zs:
                    m = m + pltpu.roll(m, shift, 1)
                    shift *= 2
                parts.append(m)
            coeff2[off] = jnp.concatenate(parts, axis=0)

    spread = spread_table(2, zs)
    beside = beside_table(2, zs, zs)
    both0 = jnp.concatenate([spread, beside], axis=1)
    both1 = jnp.concatenate([spread, beside_table(2, zs, width1)], axis=1)

    def sweeps(start):
        level2 = start
        zero = jnp.zeros_like(start[0])
        for sweep in range(1, SWEEPS):
            wide = SWEEPS - sweep
            after = {}
            for off in range(-min(wide, reach), min(wide, reach) + 1):
                x = level2[off]
                around = in_plane(x, width2) + level2.get(off - 1, zero) + level2.get(off + 1, zero)
                after[off] = keep * x + start[off] + coeff2[off] * around
            level2 = after
        return level2

    def lift_up(level2, at, room, dot):
        wide = dot(level2[at], spread)
        plane, flat = [], []
        for pair in range(2):
            view = room.at[pair]
            piece = wide[:, pair * zs:(pair + 1) * zs]
            view[pl.ds(0, y2, stride=2), :] = piece
            view[pl.ds(1, y2, stride=2), :] = piece
            plane.append(view[...])
            flat.append(in_plane(view[...], width1))
        return plane, flat

    def sides(x):
        row = lax.broadcasted_iota(jnp.int32, x.shape, 0)
        low = jnp.where(row == 0, 0.0, pltpu.roll(x, 1, 0))
        high = jnp.where(row == y1 - 1, 0.0, pltpu.roll(x, y1 - 1, 0))
        return low, high

    def half_dot(x, table):
        return jnp.dot(x.astype(BF16), table, preferred_element_type=F32)

    arrive_from(offs, lambda n: sl.at[pl.ds(0, n)], sem_s)
    arrive(sl.at[reach, pl.ds(0, group - 1)], sem_c)
    quads = group // blocks
    starts = [{} for _ in range(quads)]
    for off in range(-reach, reach + 1):
        for q in range(quads):
            parts = [None] * blocks
            for u in range(blocks):
                c = sl[off + reach, q * blocks + u].astype(F32)
                for j in range(blocks):
                    piece = c if j == u else pltpu.roll(c, width2 * ((u - j) % blocks), 1)
                    parts[j] = piece if u == 0 else jnp.where(quad == u, piece, parts[j])
            starts[q][off] = jnp.concatenate(parts, axis=0)
    def padded_sweeps(start):
        level2 = start
        for off in range(1 - SWEEPS, SWEEPS):
            if abs(off) <= reach:
                pad2[off + SWEEPS, pl.ds(8, y2), :] = start[off]
        zero = jnp.zeros_like(x20)
        for sweep in range(1, SWEEPS):
            wide = min(SWEEPS - sweep, reach)
            after = {}
            for off in range(-wide, wide + 1):
                x = level2[off]
                view = pad2.at[off + SWEEPS]
                around = (rolled_sides(x, 1, width2) + view[pl.ds(7, y2), :] + view[pl.ds(9, y2), :]
                          + level2.get(off - 1, zero) + level2.get(off + 1, zero))
                after[off] = keep * x + start[off] + coeff2[off] * around
            if sweep < SWEEPS - 1:
                for off in range(1 - wide, wide):
                    pad2[off + SWEEPS, pl.ds(8, y2), :] = after[off]
            level2 = after
        return level2

    ends = [padded_sweeps(start) for start in starts]
    arrive(mr.at[pl.ds(0, group - 1)], sem_m)
    for q in range(quads):
        stack = jnp.concatenate([ends[q][off] for off in (-1, 0, 1)], axis=0).astype(BF16)
        wide = jnp.dot(stack, both1, preferred_element_type=F32)
        raised = []
        for at in range(3):
            for pair in range(2):
                piece = wide[at * y2:(at + 1) * y2, pair * zs:(pair + 1) * zs]
                flank = wide[at * y2:(at + 1) * y2, (2 + pair) * zs:(3 + pair) * zs]
                view = t4.at[at, pair]
                for r in range(2):
                    view[pl.ds(8 + r, y2, stride=2), :] = piece
                    t5.at[at, pair][pl.ds(r, y2, stride=2), :] = flank
                raised.append((view[pl.ds(8, y1), :],
                               t5[at, pair] + view[pl.ds(7, y1), :] + view[pl.ds(9, y1), :]))
        for pair in range(2):
            first = q * blocks + 2 * pair
            rising = []
            for i in range(1, half + 3):
                even, odd = mr[first, i - 1].astype(F32), mr[first + 1, i - 1].astype(F32)
                left = lane_of(even) < width1
                mixed = jnp.concatenate([jnp.where(left, even, pltpu.roll(odd, width1, 1)),
                                         jnp.where(left, pltpu.roll(even, width1, 1), odd)], axis=0)
                at = i // half
                around = (raised[2 * at + pair][1] + raised[2 * ((i - 1) // half) + pair][0]
                          + raised[2 * ((i + 1) // half) + pair][0])
                rising.append((mixed + keep * raised[2 * at + pair][0] + coeff1(i) * around).astype(BF16))
            wide = jnp.dot(jnp.concatenate(rising, axis=0), both0, preferred_element_type=F32)
            for i in range(half + 2):
                piece = wide[i * y1:(i + 1) * y1]
                for inner in range(2):
                    v1[first + inner, i, pl.ds(8, y1), :] = piece[:, inner * zs:(inner + 1) * zs]
                    if 1 <= i <= half:
                        vz[first + inner, i - 1] = piece[:, (2 + inner) * zs:(3 + inner) * zs]
    arrive(lr.at[pl.ds(0, group - 1)], sem_l)
    keys = [(i, j) for i in range(group) for j in range(i, group)]
    totals = [None] * len(keys)
    tall = y1 // 2
    for i in range(share):
        p = i % planes if whole_fields else (place_of(v) * share + i) % planes
        h, e = p // 2, p % 2
        for cut in range(2):
            rows = pl.ds(8 + cut * tall, tall)
            halves = []
            for u in range(group):
                x = v1[u, h + 1, rows, :]
                halves.append((keep * x, vz[u, h, pl.ds(cut * tall, tall), :] + 2.0 * x + v1[u, h + 2 * e, rows, :]))
            for r in range(2):
                k = gk.at[p][pl.ds(2 * cut * tall + r, tall, stride=2), :]
                z = []
                for u in range(group):
                    kept, around = halves[u]
                    z.append(lr[u, i, r, pl.ds(cut * tall, tall), :].astype(F32) + kept
                             + k * (around + v1[u, h + 1, pl.ds(7 + 2 * r + cut * tall, tall), :]))
                for n, (one, other) in enumerate(keys):
                    product = (z[one] * z[other]).reshape(tall // 8, 8, zs).sum(axis=0)
                    totals[n] = product if totals[n] is None else totals[n] + product
    lines = [None] * group
    lane = lax.broadcasted_iota(jnp.int32, (1, zs), 1)
    for (i, j), total in zip(keys, totals):
        value = jnp.sum(jnp.sum(total, axis=0, keepdims=True), axis=1, keepdims=True)
        for one, other in {(i, j), (j, i)}:
            placed = jnp.where(lane == other, value, 0.0)
            lines[one] = placed if lines[one] is None else lines[one] + placed
    for i in range(group):
        part[i] = lines[i]
    mine = part[v]
    def own():
        start = {0: x20}
        arrive_from(near, lambda n: x2h.at[pl.ds(0, n)], sem_near)
        if far:
            arrive_from(far, lambda n: x2hb.at[pl.ds(0, n)], sem_far)
        for off in offs:
            start[off] = x2h[off + reach] if abs(off) <= NEAR else x2hb[off + reach].astype(F32)
        level2 = sweeps(start)
        raised = [lift_up(level2, off, t2.at[off + 1], split_dot) for off in (-1, 0, 1)]
        for i in range(1, half + 3):
            for pair in range(pairs):
                at = i // half
                around = raised[at][1][pair] + raised[(i - 1) // half][0][pair] + raised[(i + 1) // half][0][pair]
                x = m1[pair, i] + keep * raised[at][0][pair] + coeff1(i) * around
                wide = split_dot(x, spread)
                w1[2 * pair, i - 1] = wide[:, :zs]
                w1[2 * pair + 1, i - 1] = wide[:, zs:]
                if 2 <= i < half + 2:
                    wide = split_dot(x, beside)
                    wz[2 * pair, i - 2] = wide[:, :zs]
                    wz[2 * pair + 1, i - 2] = wide[:, zs:]
        for f in range(fields):
            for h in range(half):
                x = w1[f, h + 1]
                base = wz[f, h] + 2.0 * x
                kept = keep * x
                rims = sides(x)
                for e in range(2):
                    p = 2 * h + e
                    around = base + w1[f, h + 2 * e]
                    for r in range(2):
                        rows = pl.ds(r, y1, stride=2)
                        out.at[0, f, p][rows, :] = (
                            lo.at[f, p][rows, :] + kept + gk.at[p][rows, :] * (around + rims[r]))


    if bricks * group <= ONE_ROUND:
        for index in range(1, bricks * group):
            brick, vec = (b + index // group) % bricks, (v + index % group) % group
            begin(None, part.at[vec], g2h.at[index], sem_g2, brick, vec)
        own()
        arrive(g2h.at[pl.ds(1, bricks * group - 1)], sem_g2)
        rows = [mine] + [g2h[index] for index in range(1, bricks * group)]
        while len(rows) > 1:
            rows = [a + b for a, b in zip(rows[::2], rows[1::2])] + rows[len(rows) & ~1:]
        mine = rows[0]
    else:
        for step in range(1, group):
            peer = (v + step) % group
            begin(None, part.at[peer], g1h.at[step], sem_g1, b, peer)
        own()
        arrive(g1h.at[pl.ds(1, group - 1)], sem_g1)
        for step in range(1, group):
            mine = mine + g1h[step]
        rows_s[...] = mine
        for step in range(1, bricks):
            begin(None, rows_s, g2h.at[step], sem_g2, (b + step) % bricks, v)
        arrive(g2h.at[pl.ds(1, bricks - 1)], sem_g2)
        for step in range(1, bricks):
            mine = mine + g2h[step]
    gram[...] = mine[:, :group]
    for finish in sends:
        finish()


def local(bricks, group, right_side, diffusivity):
    fields, planes, ys, zs = right_side.shape[1:]
    assert right_side.shape[0] == 1 and planes == 4 and ys == zs == 128 and fields == 4 and group % 4 == 0 and SWEEPS == 6
    pairs, half = fields // 2, planes // 2
    y1, y2 = ys // 2, ys // 4
    reach = min(SWEEPS, bricks - 1)
    units = fields * planes
    share = units // group
    slots = 2 * reach + 1
    ends = bricks * group if bricks * group <= ONE_ROUND else bricks
    count = 2 * pairs + 14
    vm = pltpu.VMEM
    result, rows = pl.pallas_call(
        functools.partial(kernel, bricks, group, reach),
        out_shape=(
            jax.ShapeDtypeStruct(right_side.shape, F32),
            jax.ShapeDtypeStruct((1, group), F32),
        ),
        in_specs=[pl.BlockSpec(memory_space=pl.ANY)] * 2,
        out_specs=(pl.BlockSpec(memory_space=pltpu.VMEM),) * 2,
        scratch_shapes=[
            vm((fields, planes, ys, zs), F32),
            vm((planes, ys, zs), F32),
            vm((fields, planes, ys, zs), F32),
            vm((planes, ys, zs), F32),
            vm((planes, ys, zs), F32),
            vm((fields, planes, ys, zs), F32),
            vm((units, 2, y1, zs), BF16),
            vm((group, share, 2, y1, zs), BF16),
            vm((2, fields, ys, zs), BF16),
            vm((2, fields, ys, zs), BF16),
            vm((fields, half, ys, zs), F32),
            vm((half, ys, zs), F32),
            vm((half, y1, zs), F32),
            vm((half, y1, zs), F32),
            vm((2, 2, y1, zs), BF16),
            vm((2, 2, y1, zs), BF16),
            vm((fields, ys, zs), F32),
            vm((2, y2, zs), F32),
            vm((2, 2, y2 // 2, zs), F32),
            vm((2, 2, y2 // 2, zs), F32),
            vm((2, y1, zs), F32),
            vm((2, y1, zs), F32),
            vm((pairs, half, y1, zs), F32),
            vm((pairs, half + 4, y1, zs), F32),
            vm((2, pairs, half, y1, zs), BF16),
            vm((2, pairs, half, y1, zs), BF16),
            vm((pairs, half + 4, y1, zs), F32),
            vm((pairs, y1, zs), F32),
            vm((2, pairs, y1, zs), F32),
            vm((2, y2, zs), F32),
            vm((2, y2, zs), F32),
            vm((y2, zs), F32),
            vm((8, zs), F32),
            vm((slots, 8, zs), F32),
            vm((y2, zs), F32),
            vm((y2, zs), BF16),
            vm((slots, y2, zs), F32),
            vm((slots, y2, zs), BF16),
            vm((fields, 8, zs), BF16),
            vm((slots, group, 8, zs), BF16),
            vm((3, pairs, y1, zs), F32),
            vm((3, 2, y1 + 16, zs), F32),
            vm((3, 2, y1, zs), F32),
            vm((2 * SWEEPS + 1, y2 + 16, zs), F32),
            vm((fields, half + 2, y2, zs), BF16),
            vm((group, half + 2, y2, zs), BF16),
            vm((fields, half + 2, y1, zs), F32),
            vm((fields, half, y1, zs), F32),
            vm((group, half + 2, y1 + 16, zs), F32),
            vm((group, half, y1, zs), F32),
            vm((group, 1, zs), F32),
            vm((group, 1, zs), F32),
            vm((1, zs), F32),
            vm((ends, 1, zs), F32),
            pltpu.SemaphoreType.REGULAR((2, 3)),
            pltpu.SemaphoreType.DMA((3,)),
            pltpu.SemaphoreType.DMA((count,)),
            pltpu.SemaphoreType.DMA((1,)),
        ],
        compiler_params=pltpu.CompilerParams(
            collective_id=0, has_side_effects=True, vmem_limit_bytes=48 << 20
        ),
    )(pltpu.with_memory_space_constraint(right_side, pltpu.HBM), pltpu.with_memory_space_constraint(diffusivity, pltpu.HBM))
    return pl.pallas_call(
        write,
        out_shape=(
            jax.ShapeDtypeStruct(right_side.shape, F32),
            jax.ShapeDtypeStruct((1, group), F32),
        ),
        in_specs=[pl.BlockSpec(memory_space=pltpu.VMEM)] * 2,
        out_specs=(pl.BlockSpec(memory_space=pl.ANY),) * 2,
        scratch_shapes=[pltpu.SemaphoreType.DMA((2,))],
    )(pltpu.with_memory_space_constraint(result, pltpu.VMEM), pltpu.with_memory_space_constraint(rows, pltpu.VMEM))


def solution(mesh):
    return jax.shard_map(
        functools.partial(local, mesh.shape["brick"], mesh.shape["vec"]),
        mesh=mesh,
        in_specs=(P("vec", None, "brick", None, None), P("brick", None, None)),
        out_specs=(P("vec", None, "brick", None, None), P("vec", None)),
        check_vma=False,
    )
```

```python
import functools

import jax
import jax.numpy as jnp
from jax import lax
from jax.experimental import pallas as pl
from jax.experimental.pallas import tpu as pltpu
from jax.sharding import PartitionSpec as P

SWEEPS = 6
NEAR = 2
ONE_ROUND = 64
shift_value = 0.1
damping = 0.8
keep = 1.0 - damping
F32 = jnp.float32
BF16 = jnp.bfloat16
MESH = pl.DeviceIdType.MESH


def rolled_sides(x, axis, width):
    size = x.shape[axis]
    place = lax.broadcasted_iota(jnp.int32, x.shape, axis) % width
    low = jnp.where(place == 0, 0.0, pltpu.roll(x, 1, axis))
    high = jnp.where(place == width - 1, 0.0, pltpu.roll(x, size - 1, axis))
    return low + high


def in_plane(x, width):
    return rolled_sides(x, 0, x.shape[0]) + rolled_sides(x, 1, width)


def split_dot(x, table):
    head = x.astype(BF16)
    tail = (x - head.astype(F32)).astype(BF16)
    return jnp.dot(head, table, preferred_element_type=F32) + jnp.dot(
        tail, table, preferred_element_type=F32
    )


def iotas(rows, cols):
    return (lax.broadcasted_iota(jnp.int32, (rows, cols), 0),
            lax.broadcasted_iota(jnp.int32, (rows, cols), 1))


def merge_table(parts, lanes):
    row, col = iotas(parts * lanes, lanes)
    return jnp.where(row // 2 == col, 1.0, 0.0).astype(BF16)


def spread_table(parts, lanes):
    row, col = iotas(lanes, parts * lanes)
    return jnp.where(col // 2 == row, 1.0, 0.0).astype(BF16)


def beside_table(parts, lanes, width):
    row, col = iotas(lanes, parts * lanes)
    place = col % width
    low = ((col - 1) // 2 == row) & (place > 0)
    high = ((col + 1) // 2 == row) & (place < width - 1)
    return jnp.where(low | high, 1.0, 0.0).astype(BF16)


def repeat_table(lanes, source, width):
    row, col = iotas(lanes, lanes)
    hit = (row // 2 == col % width) & (row < source)
    return jnp.where(hit, 1.0, 0.0).astype(BF16)


def lane_of(x):
    return lax.broadcasted_iota(jnp.int32, x.shape, x.ndim - 1)


def write(result, rows, out, gram, sems):
    copies = [pltpu.make_async_copy(result, out, sems.at[0]), pltpu.make_async_copy(rows, gram, sems.at[1])]
    for made in copies:
        made.start()
    for made in copies:
        made.wait()


def kernel(bricks, group, reach, rhs_in, kap_in, out, gram, rhs, kap, xp, g0, gk, lo, lb, lr, x0s, x0h, tmp,
           ktmp, k1s, q1s, kaps, kaph, fix, f1e, k1c, k1h, k1e, q1e, b1s, x1p, x1b, x1h, m1, t1, t3, f1s, f1h, q2s, q2c, q2h, x2s, x2b,
           x2h, x2hb, x2c, sl, t2, t4, t5, pad2, ms, mr, w1, wz, v1, vz, part, g1h, rows_s, g2h, waves, sems_l, sems_r, sems_s):
    fields, planes, ys, zs = rhs.shape
    pairs = fields // 2
    y1, y2 = ys // 2, ys // 4
    width1, width2 = zs // 2, zs // 4
    half = planes // 2
    units = fields * planes
    share = units // group
    whole_fields = share % planes == 0
    b = lax.axis_index("brick")
    v = lax.axis_index("vec")
    has = (b > 0, b < bricks - 1)
    turns = (b % 2, 1 - b % 2)
    side = (-1, 1)
    edge = (0, planes - 1)
    edge1 = (0, half - 1)
    offs = [sign * size for size in range(1, reach + 1) for sign in (-1, 1)]
    counter = [0]
    sends = []

    def copy(src, dst, sem, brick, vec):
        return pltpu.make_async_remote_copy(
            src_ref=src, dst_ref=dst, send_sem=sems_s.at[0], recv_sem=sems_r.at[sem],
            device_id=(brick, vec), device_id_type=MESH)

    def begin(cond, *asked):
        asked = [asked] if len(asked) == 5 else asked[0]

        def start():
            for one in asked:
                copy(*one).start()

        def finish():
            for one in asked:
                copy(*one).wait_send()

        if cond is None:
            start()
            sends.append(finish)
        else:
            pl.when(cond)(start)
            sends.append(lambda: pl.when(cond)(finish))

    def arrive(dst, sem):
        copy(dst, dst, sem, b, v).wait_recv()

    def number(count):
        base = counter[0]
        counter[0] += count
        return base

    def inside(off):
        return (b + off >= 0) & (b + off < bricks)

    def arrive_from(hops, view, sem):
        count = sum(inside(hop).astype(jnp.int32) for hop in hops)
        for n in sorted({sum(0 <= brick + hop < bricks for hop in hops) for brick in range(bricks)} - {0}):
            pl.when(count == n)(copy(view(n), view(n), sem, b, v).wait_recv)

    sem_x0, sem_x1 = number(pairs), number(pairs)
    sem_kap, sem_k1 = number(2), number(2)
    sem_f1, sem_near, sem_far, sem_q2, sem_s, sem_c, sem_l, sem_m, sem_g1, sem_g2 = (
        number(1) for _ in range(10))
    near = [off for off in offs if abs(off) <= NEAR]
    far = [off for off in offs if abs(off) > NEAR]

    load_kap = pltpu.make_async_copy(kap_in, kap, sems_l.at[0])
    load_kap.start()
    for p in edge:
        pltpu.make_async_copy(rhs_in.at[0, :, p], rhs.at[:, p], sems_l.at[1]).start()
    load_mid = pltpu.make_async_copy(rhs_in.at[0, :, pl.ds(1, planes - 2)], rhs.at[:, pl.ds(1, planes - 2)],
                                     sems_l.at[2])
    load_mid.start()

    barrier = pltpu.get_barrier_semaphore()
    for s in range(2):
        @pl.when(has[s])
        def _(s=s):
            pl.semaphore_signal(barrier, inc=1, device_id=(b + side[s], v), device_id_type=MESH)
    for step in range(1, group):
        pl.semaphore_signal(barrier, inc=1, device_id=(b, (v + step) % group),
                            device_id_type=MESH)
    for pad in (t4, v1):
        for rows in (pl.ds(0, 8), pl.ds(y1 + 8, 8)):
            pad[:, :, rows, :] = jnp.zeros_like(pad.at[:, :, rows, :])
    for rows in (pl.ds(0, 8), pl.ds(y2 + 8, 8)):
        pad2[:, rows, :] = jnp.zeros_like(pad2.at[:, rows, :])
    for s in range(2):
        @pl.when(jnp.logical_not(has[s]))
        def _(s=s):
            x0h[s] = jnp.zeros_like(x0h.at[s])
            x1h[s] = jnp.zeros_like(x1h.at[s])
            k1h[s] = jnp.zeros_like(k1h.at[s])
            kaph[s] = jnp.zeros_like(kaph.at[s])
            f1h[s] = jnp.zeros_like(f1h.at[s])
    for off in offs:
        @pl.when(jnp.logical_not(inside(off)))
        def _(off=off):
            q2h[off + reach] = jnp.zeros_like(q2h.at[off + reach])
            sl[off + reach] = jnp.zeros_like(sl.at[off + reach])
            if abs(off) <= NEAR:
                x2h[off + reach] = jnp.zeros_like(x2h.at[off + reach])
            else:
                x2hb[off + reach] = jnp.zeros_like(x2hb.at[off + reach])

    load_kap.wait()
    for p in range(planes):
        g = damping / (shift_value + 6.0 * kap[p])
        g0[p] = g
        gk[p] = g * kap[p]
    for s in range(2):
        for r in range(2):
            kaps[s, r] = kap[edge[s], r * y1:(r + 1) * y1].astype(BF16)
    pl.semaphore_wait(barrier, (b > 0).astype(jnp.int32) + (b < bricks - 1).astype(jnp.int32) + group - 1)
    core = v % 2
    mate = v + 1 - 2 * core
    for s in turns:
        begin(inside(2 * s - 1), kaps.at[s, core], kaph.at[1 - s, core], sem_kap, b + 2 * s - 1, v)
    pltpu.make_async_copy(rhs.at[:, pl.ds(0, 2)], rhs.at[:, pl.ds(0, 2)], sems_l.at[1]).wait()
    for f in range(fields):
        for s in range(2):
            x = g0[edge[s]] * rhs[f, edge[s]]
            xp[f, edge[s]] = x
            x0s[s, f] = x.astype(BF16)

    def tell(stage, far):
        for s in range(2):
            @pl.when(inside(side[s] * far))
            def _(s=s):
                pl.semaphore_signal(waves.at[1 - s, stage], inc=1, device_id=(b + side[s] * far, v), device_id_type=MESH)

    def hear(stage, far):
        for s in range(2):
            @pl.when(inside(side[s] * far))
            def _(s=s):
                pl.semaphore_wait(waves.at[s, stage], 1)

    tell(0, 1)

    merge = merge_table(2, zs)
    for h in range(half):
        ktmp[h] = kap[2 * h] + kap[2 * h + 1]
    k1 = []
    for h in range(half):
        summed = ktmp.at[h][pl.ds(0, y1, stride=2), :] + ktmp.at[h][pl.ds(1, y1, stride=2), :]
        k = split_dot(summed, repeat_table(zs, zs, width1)) * 0.125
        k1s[h] = k
        k1.append(k)
    for s in range(2):
        k = k1[edge1[s]]
        low, high = k[:y2], k[y2:]
        packed = jnp.where(lane_of(low) < width1, low, high)
        for r in range(2):
            k1c[s, r] = packed[r * y2 // 2:(r + 1) * y2 // 2]
    for s in turns:
        begin(inside(2 * s - 1), k1c.at[s, core], k1h.at[1 - s, core], sem_k1, b + 2 * s - 1, v)
    for pair in range(pairs):
        for s in turns:
            both = pl.ds(2 * pair, 2)
            begin(inside(2 * s - 1), x0s.at[s, both], x0h.at[1 - s, both], sem_x0 + pair, b + 2 * s - 1, v)

    gd1 = [damping / (shift_value + 6.0 * 0.25 * k) for k in k1]
    for h in range(half):
        q1s[h] = gd1[h] * (0.25 * k1[h])
    t1[0] = k1[0] + k1[1]
    summed = t1.at[0][pl.ds(0, y2, stride=2), :] + t1.at[0][pl.ds(1, y2, stride=2), :]
    k2 = split_dot(summed, repeat_table(zs, width1, width2)) * 0.125
    gd2 = damping / (shift_value + 6.0 * 0.0625 * k2)
    q2 = gd2 * (0.0625 * k2)
    q2s[...] = q2
    blocks = zs // width2
    tall2 = y2 // blocks
    packed = q2[:tall2]
    place = lane_of(packed) // width2
    for j in range(1, blocks):
        packed = jnp.where(place == j, q2[j * tall2:(j + 1) * tall2], packed)
    q2c[...] = packed

    load_mid.wait()
    for f in range(fields):
        for p in range(1, planes - 1):
            xp[f, p] = g0[p] * rhs[f, p]
    for f in range(fields):
        for h in range(half):
            total = None
            for p in (2 * h, 2 * h + 1):
                x = xp[f, p]
                around = in_plane(x, zs)
                if p > 0:
                    around = around + xp[f, p - 1]
                if p < planes - 1:
                    around = around + xp[f, p + 1]
                resid = keep * rhs[f, p] + kap[p] * around
                lo[f, p] = x + g0[p] * resid
                total = resid if total is None else total + resid
            tmp[f, h] = total

    def pack(f, p):
        view = lo.at[f, p]
        for e in range(2):
            lb[f * planes + p, e] = view[pl.ds(e, y1, stride=2), :].astype(BF16)

    def place_of(vec):
        return vec % 2 * (group // 2) + vec // 2

    steps = sorted(range(1, group), key=lambda step: -min(step, group - step))

    def field_of(vec):
        return place_of(vec) * share // planes

    def share_out(first, count, chosen):
        for step in steps:
            peer = (v + step) % group
            begin(chosen(peer), lb.at[pl.ds(place_of(peer) * share + first, count)], lr.at[v, pl.ds(first, count)],
                  sem_l, b, peer)

    early = share == planes
    for f in range(fields):
        for p in range(1, planes - 1):
            pack(f, p)
    if early:
        share_out(1, planes - 2, lambda peer: None)

    def send_x1(pair, orders):
        for s in range(2):
            for order in orders:
                plane = order if s == 0 else half - 1 - order
                x1b[s, pair, order] = x1p[pair, plane + 2].astype(BF16)
        for s in turns:
            part = pl.ds(orders[0], len(orders))
            begin(inside(2 * s - 1), x1b.at[s, pair, part], x1h.at[1 - s, pair, part], sem_x1 + pair,
                  b + 2 * s - 1, v)

    hear(0, 1)
    tell(1, 2)

    def to_level1(source):
        for pair in range(pairs):
            parts = [view[pl.ds(0, y1, stride=2), :] + view[pl.ds(1, y1, stride=2), :]
                     for view in (source(2 * pair), source(2 * pair + 1))]
            yield pair, split_dot(jnp.concatenate(parts, axis=1), merge) * 0.125

    def to_level2(source):
        parts = [view[pl.ds(0, y2, stride=2), :] + view[pl.ds(1, y2, stride=2), :] for view in map(source, range(pairs))]
        return split_dot(jnp.concatenate(parts, axis=1), merge)

    for h in range(half):
        for pair, b1 in to_level1(lambda f: tmp.at[f, h]):
            b1s[pair, h] = b1
            x1p[pair, h + 2] = gd1[h] * b1
    for halo, sem in ((k1h, sem_k1), (kaph, sem_kap)):
        arrive_from(side, lambda n: halo.at[pl.ds(0, n), 0], sem)
        for s in range(2):
            begin(has[s], halo.at[s, core], halo.at[s, core], sem + 1, b, mate)
    arrive_from(side, lambda n: k1h.at[pl.ds(0, n), 0], sem_k1 + 1)
    for s in range(2):
        c = jnp.concatenate([k1h[s, 0], k1h[s, 1]], axis=0)
        turned = pltpu.roll(c, width1, 1)
        lane = lane_of(c)
        k1e[s, :y2] = jnp.where(lane < width1, c, turned)
        k1e[s, y2:] = jnp.where(lane < width1, turned, c)
        for pair in range(pairs):
            t3[s, pair] = k1e[s] * x1p[pair, edge1[s] + 2]
        f1s[s] = to_level2(lambda pair: t3.at[s, pair])
    for s in turns:
        begin(inside(2 * s - 1), f1s.at[s], f1h.at[1 - s], sem_f1, b + 2 * s - 1, v)
    hear(1, 2)
    tell(2, 3)

    def fix_f1():
        arrive_from(side, lambda n: kaph.at[pl.ds(0, n), 0], sem_kap + 1)
        for s in range(2):
            k = k1e[s]
            gd = damping / (shift_value + 6.0 * 0.25 * k)
            q1e[s] = gd * (0.25 * k)
            for f in range(fields):
                for r in range(2):
                    rows = slice(r * y1, (r + 1) * y1)
                    fix[f, rows] = kaph[s, r].astype(F32) * xp[f, edge[s], rows]
            for pair, flux in to_level1(lambda f: fix.at[f]):
                t3[s, pair] = k1s[edge1[s]] * gd * flux
            f1e[s] = to_level2(lambda pair: t3.at[s, pair])

    def resid1(pair):
        total = None
        for h in range(half):
            around = in_plane(x1p[pair, h + 2], width1)
            if h > 0:
                around = around + x1p[pair, h + 1]
            if h < half - 1:
                around = around + x1p[pair, h + 3]
            resid = keep * b1s[pair, h] + 0.25 * k1s[h] * around
            total = resid if total is None else total + resid
        t1[pair] = total

    def rim_out(pair):
        for f in (2 * pair, 2 * pair + 1):
            for s in range(2):
                pack(f, edge[s])
        if early:
            for p in edge:
                share_out(p, 1, lambda peer: field_of(peer) // 2 == pair)
        elif pair == pairs - 1:
            share_out(0, share, lambda peer: None)

    for pair in range(pairs):
        arrive_from(side, lambda n: x0h.at[pl.ds(0, n), pl.ds(2 * pair, 2)], sem_x0 + pair)
        for s in range(2):
            p, h = edge[s], edge1[s]
            halved = []
            for f in (2 * pair, 2 * pair + 1):
                flux = kap[p] * x0h[s, f].astype(F32)
                tmp[f, h] = flux
                lo[f, p] = lo[f, p] + g0[p] * flux
                view = tmp.at[f, h]
                halved.append(view[pl.ds(0, y1, stride=2), :] + view[pl.ds(1, y1, stride=2), :])
            b1 = split_dot(jnp.concatenate(halved, axis=1), merge) * 0.125
            b1s[pair, h] = b1s[pair, h] + b1
            x1p[pair, h + 2] = x1p[pair, h + 2] + gd1[h] * b1
        if pair < pairs - 1:
            send_x1(pair, tuple(range(half)))
        if pair == 0:
            fix_f1()
            rim_out(pair)
            hear(2, 3)
            for off in offs:
                begin(inside(off), q2c, q2h.at[reach - off], sem_q2, b + off, v)
        if pair < pairs - 1:
            resid1(pair)

    send_x1(pairs - 1, tuple(range(half)))
    resid1(pairs - 1)
    halved = [t1.at[pair][pl.ds(0, y2, stride=2), :] + t1.at[pair][pl.ds(1, y2, stride=2), :] for pair in range(pairs)]
    b2 = split_dot(jnp.concatenate(halved, axis=1), merge) * 0.125

    arrive_from(side, lambda n: f1h.at[pl.ds(0, n)], sem_f1)
    for s in range(2):
        b2 = b2 + (0.125 * 0.25) * (f1h[s] + f1e[s])
    x20 = gd2 * b2
    x2s[...] = x20
    x2b[...] = x20.astype(BF16)
    quad = lane_of(x20[:tall2]) // width2
    for f in range(fields):
        slab = None
        for j in range(blocks):
            piece = x20[j * tall2:(j + 1) * tall2]
            if j != f:
                piece = pltpu.roll(piece, width2 * ((j - f) % blocks), 1)
            slab = piece if slab is None else jnp.where(quad == j, piece, slab)
        x2c[f] = slab.astype(BF16)

    peers = [(v + step) % group for step in range(group)]
    for off in reversed(offs):
        begin(inside(off), [(x2c.at[field_of(peer)], sl.at[reach - off, v], sem_s, b + off, peer) for peer in peers])
    for step in steps:
        peer = (v + step) % group
        begin(None, x2c.at[field_of(peer)], sl.at[reach, v], sem_c, b, peer)
    sl[reach, v] = x2c[field_of(v)]
    for off in reversed(offs):
        slot = reach - off
        if abs(off) <= NEAR:
            begin(inside(off), x2s, x2h.at[slot], sem_near, b + off, v)
        else:
            begin(inside(off), x2b, x2hb.at[slot], sem_far, b + off, v)

    rim_out(pairs - 1)
    for i in range(share):
        lr[v, i] = lb[place_of(v) * share + i]
    def coeff1(i):
        return q1e[0] if i == 1 else q1e[1] if i == half + 2 else q1s[i - 2]

    def raise_m(pair):
        arrive_from(side, lambda n: x1h.at[pl.ds(0, n), pair], sem_x1 + pair)
        for s in range(2):
            for order in range(half):
                x1p[pair, 1 - order if s == 0 else half + 2 + order] = x1h[s, pair, order].astype(F32)
        for i in range(1, half + 3):
            x = x1p[pair, i]
            around = in_plane(x, width1) + x1p[pair, i - 1] + x1p[pair, i + 1]
            x = (1.0 + keep) * x + coeff1(i) * around
            m1[pair, i] = x
            low, high = x[:y2], x[y2:]
            left = lane_of(low) < width1
            ms[2 * pair, i - 1] = jnp.where(left, low, pltpu.roll(high, width1, 1)).astype(BF16)
            ms[2 * pair + 1, i - 1] = jnp.where(left, pltpu.roll(low, width1, 1), high).astype(BF16)
        for step in steps:
            peer = (v + step) % group
            begin(field_of(peer) // 2 == pair, ms.at[field_of(peer)], mr.at[v], sem_m, b, peer)

    for pair in range(pairs - 1):
        raise_m(pair)
    raise_m(pairs - 1)
    mr[v] = ms[field_of(v)]

    coeff2 = {0: q2s[...]}
    arrive_from(offs, lambda n: q2h.at[pl.ds(0, n)], sem_q2)
    for off in offs:
        c = q2h[off + reach]
        if abs(off) < SWEEPS:
            parts = []
            for j in range(blocks):
                m = jnp.where(lane_of(c) // width2 == j, c, 0.0)
                shift = width2
                while shift < zs:
                    m = m + pltpu.roll(m, shift, 1)
                    shift *= 2
                parts.append(m)
            coeff2[off] = jnp.concatenate(parts, axis=0)

    spread = spread_table(2, zs)
    beside = beside_table(2, zs, zs)
    both0 = jnp.concatenate([spread, beside], axis=1)
    both1 = jnp.concatenate([spread, beside_table(2, zs, width1)], axis=1)

    def sweeps(start):
        level2 = start
        zero = jnp.zeros_like(start[0])
        for sweep in range(1, SWEEPS):
            wide = SWEEPS - sweep
            after = {}
            for off in range(-min(wide, reach), min(wide, reach) + 1):
                x = level2[off]
                around = in_plane(x, width2) + level2.get(off - 1, zero) + level2.get(off + 1, zero)
                after[off] = keep * x + start[off] + coeff2[off] * around
            level2 = after
        return level2

    def lift_up(level2, at, room, dot):
        wide = dot(level2[at], spread)
        plane, flat = [], []
        for pair in range(2):
            view = room.at[pair]
            piece = wide[:, pair * zs:(pair + 1) * zs]
            view[pl.ds(0, y2, stride=2), :] = piece
            view[pl.ds(1, y2, stride=2), :] = piece
            plane.append(view[...])
            flat.append(in_plane(view[...], width1))
        return plane, flat

    def sides(x):
        row = lax.broadcasted_iota(jnp.int32, x.shape, 0)
        low = jnp.where(row == 0, 0.0, pltpu.roll(x, 1, 0))
        high = jnp.where(row == y1 - 1, 0.0, pltpu.roll(x, y1 - 1, 0))
        return low, high

    def half_dot(x, table):
        return jnp.dot(x.astype(BF16), table, preferred_element_type=F32)

    arrive_from(offs, lambda n: sl.at[pl.ds(0, n)], sem_s)
    arrive(sl.at[reach, pl.ds(0, group - 1)], sem_c)
    quads = group // blocks
    starts = [{} for _ in range(quads)]
    for off in range(-reach, reach + 1):
        for q in range(quads):
            parts = [None] * blocks
            for u in range(blocks):
                c = sl[off + reach, q * blocks + u].astype(F32)
                for j in range(blocks):
                    piece = c if j == u else pltpu.roll(c, width2 * ((u - j) % blocks), 1)
                    parts[j] = piece if u == 0 else jnp.where(quad == u, piece, parts[j])
            starts[q][off] = jnp.concatenate(parts, axis=0)
    def padded_sweeps(start):
        level2 = start
        for off in range(1 - SWEEPS, SWEEPS):
            if abs(off) <= reach:
                pad2[off + SWEEPS, pl.ds(8, y2), :] = start[off]
        zero = jnp.zeros_like(x20)
        for sweep in range(1, SWEEPS):
            wide = min(SWEEPS - sweep, reach)
            after = {}
            for off in range(-wide, wide + 1):
                x = level2[off]
                view = pad2.at[off + SWEEPS]
                around = (rolled_sides(x, 1, width2) + view[pl.ds(7, y2), :] + view[pl.ds(9, y2), :]
                          + level2.get(off - 1, zero) + level2.get(off + 1, zero))
                after[off] = keep * x + start[off] + coeff2[off] * around
            if sweep < SWEEPS - 1:
                for off in range(1 - wide, wide):
                    pad2[off + SWEEPS, pl.ds(8, y2), :] = after[off]
            level2 = after
        return level2

    ends = [padded_sweeps(start) for start in starts]
    arrive(mr.at[pl.ds(0, group - 1)], sem_m)
    for q in range(quads):
        stack = jnp.concatenate([ends[q][off] for off in (-1, 0, 1)], axis=0).astype(BF16)
        wide = jnp.dot(stack, both1, preferred_element_type=F32)
        raised = []
        for at in range(3):
            for pair in range(2):
                piece = wide[at * y2:(at + 1) * y2, pair * zs:(pair + 1) * zs]
                flank = wide[at * y2:(at + 1) * y2, (2 + pair) * zs:(3 + pair) * zs]
                view = t4.at[at, pair]
                for r in range(2):
                    view[pl.ds(8 + r, y2, stride=2), :] = piece
                    t5.at[at, pair][pl.ds(r, y2, stride=2), :] = flank
                raised.append((view[pl.ds(8, y1), :],
                               t5[at, pair] + view[pl.ds(7, y1), :] + view[pl.ds(9, y1), :]))
        for pair in range(2):
            first = q * blocks + 2 * pair
            rising = []
            for i in range(1, half + 3):
                even, odd = mr[first, i - 1].astype(F32), mr[first + 1, i - 1].astype(F32)
                left = lane_of(even) < width1
                mixed = jnp.concatenate([jnp.where(left, even, pltpu.roll(odd, width1, 1)),
                                         jnp.where(left, pltpu.roll(even, width1, 1), odd)], axis=0)
                at = i // half
                around = (raised[2 * at + pair][1] + raised[2 * ((i - 1) // half) + pair][0]
                          + raised[2 * ((i + 1) // half) + pair][0])
                rising.append((mixed + keep * raised[2 * at + pair][0] + coeff1(i) * around).astype(BF16))
            wide = jnp.dot(jnp.concatenate(rising, axis=0), both0, preferred_element_type=F32)
            for i in range(half + 2):
                piece = wide[i * y1:(i + 1) * y1]
                for inner in range(2):
                    v1[first + inner, i, pl.ds(8, y1), :] = piece[:, inner * zs:(inner + 1) * zs]
                    if 1 <= i <= half:
                        vz[first + inner, i - 1] = piece[:, (2 + inner) * zs:(3 + inner) * zs]
    arrive(lr.at[pl.ds(0, group - 1)], sem_l)
    keys = [(i, j) for i in range(group) for j in range(i, group)]
    totals = [None] * len(keys)
    tall = y1 // 2
    for i in range(share):
        p = i % planes if whole_fields else (place_of(v) * share + i) % planes
        h, e = p // 2, p % 2
        for cut in range(2):
            rows = pl.ds(8 + cut * tall, tall)
            halves = []
            for u in range(group):
                x = v1[u, h + 1, rows, :]
                halves.append((keep * x, vz[u, h, pl.ds(cut * tall, tall), :] + 2.0 * x + v1[u, h + 2 * e, rows, :]))
            for r in range(2):
                k = gk.at[p][pl.ds(2 * cut * tall + r, tall, stride=2), :]
                z = []
                for u in range(group):
                    kept, around = halves[u]
                    z.append(lr[u, i, r, pl.ds(cut * tall, tall), :].astype(F32) + kept
                             + k * (around + v1[u, h + 1, pl.ds(7 + 2 * r + cut * tall, tall), :]))
                for n, (one, other) in enumerate(keys):
                    product = (z[one] * z[other]).reshape(tall // 8, 8, zs).sum(axis=0)
                    totals[n] = product if totals[n] is None else totals[n] + product
    lines = [None] * group
    lane = lax.broadcasted_iota(jnp.int32, (1, zs), 1)
    for (i, j), total in zip(keys, totals):
        value = jnp.sum(jnp.sum(total, axis=0, keepdims=True), axis=1, keepdims=True)
        for one, other in {(i, j), (j, i)}:
            placed = jnp.where(lane == other, value, 0.0)
            lines[one] = placed if lines[one] is None else lines[one] + placed
    for i in range(group):
        part[i] = lines[i]
    mine = part[v]
    def own():
        start = {0: x20}
        arrive_from(near, lambda n: x2h.at[pl.ds(0, n)], sem_near)
        if far:
            arrive_from(far, lambda n: x2hb.at[pl.ds(0, n)], sem_far)
        for off in offs:
            start[off] = x2h[off + reach] if abs(off) <= NEAR else x2hb[off + reach].astype(F32)
        level2 = sweeps(start)
        raised = [lift_up(level2, off, t2.at[off + 1], split_dot) for off in (-1, 0, 1)]
        for i in range(1, half + 3):
            for pair in range(pairs):
                at = i // half
                around = raised[at][1][pair] + raised[(i - 1) // half][0][pair] + raised[(i + 1) // half][0][pair]
                x = m1[pair, i] + keep * raised[at][0][pair] + coeff1(i) * around
                wide = split_dot(x, spread)
                w1[2 * pair, i - 1] = wide[:, :zs]
                w1[2 * pair + 1, i - 1] = wide[:, zs:]
                if 2 <= i < half + 2:
                    wide = split_dot(x, beside)
                    wz[2 * pair, i - 2] = wide[:, :zs]
                    wz[2 * pair + 1, i - 2] = wide[:, zs:]
        for f in range(fields):
            for h in range(half):
                x = w1[f, h + 1]
                base = wz[f, h] + 2.0 * x
                kept = keep * x
                rims = sides(x)
                for e in range(2):
                    p = 2 * h + e
                    around = base + w1[f, h + 2 * e]
                    for r in range(2):
                        rows = pl.ds(r, y1, stride=2)
                        out.at[0, f, p][rows, :] = (
                            lo.at[f, p][rows, :] + kept + gk.at[p][rows, :] * (around + rims[r]))


    if bricks * group <= ONE_ROUND:
        for index in range(1, bricks * group):
            brick, vec = (b + index // group) % bricks, (v + index % group) % group
            begin(None, part.at[vec], g2h.at[index], sem_g2, brick, vec)
        own()
        arrive(g2h.at[pl.ds(1, bricks * group - 1)], sem_g2)
        rows = [mine] + [g2h[index] for index in range(1, bricks * group)]
        while len(rows) > 1:
            rows = [a + b for a, b in zip(rows[::2], rows[1::2])] + rows[len(rows) & ~1:]
        mine = rows[0]
    else:
        for step in range(1, group):
            peer = (v + step) % group
            begin(None, part.at[peer], g1h.at[step], sem_g1, b, peer)
        own()
        arrive(g1h.at[pl.ds(1, group - 1)], sem_g1)
        for step in range(1, group):
            mine = mine + g1h[step]
        rows_s[...] = mine
        for step in range(1, bricks):
            begin(None, rows_s, g2h.at[step], sem_g2, (b + step) % bricks, v)
        arrive(g2h.at[pl.ds(1, bricks - 1)], sem_g2)
        for step in range(1, bricks):
            mine = mine + g2h[step]
    gram[...] = mine[:, :group]
    for finish in sends:
        finish()


def local(bricks, group, right_side, diffusivity):
    fields, planes, ys, zs = right_side.shape[1:]
    assert right_side.shape[0] == 1 and planes == 4 and ys == zs == 128 and fields == 4 and group % 4 == 0 and SWEEPS == 6
    pairs, half = fields // 2, planes // 2
    y1, y2 = ys // 2, ys // 4
    reach = min(SWEEPS, bricks - 1)
    units = fields * planes
    share = units // group
    slots = 2 * reach + 1
    ends = bricks * group if bricks * group <= ONE_ROUND else bricks
    count = 2 * pairs + 14
    vm = pltpu.VMEM
    result, rows = pl.pallas_call(
        functools.partial(kernel, bricks, group, reach),
        out_shape=(
            jax.ShapeDtypeStruct(right_side.shape, F32),
            jax.ShapeDtypeStruct((1, group), F32),
        ),
        in_specs=[pl.BlockSpec(memory_space=pl.ANY)] * 2,
        out_specs=(pl.BlockSpec(memory_space=pltpu.VMEM),) * 2,
        scratch_shapes=[
            vm((fields, planes, ys, zs), F32),
            vm((planes, ys, zs), F32),
            vm((fields, planes, ys, zs), F32),
            vm((planes, ys, zs), F32),
            vm((planes, ys, zs), F32),
            vm((fields, planes, ys, zs), F32),
            vm((units, 2, y1, zs), BF16),
            vm((group, share, 2, y1, zs), BF16),
            vm((2, fields, ys, zs), BF16),
            vm((2, fields, ys, zs), BF16),
            vm((fields, half, ys, zs), F32),
            vm((half, ys, zs), F32),
            vm((half, y1, zs), F32),
            vm((half, y1, zs), F32),
            vm((2, 2, y1, zs), BF16),
            vm((2, 2, y1, zs), BF16),
            vm((fields, ys, zs), F32),
            vm((2, y2, zs), F32),
            vm((2, 2, y2 // 2, zs), F32),
            vm((2, 2, y2 // 2, zs), F32),
            vm((2, y1, zs), F32),
            vm((2, y1, zs), F32),
            vm((pairs, half, y1, zs), F32),
            vm((pairs, half + 4, y1, zs), F32),
            vm((2, pairs, half, y1, zs), BF16),
            vm((2, pairs, half, y1, zs), BF16),
            vm((pairs, half + 4, y1, zs), F32),
            vm((pairs, y1, zs), F32),
            vm((2, pairs, y1, zs), F32),
            vm((2, y2, zs), F32),
            vm((2, y2, zs), F32),
            vm((y2, zs), F32),
            vm((8, zs), F32),
            vm((slots, 8, zs), F32),
            vm((y2, zs), F32),
            vm((y2, zs), BF16),
            vm((slots, y2, zs), F32),
            vm((slots, y2, zs), BF16),
            vm((fields, 8, zs), BF16),
            vm((slots, group, 8, zs), BF16),
            vm((3, pairs, y1, zs), F32),
            vm((3, 2, y1 + 16, zs), F32),
            vm((3, 2, y1, zs), F32),
            vm((2 * SWEEPS + 1, y2 + 16, zs), F32),
            vm((fields, half + 2, y2, zs), BF16),
            vm((group, half + 2, y2, zs), BF16),
            vm((fields, half + 2, y1, zs), F32),
            vm((fields, half, y1, zs), F32),
            vm((group, half + 2, y1 + 16, zs), F32),
            vm((group, half, y1, zs), F32),
            vm((group, 1, zs), F32),
            vm((group, 1, zs), F32),
            vm((1, zs), F32),
            vm((ends, 1, zs), F32),
            pltpu.SemaphoreType.REGULAR((2, 3)),
            pltpu.SemaphoreType.DMA((3,)),
            pltpu.SemaphoreType.DMA((count,)),
            pltpu.SemaphoreType.DMA((1,)),
        ],
        compiler_params=pltpu.CompilerParams(
            collective_id=0, has_side_effects=True, vmem_limit_bytes=48 << 20
        ),
    )(pltpu.with_memory_space_constraint(right_side, pltpu.HBM), pltpu.with_memory_space_constraint(diffusivity, pltpu.HBM))
    return pl.pallas_call(
        write,
        out_shape=(
            jax.ShapeDtypeStruct(right_side.shape, F32),
            jax.ShapeDtypeStruct((1, group), F32),
        ),
        in_specs=[pl.BlockSpec(memory_space=pltpu.VMEM)] * 2,
        out_specs=(pl.BlockSpec(memory_space=pl.ANY),) * 2,
        scratch_shapes=[pltpu.SemaphoreType.DMA((2,))],
    )(pltpu.with_memory_space_constraint(result, pltpu.VMEM), pltpu.with_memory_space_constraint(rows, pltpu.VMEM))


def solution(mesh):
    return jax.shard_map(
        functools.partial(local, mesh.shape["brick"], mesh.shape["vec"]),
        mesh=mesh,
        in_specs=(P("vec", None, "brick", None, None), P("brick", None, None)),
        out_specs=(P("vec", None, "brick", None, None), P("vec", None)),
        check_vma=False,
    )
```

```python
import functools

import jax
import jax.numpy as jnp
from jax import lax
from jax.experimental import pallas as pl
from jax.experimental.pallas import tpu as pltpu
from jax.sharding import PartitionSpec as P

SWEEPS = 6
NEAR = 2
ONE_ROUND = 64
shift_value = 0.1
damping = 0.8
keep = 1.0 - damping
F32 = jnp.float32
BF16 = jnp.bfloat16
MESH = pl.DeviceIdType.MESH


def rolled_sides(x, axis, width):
    size = x.shape[axis]
    place = lax.broadcasted_iota(jnp.int32, x.shape, axis) % width
    low = jnp.where(place == 0, 0.0, pltpu.roll(x, 1, axis))
    high = jnp.where(place == width - 1, 0.0, pltpu.roll(x, size - 1, axis))
    return low + high


def in_plane(x, width):
    return rolled_sides(x, 0, x.shape[0]) + rolled_sides(x, 1, width)


def split_dot(x, table):
    head = x.astype(BF16)
    tail = (x - head.astype(F32)).astype(BF16)
    return jnp.dot(head, table, preferred_element_type=F32) + jnp.dot(
        tail, table, preferred_element_type=F32
    )


def iotas(rows, cols):
    return (lax.broadcasted_iota(jnp.int32, (rows, cols), 0),
            lax.broadcasted_iota(jnp.int32, (rows, cols), 1))


def merge_table(parts, lanes):
    row, col = iotas(parts * lanes, lanes)
    return jnp.where(row // 2 == col, 1.0, 0.0).astype(BF16)


def spread_table(parts, lanes):
    row, col = iotas(lanes, parts * lanes)
    return jnp.where(col // 2 == row, 1.0, 0.0).astype(BF16)


def beside_table(parts, lanes, width):
    row, col = iotas(lanes, parts * lanes)
    place = col % width
    low = ((col - 1) // 2 == row) & (place > 0)
    high = ((col + 1) // 2 == row) & (place < width - 1)
    return jnp.where(low | high, 1.0, 0.0).astype(BF16)


def repeat_table(lanes, source, width):
    row, col = iotas(lanes, lanes)
    hit = (row // 2 == col % width) & (row < source)
    return jnp.where(hit, 1.0, 0.0).astype(BF16)


def lane_of(x):
    return lax.broadcasted_iota(jnp.int32, x.shape, x.ndim - 1)


def write(result, rows, out, gram, sems):
    copies = [pltpu.make_async_copy(result, out, sems.at[0]), pltpu.make_async_copy(rows, gram, sems.at[1])]
    for made in copies:
        made.start()
    for made in copies:
        made.wait()


def kernel(bricks, group, reach, rhs_in, kap_in, out, gram, rhs, kap, xp, g0, gk, lo, lb, lr, x0s, x0h, tmp,
           ktmp, k1s, q1s, kaps, kaph, fix, f1e, k1c, k1h, k1e, q1e, b1s, x1p, x1b, x1h, m1, t1, t3, f1s, f1h, q2s, q2c, q2h, x2s, x2b,
           x2h, x2hb, x2c, sl, t2, t4, t5, pad2, ms, mr, w1, wz, v1, vz, part, g1h, rows_s, g2h, waves, sems_l, sems_r, sems_s):
    fields, planes, ys, zs = rhs.shape
    pairs = fields // 2
    y1, y2 = ys // 2, ys // 4
    width1, width2 = zs // 2, zs // 4
    half = planes // 2
    units = fields * planes
    share = units // group
    whole_fields = share % planes == 0
    b = lax.axis_index("brick")
    v = lax.axis_index("vec")
    has = (b > 0, b < bricks - 1)
    turns = (b % 2, 1 - b % 2)
    side = (-1, 1)
    edge = (0, planes - 1)
    edge1 = (0, half - 1)
    offs = [sign * size for size in range(1, reach + 1) for sign in (-1, 1)]
    counter = [0]
    sends = []

    def copy(src, dst, sem, brick, vec):
        return pltpu.make_async_remote_copy(
            src_ref=src, dst_ref=dst, send_sem=sems_s.at[0], recv_sem=sems_r.at[sem],
            device_id=(brick, vec), device_id_type=MESH)

    def begin(cond, *asked):
        asked = [asked] if len(asked) == 5 else asked[0]

        def start():
            for one in asked:
                copy(*one).start()

        def finish():
            for one in asked:
                copy(*one).wait_send()

        if cond is None:
            start()
            sends.append(finish)
        else:
            pl.when(cond)(start)
            sends.append(lambda: pl.when(cond)(finish))

    def arrive(dst, sem):
        copy(dst, dst, sem, b, v).wait_recv()

    def number(count):
        base = counter[0]
        counter[0] += count
        return base

    def inside(off):
        return (b + off >= 0) & (b + off < bricks)

    def arrive_from(hops, view, sem):
        count = sum(inside(hop).astype(jnp.int32) for hop in hops)
        for n in sorted({sum(0 <= brick + hop < bricks for hop in hops) for brick in range(bricks)} - {0}):
            pl.when(count == n)(copy(view(n), view(n), sem, b, v).wait_recv)

    sem_x0, sem_x1 = number(pairs), number(pairs)
    sem_kap, sem_k1 = number(2), number(2)
    sem_f1, sem_near, sem_far, sem_q2, sem_s, sem_c, sem_l, sem_m, sem_g1, sem_g2 = (
        number(1) for _ in range(10))
    near = [off for off in offs if abs(off) <= NEAR]
    far = [off for off in offs if abs(off) > NEAR]

    load_kap = pltpu.make_async_copy(kap_in, kap, sems_l.at[0])
    load_kap.start()
    for p in edge:
        pltpu.make_async_copy(rhs_in.at[0, :, p], rhs.at[:, p], sems_l.at[1]).start()
    load_mid = pltpu.make_async_copy(rhs_in.at[0, :, pl.ds(1, planes - 2)], rhs.at[:, pl.ds(1, planes - 2)],
                                     sems_l.at[2])
    load_mid.start()

    barrier = pltpu.get_barrier_semaphore()
    for s in range(2):
        @pl.when(has[s])
        def _(s=s):
            pl.semaphore_signal(barrier, inc=1, device_id=(b + side[s], v), device_id_type=MESH)
    for step in range(1, group):
        pl.semaphore_signal(barrier, inc=1, device_id=(b, (v + step) % group),
                            device_id_type=MESH)
    for pad in (t4, v1):
        for rows in (pl.ds(0, 8), pl.ds(y1 + 8, 8)):
            pad[:, :, rows, :] = jnp.zeros_like(pad.at[:, :, rows, :])
    for rows in (pl.ds(0, 8), pl.ds(y2 + 8, 8)):
        pad2[:, rows, :] = jnp.zeros_like(pad2.at[:, rows, :])
    for s in range(2):
        @pl.when(jnp.logical_not(has[s]))
        def _(s=s):
            x0h[s] = jnp.zeros_like(x0h.at[s])
            x1h[s] = jnp.zeros_like(x1h.at[s])
            k1h[s] = jnp.zeros_like(k1h.at[s])
            kaph[s] = jnp.zeros_like(kaph.at[s])
            f1h[s] = jnp.zeros_like(f1h.at[s])
    for off in offs:
        @pl.when(jnp.logical_not(inside(off)))
        def _(off=off):
            q2h[off + reach] = jnp.zeros_like(q2h.at[off + reach])
            sl[off + reach] = jnp.zeros_like(sl.at[off + reach])
            if abs(off) <= NEAR:
                x2h[off + reach] = jnp.zeros_like(x2h.at[off + reach])
            else:
                x2hb[off + reach] = jnp.zeros_like(x2hb.at[off + reach])

    load_kap.wait()
    for p in range(planes):
        g = damping / (shift_value + 6.0 * kap[p])
        g0[p] = g
        gk[p] = g * kap[p]
    for s in range(2):
        for r in range(2):
            kaps[s, r] = kap[edge[s], r * y1:(r + 1) * y1].astype(BF16)
    pl.semaphore_wait(barrier, (b > 0).astype(jnp.int32) + (b < bricks - 1).astype(jnp.int32) + group - 1)
    core = v % 2
    mate = v + 1 - 2 * core
    for s in turns:
        begin(inside(2 * s - 1), kaps.at[s, core], kaph.at[1 - s, core], sem_kap, b + 2 * s - 1, v)
    pltpu.make_async_copy(rhs.at[:, pl.ds(0, 2)], rhs.at[:, pl.ds(0, 2)], sems_l.at[1]).wait()
    for f in range(fields):
        for s in range(2):
            x = g0[edge[s]] * rhs[f, edge[s]]
            xp[f, edge[s]] = x
            x0s[s, f] = x.astype(BF16)

    def tell(stage, far):
        for s in range(2):
            @pl.when(inside(side[s] * far))
            def _(s=s):
                pl.semaphore_signal(waves.at[1 - s, stage], inc=1, device_id=(b + side[s] * far, v), device_id_type=MESH)

    def hear(stage, far):
        for s in range(2):
            @pl.when(inside(side[s] * far))
            def _(s=s):
                pl.semaphore_wait(waves.at[s, stage], 1)

    tell(0, 1)

    merge = merge_table(2, zs)
    for h in range(half):
        ktmp[h] = kap[2 * h] + kap[2 * h + 1]
    k1 = []
    for h in range(half):
        summed = ktmp.at[h][pl.ds(0, y1, stride=2), :] + ktmp.at[h][pl.ds(1, y1, stride=2), :]
        k = split_dot(summed, repeat_table(zs, zs, width1)) * 0.125
        k1s[h] = k
        k1.append(k)
    for s in range(2):
        k = k1[edge1[s]]
        low, high = k[:y2], k[y2:]
        packed = jnp.where(lane_of(low) < width1, low, high)
        for r in range(2):
            k1c[s, r] = packed[r * y2 // 2:(r + 1) * y2 // 2]
    for s in turns:
        begin(inside(2 * s - 1), k1c.at[s, core], k1h.at[1 - s, core], sem_k1, b + 2 * s - 1, v)
    for pair in range(pairs):
        for s in turns:
            both = pl.ds(2 * pair, 2)
            begin(inside(2 * s - 1), x0s.at[s, both], x0h.at[1 - s, both], sem_x0 + pair, b + 2 * s - 1, v)

    gd1 = [damping / (shift_value + 6.0 * 0.25 * k) for k in k1]
    for h in range(half):
        q1s[h] = gd1[h] * (0.25 * k1[h])
    t1[0] = k1[0] + k1[1]
    summed = t1.at[0][pl.ds(0, y2, stride=2), :] + t1.at[0][pl.ds(1, y2, stride=2), :]
    k2 = split_dot(summed, repeat_table(zs, width1, width2)) * 0.125
    gd2 = damping / (shift_value + 6.0 * 0.0625 * k2)
    q2 = gd2 * (0.0625 * k2)
    q2s[...] = q2
    blocks = zs // width2
    tall2 = y2 // blocks
    packed = q2[:tall2]
    place = lane_of(packed) // width2
    for j in range(1, blocks):
        packed = jnp.where(place == j, q2[j * tall2:(j + 1) * tall2], packed)
    q2c[...] = packed

    load_mid.wait()
    for f in range(fields):
        for p in range(1, planes - 1):
            xp[f, p] = g0[p] * rhs[f, p]
    for f in range(fields):
        for h in range(half):
            total = None
            for p in (2 * h, 2 * h + 1):
                x = xp[f, p]
                around = in_plane(x, zs)
                if p > 0:
                    around = around + xp[f, p - 1]
                if p < planes - 1:
                    around = around + xp[f, p + 1]
                resid = keep * rhs[f, p] + kap[p] * around
                lo[f, p] = x + g0[p] * resid
                total = resid if total is None else total + resid
            tmp[f, h] = total

    def pack(f, p):
        view = lo.at[f, p]
        for e in range(2):
            lb[f * planes + p, e] = view[pl.ds(e, y1, stride=2), :].astype(BF16)

    def place_of(vec):
        return vec % 2 * (group // 2) + vec // 2

    steps = sorted(range(1, group), key=lambda step: -min(step, group - step))

    def field_of(vec):
        return place_of(vec) * share // planes

    def share_out(first, count, chosen):
        for step in steps:
            peer = (v + step) % group
            begin(chosen(peer), lb.at[pl.ds(place_of(peer) * share + first, count)], lr.at[v, pl.ds(first, count)],
                  sem_l, b, peer)

    early = share == planes
    for f in range(fields):
        for p in range(1, planes - 1):
            pack(f, p)
    if early:
        share_out(1, planes - 2, lambda peer: None)

    def send_x1(pair, orders):
        for s in range(2):
            for order in orders:
                plane = order if s == 0 else half - 1 - order
                x1b[s, pair, order] = x1p[pair, plane + 2].astype(BF16)
        for s in turns:
            part = pl.ds(orders[0], len(orders))
            begin(inside(2 * s - 1), x1b.at[s, pair, part], x1h.at[1 - s, pair, part], sem_x1 + pair,
                  b + 2 * s - 1, v)

    hear(0, 1)
    tell(1, 2)

    def to_level1(source):
        for pair in range(pairs):
            parts = [view[pl.ds(0, y1, stride=2), :] + view[pl.ds(1, y1, stride=2), :]
                     for view in (source(2 * pair), source(2 * pair + 1))]
            yield pair, split_dot(jnp.concatenate(parts, axis=1), merge) * 0.125

    def to_level2(source):
        parts = [view[pl.ds(0, y2, stride=2), :] + view[pl.ds(1, y2, stride=2), :] for view in map(source, range(pairs))]
        return split_dot(jnp.concatenate(parts, axis=1), merge)

    for h in range(half):
        for pair, b1 in to_level1(lambda f: tmp.at[f, h]):
            b1s[pair, h] = b1
            x1p[pair, h + 2] = gd1[h] * b1
    for halo, sem in ((k1h, sem_k1), (kaph, sem_kap)):
        arrive_from(side, lambda n: halo.at[pl.ds(0, n), 0], sem)
        for s in range(2):
            begin(has[s], halo.at[s, core], halo.at[s, core], sem + 1, b, mate)
    arrive_from(side, lambda n: k1h.at[pl.ds(0, n), 0], sem_k1 + 1)
    for s in range(2):
        c = jnp.concatenate([k1h[s, 0], k1h[s, 1]], axis=0)
        turned = pltpu.roll(c, width1, 1)
        lane = lane_of(c)
        k1e[s, :y2] = jnp.where(lane < width1, c, turned)
        k1e[s, y2:] = jnp.where(lane < width1, turned, c)
        for pair in range(pairs):
            t3[s, pair] = k1e[s] * x1p[pair, edge1[s] + 2]
        f1s[s] = to_level2(lambda pair: t3.at[s, pair])
    for s in turns:
        begin(inside(2 * s - 1), f1s.at[s], f1h.at[1 - s], sem_f1, b + 2 * s - 1, v)
    hear(1, 2)
    tell(2, 3)

    def fix_f1():
        arrive_from(side, lambda n: kaph.at[pl.ds(0, n), 0], sem_kap + 1)
        for s in range(2):
            k = k1e[s]
            gd = damping / (shift_value + 6.0 * 0.25 * k)
            q1e[s] = gd * (0.25 * k)
            for f in range(fields):
                for r in range(2):
                    rows = slice(r * y1, (r + 1) * y1)
                    fix[f, rows] = kaph[s, r].astype(F32) * xp[f, edge[s], rows]
            for pair, flux in to_level1(lambda f: fix.at[f]):
                t3[s, pair] = k1s[edge1[s]] * gd * flux
            f1e[s] = to_level2(lambda pair: t3.at[s, pair])

    def resid1(pair):
        total = None
        for h in range(half):
            around = in_plane(x1p[pair, h + 2], width1)
            if h > 0:
                around = around + x1p[pair, h + 1]
            if h < half - 1:
                around = around + x1p[pair, h + 3]
            resid = keep * b1s[pair, h] + 0.25 * k1s[h] * around
            total = resid if total is None else total + resid
        t1[pair] = total

    def rim_out(pair):
        for f in (2 * pair, 2 * pair + 1):
            for s in range(2):
                lo[f, edge[s]] = lo[f, edge[s]] + g0[edge[s]] * tmp[f, edge1[s]]
                pack(f, edge[s])
        if early:
            for p in edge:
                share_out(p, 1, lambda peer: field_of(peer) // 2 == pair)
        elif pair == pairs - 1:
            share_out(0, share, lambda peer: None)

    for pair in range(pairs):
        arrive_from(side, lambda n: x0h.at[pl.ds(0, n), pl.ds(2 * pair, 2)], sem_x0 + pair)
        for s in range(2):
            p, h = edge[s], edge1[s]
            halved = []
            for f in (2 * pair, 2 * pair + 1):
                flux = kap[p] * x0h[s, f].astype(F32)
                tmp[f, h] = flux
                view = tmp.at[f, h]
                halved.append(view[pl.ds(0, y1, stride=2), :] + view[pl.ds(1, y1, stride=2), :])
            b1 = split_dot(jnp.concatenate(halved, axis=1), merge) * 0.125
            b1s[pair, h] = b1s[pair, h] + b1
            x1p[pair, h + 2] = x1p[pair, h + 2] + gd1[h] * b1
        if pair < pairs - 1:
            send_x1(pair, tuple(range(half)))
        if pair == 0:
            fix_f1()
            rim_out(pair)
            hear(2, 3)
            for off in offs:
                begin(inside(off), q2c, q2h.at[reach - off], sem_q2, b + off, v)
        if pair < pairs - 1:
            resid1(pair)

    send_x1(pairs - 1, tuple(range(half)))
    resid1(pairs - 1)
    halved = [t1.at[pair][pl.ds(0, y2, stride=2), :] + t1.at[pair][pl.ds(1, y2, stride=2), :] for pair in range(pairs)]
    b2 = split_dot(jnp.concatenate(halved, axis=1), merge) * 0.125

    arrive_from(side, lambda n: f1h.at[pl.ds(0, n)], sem_f1)
    for s in range(2):
        b2 = b2 + (0.125 * 0.25) * (f1h[s] + f1e[s])
    x20 = gd2 * b2
    x2s[...] = x20
    x2b[...] = x20.astype(BF16)
    quad = lane_of(x20[:tall2]) // width2
    for f in range(fields):
        slab = None
        for j in range(blocks):
            piece = x20[j * tall2:(j + 1) * tall2]
            if j != f:
                piece = pltpu.roll(piece, width2 * ((j - f) % blocks), 1)
            slab = piece if slab is None else jnp.where(quad == j, piece, slab)
        x2c[f] = slab.astype(BF16)

    peers = [(v + step) % group for step in range(group)]
    for off in reversed(offs):
        begin(inside(off), [(x2c.at[field_of(peer)], sl.at[reach - off, v], sem_s, b + off, peer) for peer in peers])
    for step in steps:
        peer = (v + step) % group
        begin(None, x2c.at[field_of(peer)], sl.at[reach, v], sem_c, b, peer)
    sl[reach, v] = x2c[field_of(v)]
    for off in reversed(offs):
        slot = reach - off
        if abs(off) <= NEAR:
            begin(inside(off), x2s, x2h.at[slot], sem_near, b + off, v)
        else:
            begin(inside(off), x2b, x2hb.at[slot], sem_far, b + off, v)

    rim_out(pairs - 1)
    for i in range(share):
        lr[v, i] = lb[place_of(v) * share + i]
    def coeff1(i):
        return q1e[0] if i == 1 else q1e[1] if i == half + 2 else q1s[i - 2]

    def raise_m(pair):
        arrive_from(side, lambda n: x1h.at[pl.ds(0, n), pair], sem_x1 + pair)
        for s in range(2):
            for order in range(half):
                x1p[pair, 1 - order if s == 0 else half + 2 + order] = x1h[s, pair, order].astype(F32)
        for i in range(1, half + 3):
            x = x1p[pair, i]
            around = in_plane(x, width1) + x1p[pair, i - 1] + x1p[pair, i + 1]
            x = (1.0 + keep) * x + coeff1(i) * around
            m1[pair, i] = x
            low, high = x[:y2], x[y2:]
            left = lane_of(low) < width1
            ms[2 * pair, i - 1] = jnp.where(left, low, pltpu.roll(high, width1, 1)).astype(BF16)
            ms[2 * pair + 1, i - 1] = jnp.where(left, pltpu.roll(low, width1, 1), high).astype(BF16)
        for step in steps:
            peer = (v + step) % group
            begin(field_of(peer) // 2 == pair, ms.at[field_of(peer)], mr.at[v], sem_m, b, peer)

    for pair in range(pairs - 1):
        raise_m(pair)
    raise_m(pairs - 1)
    mr[v] = ms[field_of(v)]

    coeff2 = {0: q2s[...]}
    arrive_from(offs, lambda n: q2h.at[pl.ds(0, n)], sem_q2)
    for off in offs:
        c = q2h[off + reach]
        if abs(off) < SWEEPS:
            parts = []
            for j in range(blocks):
                m = jnp.where(lane_of(c) // width2 == j, c, 0.0)
                shift = width2
                while shift < zs:
                    m = m + pltpu.roll(m, shift, 1)
                    shift *= 2
                parts.append(m)
            coeff2[off] = jnp.concatenate(parts, axis=0)

    spread = spread_table(2, zs)
    beside = beside_table(2, zs, zs)
    both0 = jnp.concatenate([spread, beside], axis=1)
    both1 = jnp.concatenate([spread, beside_table(2, zs, width1)], axis=1)

    def sweeps(start):
        level2 = start
        zero = jnp.zeros_like(start[0])
        for sweep in range(1, SWEEPS):
            wide = SWEEPS - sweep
            after = {}
            for off in range(-min(wide, reach), min(wide, reach) + 1):
                x = level2[off]
                around = in_plane(x, width2) + level2.get(off - 1, zero) + level2.get(off + 1, zero)
                after[off] = keep * x + start[off] + coeff2[off] * around
            level2 = after
        return level2

    def lift_up(level2, at, room, dot):
        wide = dot(level2[at], spread)
        plane, flat = [], []
        for pair in range(2):
            view = room.at[pair]
            piece = wide[:, pair * zs:(pair + 1) * zs]
            view[pl.ds(0, y2, stride=2), :] = piece
            view[pl.ds(1, y2, stride=2), :] = piece
            plane.append(view[...])
            flat.append(in_plane(view[...], width1))
        return plane, flat

    def sides(x):
        row = lax.broadcasted_iota(jnp.int32, x.shape, 0)
        low = jnp.where(row == 0, 0.0, pltpu.roll(x, 1, 0))
        high = jnp.where(row == y1 - 1, 0.0, pltpu.roll(x, y1 - 1, 0))
        return low, high

    def half_dot(x, table):
        return jnp.dot(x.astype(BF16), table, preferred_element_type=F32)

    arrive_from(offs, lambda n: sl.at[pl.ds(0, n)], sem_s)
    arrive(sl.at[reach, pl.ds(0, group - 1)], sem_c)
    quads = group // blocks
    starts = [{} for _ in range(quads)]
    for off in range(-reach, reach + 1):
        for q in range(quads):
            parts = [None] * blocks
            for u in range(blocks):
                c = sl[off + reach, q * blocks + u].astype(F32)
                for j in range(blocks):
                    piece = c if j == u else pltpu.roll(c, width2 * ((u - j) % blocks), 1)
                    parts[j] = piece if u == 0 else jnp.where(quad == u, piece, parts[j])
            starts[q][off] = jnp.concatenate(parts, axis=0)
    def padded_sweeps(start):
        level2 = start
        for off in range(1 - SWEEPS, SWEEPS):
            if abs(off) <= reach:
                pad2[off + SWEEPS, pl.ds(8, y2), :] = start[off]
        zero = jnp.zeros_like(x20)
        for sweep in range(1, SWEEPS):
            wide = min(SWEEPS - sweep, reach)
            after = {}
            for off in range(-wide, wide + 1):
                x = level2[off]
                view = pad2.at[off + SWEEPS]
                around = (rolled_sides(x, 1, width2) + view[pl.ds(7, y2), :] + view[pl.ds(9, y2), :]
                          + level2.get(off - 1, zero) + level2.get(off + 1, zero))
                after[off] = keep * x + start[off] + coeff2[off] * around
            if sweep < SWEEPS - 1:
                for off in range(1 - wide, wide):
                    pad2[off + SWEEPS, pl.ds(8, y2), :] = after[off]
            level2 = after
        return level2

    ends = [padded_sweeps(start) for start in starts]
    arrive(mr.at[pl.ds(0, group - 1)], sem_m)
    for q in range(quads):
        stack = jnp.concatenate([ends[q][off] for off in (-1, 0, 1)], axis=0).astype(BF16)
        wide = jnp.dot(stack, both1, preferred_element_type=F32)
        raised = []
        for at in range(3):
            for pair in range(2):
                piece = wide[at * y2:(at + 1) * y2, pair * zs:(pair + 1) * zs]
                flank = wide[at * y2:(at + 1) * y2, (2 + pair) * zs:(3 + pair) * zs]
                view = t4.at[at, pair]
                for r in range(2):
                    view[pl.ds(8 + r, y2, stride=2), :] = piece
                    t5.at[at, pair][pl.ds(r, y2, stride=2), :] = flank
                raised.append((view[pl.ds(8, y1), :],
                               t5[at, pair] + view[pl.ds(7, y1), :] + view[pl.ds(9, y1), :]))
        for pair in range(2):
            first = q * blocks + 2 * pair
            rising = []
            for i in range(1, half + 3):
                even, odd = mr[first, i - 1].astype(F32), mr[first + 1, i - 1].astype(F32)
                left = lane_of(even) < width1
                mixed = jnp.concatenate([jnp.where(left, even, pltpu.roll(odd, width1, 1)),
                                         jnp.where(left, pltpu.roll(even, width1, 1), odd)], axis=0)
                at = i // half
                around = (raised[2 * at + pair][1] + raised[2 * ((i - 1) // half) + pair][0]
                          + raised[2 * ((i + 1) // half) + pair][0])
                rising.append((mixed + keep * raised[2 * at + pair][0] + coeff1(i) * around).astype(BF16))
            wide = jnp.dot(jnp.concatenate(rising, axis=0), both0, preferred_element_type=F32)
            for i in range(half + 2):
                piece = wide[i * y1:(i + 1) * y1]
                for inner in range(2):
                    v1[first + inner, i, pl.ds(8, y1), :] = piece[:, inner * zs:(inner + 1) * zs]
                    if 1 <= i <= half:
                        vz[first + inner, i - 1] = piece[:, (2 + inner) * zs:(3 + inner) * zs]
    arrive(lr.at[pl.ds(0, group - 1)], sem_l)
    keys = [(i, j) for i in range(group) for j in range(i, group)]
    totals = [None] * len(keys)
    tall = y1 // 2
    for i in range(share):
        p = i % planes if whole_fields else (place_of(v) * share + i) % planes
        h, e = p // 2, p % 2
        for cut in range(2):
            rows = pl.ds(8 + cut * tall, tall)
            halves = []
            for u in range(group):
                x = v1[u, h + 1, rows, :]
                halves.append((keep * x, vz[u, h, pl.ds(cut * tall, tall), :] + 2.0 * x + v1[u, h + 2 * e, rows, :]))
            for r in range(2):
                k = gk.at[p][pl.ds(2 * cut * tall + r, tall, stride=2), :]
                z = []
                for u in range(group):
                    kept, around = halves[u]
                    z.append(lr[u, i, r, pl.ds(cut * tall, tall), :].astype(F32) + kept
                             + k * (around + v1[u, h + 1, pl.ds(7 + 2 * r + cut * tall, tall), :]))
                for n, (one, other) in enumerate(keys):
                    product = (z[one] * z[other]).reshape(tall // 8, 8, zs).sum(axis=0)
                    totals[n] = product if totals[n] is None else totals[n] + product
    lines = [None] * group
    lane = lax.broadcasted_iota(jnp.int32, (1, zs), 1)
    for (i, j), total in zip(keys, totals):
        value = jnp.sum(jnp.sum(total, axis=0, keepdims=True), axis=1, keepdims=True)
        for one, other in {(i, j), (j, i)}:
            placed = jnp.where(lane == other, value, 0.0)
            lines[one] = placed if lines[one] is None else lines[one] + placed
    for i in range(group):
        part[i] = lines[i]
    mine = part[v]
    def own():
        start = {0: x20}
        arrive_from(near, lambda n: x2h.at[pl.ds(0, n)], sem_near)
        if far:
            arrive_from(far, lambda n: x2hb.at[pl.ds(0, n)], sem_far)
        for off in offs:
            start[off] = x2h[off + reach] if abs(off) <= NEAR else x2hb[off + reach].astype(F32)
        level2 = sweeps(start)
        raised = [lift_up(level2, off, t2.at[off + 1], split_dot) for off in (-1, 0, 1)]
        for i in range(1, half + 3):
            for pair in range(pairs):
                at = i // half
                around = raised[at][1][pair] + raised[(i - 1) // half][0][pair] + raised[(i + 1) // half][0][pair]
                x = m1[pair, i] + keep * raised[at][0][pair] + coeff1(i) * around
                wide = split_dot(x, spread)
                w1[2 * pair, i - 1] = wide[:, :zs]
                w1[2 * pair + 1, i - 1] = wide[:, zs:]
                if 2 <= i < half + 2:
                    wide = split_dot(x, beside)
                    wz[2 * pair, i - 2] = wide[:, :zs]
                    wz[2 * pair + 1, i - 2] = wide[:, zs:]
        for f in range(fields):
            for h in range(half):
                x = w1[f, h + 1]
                base = wz[f, h] + 2.0 * x
                kept = keep * x
                rims = sides(x)
                for e in range(2):
                    p = 2 * h + e
                    around = base + w1[f, h + 2 * e]
                    for r in range(2):
                        rows = pl.ds(r, y1, stride=2)
                        out.at[0, f, p][rows, :] = (
                            lo.at[f, p][rows, :] + kept + gk.at[p][rows, :] * (around + rims[r]))


    if bricks * group <= ONE_ROUND:
        for index in range(1, bricks * group):
            brick, vec = (b + index // group) % bricks, (v + index % group) % group
            begin(None, part.at[vec], g2h.at[index], sem_g2, brick, vec)
        own()
        arrive(g2h.at[pl.ds(1, bricks * group - 1)], sem_g2)
        rows = [mine] + [g2h[index] for index in range(1, bricks * group)]
        while len(rows) > 1:
            rows = [a + b for a, b in zip(rows[::2], rows[1::2])] + rows[len(rows) & ~1:]
        mine = rows[0]
    else:
        for step in range(1, group):
            peer = (v + step) % group
            begin(None, part.at[peer], g1h.at[step], sem_g1, b, peer)
        own()
        arrive(g1h.at[pl.ds(1, group - 1)], sem_g1)
        for step in range(1, group):
            mine = mine + g1h[step]
        rows_s[...] = mine
        for step in range(1, bricks):
            begin(None, rows_s, g2h.at[step], sem_g2, (b + step) % bricks, v)
        arrive(g2h.at[pl.ds(1, bricks - 1)], sem_g2)
        for step in range(1, bricks):
            mine = mine + g2h[step]
    gram[...] = mine[:, :group]
    for finish in sends:
        finish()


def local(bricks, group, right_side, diffusivity):
    fields, planes, ys, zs = right_side.shape[1:]
    assert right_side.shape[0] == 1 and planes == 4 and ys == zs == 128 and fields == 4 and group % 4 == 0 and SWEEPS == 6
    pairs, half = fields // 2, planes // 2
    y1, y2 = ys // 2, ys // 4
    reach = min(SWEEPS, bricks - 1)
    units = fields * planes
    share = units // group
    slots = 2 * reach + 1
    ends = bricks * group if bricks * group <= ONE_ROUND else bricks
    count = 2 * pairs + 14
    vm = pltpu.VMEM
    result, rows = pl.pallas_call(
        functools.partial(kernel, bricks, group, reach),
        out_shape=(
            jax.ShapeDtypeStruct(right_side.shape, F32),
            jax.ShapeDtypeStruct((1, group), F32),
        ),
        in_specs=[pl.BlockSpec(memory_space=pl.ANY)] * 2,
        out_specs=(pl.BlockSpec(memory_space=pltpu.VMEM),) * 2,
        scratch_shapes=[
            vm((fields, planes, ys, zs), F32),
            vm((planes, ys, zs), F32),
            vm((fields, planes, ys, zs), F32),
            vm((planes, ys, zs), F32),
            vm((planes, ys, zs), F32),
            vm((fields, planes, ys, zs), F32),
            vm((units, 2, y1, zs), BF16),
            vm((group, share, 2, y1, zs), BF16),
            vm((2, fields, ys, zs), BF16),
            vm((2, fields, ys, zs), BF16),
            vm((fields, half, ys, zs), F32),
            vm((half, ys, zs), F32),
            vm((half, y1, zs), F32),
            vm((half, y1, zs), F32),
            vm((2, 2, y1, zs), BF16),
            vm((2, 2, y1, zs), BF16),
            vm((fields, ys, zs), F32),
            vm((2, y2, zs), F32),
            vm((2, 2, y2 // 2, zs), F32),
            vm((2, 2, y2 // 2, zs), F32),
            vm((2, y1, zs), F32),
            vm((2, y1, zs), F32),
            vm((pairs, half, y1, zs), F32),
            vm((pairs, half + 4, y1, zs), F32),
            vm((2, pairs, half, y1, zs), BF16),
            vm((2, pairs, half, y1, zs), BF16),
            vm((pairs, half + 4, y1, zs), F32),
            vm((pairs, y1, zs), F32),
            vm((2, pairs, y1, zs), F32),
            vm((2, y2, zs), F32),
            vm((2, y2, zs), F32),
            vm((y2, zs), F32),
            vm((8, zs), F32),
            vm((slots, 8, zs), F32),
            vm((y2, zs), F32),
            vm((y2, zs), BF16),
            vm((slots, y2, zs), F32),
            vm((slots, y2, zs), BF16),
            vm((fields, 8, zs), BF16),
            vm((slots, group, 8, zs), BF16),
            vm((3, pairs, y1, zs), F32),
            vm((3, 2, y1 + 16, zs), F32),
            vm((3, 2, y1, zs), F32),
            vm((2 * SWEEPS + 1, y2 + 16, zs), F32),
            vm((fields, half + 2, y2, zs), BF16),
            vm((group, half + 2, y2, zs), BF16),
            vm((fields, half + 2, y1, zs), F32),
            vm((fields, half, y1, zs), F32),
            vm((group, half + 2, y1 + 16, zs), F32),
            vm((group, half, y1, zs), F32),
            vm((group, 1, zs), F32),
            vm((group, 1, zs), F32),
            vm((1, zs), F32),
            vm((ends, 1, zs), F32),
            pltpu.SemaphoreType.REGULAR((2, 3)),
            pltpu.SemaphoreType.DMA((3,)),
            pltpu.SemaphoreType.DMA((count,)),
            pltpu.SemaphoreType.DMA((1,)),
        ],
        compiler_params=pltpu.CompilerParams(
            collective_id=0, has_side_effects=True, vmem_limit_bytes=48 << 20
        ),
    )(pltpu.with_memory_space_constraint(right_side, pltpu.HBM), pltpu.with_memory_space_constraint(diffusivity, pltpu.HBM))
    return pl.pallas_call(
        write,
        out_shape=(
            jax.ShapeDtypeStruct(right_side.shape, F32),
            jax.ShapeDtypeStruct((1, group), F32),
        ),
        in_specs=[pl.BlockSpec(memory_space=pltpu.VMEM)] * 2,
        out_specs=(pl.BlockSpec(memory_space=pl.ANY),) * 2,
        scratch_shapes=[pltpu.SemaphoreType.DMA((2,))],
    )(pltpu.with_memory_space_constraint(result, pltpu.VMEM), pltpu.with_memory_space_constraint(rows, pltpu.VMEM))


def solution(mesh):
    return jax.shard_map(
        functools.partial(local, mesh.shape["brick"], mesh.shape["vec"]),
        mesh=mesh,
        in_specs=(P("vec", None, "brick", None, None), P("brick", None, None)),
        out_specs=(P("vec", None, "brick", None, None), P("vec", None)),
        check_vma=False,
    )
```
